128 devices in a mesh: gx: 8 (over y, core), gy: 16 (over z, x).
Axes of the slice: x: 4, y: 4, z: 4, core: 2. Of those that a mesh axis runs over, the one named last changes fastest.
Arguments:
- right_side: float32 [128, 512, 256], P('gx', 'gy'), may hold values from -30 to 30
- start_field: float32 [128, 512, 256], P('gx', 'gy'), may hold values from -1.8 to 1.8
- coef: float32 [128, 512, 256], P('gx', 'gy'), may hold values from 0.5 to 2
- deflation: float32 [8, 128, 512, 256], P(None, 'gx', 'gy'), may hold values from -9 to 9
Outputs:
- solution: float32 [128, 512, 256], P('gx', 'gy')
- residual: float32 [128, 512, 256], P('gx', 'gy')
- direction: float32 [128, 512, 256], P('gx', 'gy')
The draws below stay inside these ranges and needn't reach their ends.
All inputs are finite; a program needn't handle non-finite values.
Results may differ from the reference program's by a relative error of at most 0.0003.
Values sent between devices are 32-bit elements; how exact they have to be, the bound alone decides.
A program may use at most 192 MiB of HBM per device.

```python
import math
import jax
import jax.numpy as jnp
from jax import lax

CX = 16
CY = 32
NZ = 256
K = 8
ITERS = 2
NX = 128
NY = 512
N_GX = 8
N_GY = 16


def mode_tables():
    local_rows = (jnp.arange(NX) % CX).astype(jnp.float32)
    local_cols = (jnp.arange(NY) % CY).astype(jnp.float32)
    depth = jnp.arange(NZ).astype(jnp.float32)
    pattern = jnp.arange(8)
    freq_rows = (pattern % 2).astype(jnp.float32)
    freq_cols = (pattern // 2 % 2).astype(jnp.float32)
    freq_depth = (pattern // 4).astype(jnp.float32)
    wave_rows = jnp.cos(math.pi * freq_rows[:, None] * (local_rows[None] + 0.5) / CX)
    wave_cols = jnp.cos(math.pi * freq_cols[:, None] * (local_cols[None] + 0.5) / CY)
    wave_depth = jnp.cos(math.pi * freq_depth[:, None] * (depth[None] + 0.5) / NZ)
    return (wave_rows[:, :, None] * wave_cols[:, None, :], wave_depth)


def draw_right_side(key, part):
    key_noise = jax.random.fold_in(key, 11)
    key_amps = jax.random.fold_in(key, 12)
    plane_modes, depth_modes = mode_tables()
    amounts = 0.5 * jax.random.truncated_normal(key_amps, -2.0, 2.0, (NX // CX, NY // CY, 8), jnp.float32)
    cell_amounts = jnp.repeat(jnp.repeat(amounts, CX, axis=0), CY, axis=1)
    smooth = jnp.einsum('xym,mxy,mz->xyz', cell_amounts, plane_modes, depth_modes)
    row_frac = (jnp.arange(NX).astype(jnp.float32) + 0.5) / NX
    col_frac = (jnp.arange(NY).astype(jnp.float32) + 0.5) / NY
    ramp = (0.5 + row_frac)[:, None, None] * (0.5 + col_frac)[None, :, None]
    hump = jnp.sin(math.pi * row_frac)[:, None, None] * jnp.sin(math.pi * col_frac)[None, :, None]
    noise = jax.random.truncated_normal(key_noise, -4.0, 4.0, (NX, NY, NZ), jnp.float32)
    noise = noise + 0.8 * hump
    return ramp * (noise + smooth)


def draw_deflation(key, part):
    key_noise = jax.random.fold_in(key, 21)
    key_mix = jax.random.fold_in(key, 22)
    plane_modes, depth_modes = mode_tables()
    mixing = jnp.eye(K, 8, dtype=jnp.float32)[None, None] + 0.4 * jax.random.truncated_normal(key_mix, -2.0, 2.0, (NX // CX, NY // CY, K, 8), jnp.float32)
    cell_mixing = jnp.repeat(jnp.repeat(mixing, CX, axis=0), CY, axis=1)
    smooth = jnp.einsum('xykm,mxy,mz->kxyz', cell_mixing, plane_modes, depth_modes)
    noise = 0.03 * jax.random.truncated_normal(key_noise, -4.0, 4.0, (K, NX, NY, NZ), jnp.float32)
    return smooth + noise


def shard_levels(own_key, dims, shards, smallest, top_value):
    loudness, own = 1.0, jax.random.fold_in(own_key, 6)
    for dim, parts in shards:
        draws = jnp.exp(jax.random.uniform(jax.random.fold_in(own, dim), (parts,), jnp.float32, smallest / len(shards), top_value / len(shards)))
        loudness = loudness * jnp.repeat(draws, dims[dim] // parts).reshape([-1 if axis == dim else 1 for axis in range(len(dims))])
    return loudness


def normal_values(stream_key, shape, deviation, reach, split=(), held_as=jnp.bfloat16):
    drawn = jax.random.normal(stream_key, shape, jnp.float32) * deviation
    if len(split) > 0:
        drawn = shard_levels(stream_key, shape, split, -0.22, 0.18) * drawn
    return jnp.clip(drawn, min=-reach, max=reach).astype(held_as)


def setup_inputs(seed: int = 0) -> dict:
    streams_of = jax.random.split(jax.random.key(seed), 5)
    right_side = draw_right_side(jax.random.fold_in(streams_of[4], 71), 0)
    start_field = normal_values(streams_of[1], (NX, NY, NZ), 0.3, 1.8, ((0, 8), (1, 16)), jnp.float32)
    coef = jnp.clip(jnp.exp(math.log(2.0) - 1.3862944 * jax.random.uniform(streams_of[2], (NX, NY, NZ), jnp.float32) ** shard_levels(streams_of[2], (NX, NY, NZ), ((0, 8), (1, 16)), -0.2, 0.2)), 0.5, 2.0)
    deflation = draw_deflation(jax.random.fold_in(streams_of[4], 71), 0)
    return {"right_side": right_side, "start_field": start_field, "coef": coef, "deflation": deflation}


highest = lax.Precision.HIGHEST

def face_coef(padded, along):
    length = padded.shape[along]
    lower_side = lax.slice_in_dim(padded, 0, length - 1, axis=along)
    upper_side = lax.slice_in_dim(padded, 1, length, axis=along)
    inside = (lower_side > 0.0) & (upper_side > 0.0)
    summed = lower_side + upper_side
    return jnp.where(inside, 2.0 * lower_side * upper_side / summed, summed)

def coefficients(coef):
    padded = jnp.pad(coef, 1)
    face_rows = face_coef(padded[:, 1:-1, 1:-1], 0)
    face_cols = face_coef(padded[1:-1, :, 1:-1], 1)
    face_depth = face_coef(padded[1:-1, 1:-1, :], 2)
    diagonal = face_rows[1:] + face_rows[:-1] + face_cols[:, 1:] + face_cols[:, :-1]
    diagonal = diagonal + face_depth[:, :, 1:] + face_depth[:, :, :-1]
    return (face_rows, face_cols, face_depth, diagonal)

def operate(values, stencil):
    face_rows, face_cols, face_depth, diagonal = stencil
    padded = jnp.pad(values, 1)
    beside = face_rows[1:] * padded[2:, 1:-1, 1:-1] + face_rows[:-1] * padded[:-2, 1:-1, 1:-1]
    beside = beside + face_cols[:, 1:] * padded[1:-1, 2:, 1:-1] + face_cols[:, :-1] * padded[1:-1, :-2, 1:-1]
    beside = beside + face_depth[:, :, 1:] * padded[1:-1, 1:-1, 2:] + face_depth[:, :, :-1] * padded[1:-1, 1:-1, :-2]
    return diagonal * values - beside

def block_operate(vectors, face_rows, face_cols, face_depth, diagonal):
    padded = jnp.pad(vectors, ((0, 0), (1, 1), (1, 1), (1, 1)))
    beside = face_rows[1:] * padded[:, 2:, 1:-1, 1:-1] + face_rows[:-1] * padded[:, :-2, 1:-1, 1:-1]
    beside = beside + face_cols[:, 1:] * padded[:, 1:-1, 2:, 1:-1] + face_cols[:, :-1] * padded[:, 1:-1, :-2, 1:-1]
    beside = beside + face_depth[:, :, 1:] * padded[:, 1:-1, 1:-1, 2:] + face_depth[:, :, :-1] * padded[:, 1:-1, 1:-1, :-2]
    return diagonal * vectors - beside

def diagonal_blocks(deflation, stencil):
    face_rows, face_cols, face_depth, diagonal = stencil

    def per_block(position):
        row_start = position // N_GY * CX
        col_start = position % N_GY * CY
        anchor = jnp.zeros((), jnp.int32)
        sub_block = lax.dynamic_slice(deflation, (anchor, row_start, col_start, anchor), (K, CX, CY, NZ))
        rows_part = lax.dynamic_slice(face_rows, (row_start, col_start, anchor), (CX + 1, CY, NZ))
        cols_part = lax.dynamic_slice(face_cols, (row_start, col_start, anchor), (CX, CY + 1, NZ))
        depth_part = lax.dynamic_slice(face_depth, (row_start, col_start, anchor), (CX, CY, NZ + 1))
        diag_part = lax.dynamic_slice(diagonal, (row_start, col_start, anchor), (CX, CY, NZ))
        acted_on = block_operate(sub_block, rows_part, cols_part, depth_part, diag_part)
        return jnp.einsum('kxyz,lxyz->kl', sub_block, acted_on, precision=highest)
    return lax.map(per_block, jnp.arange(N_GX * N_GY, dtype=jnp.int32))

def lower_blocks(deflation, stencil):
    face_rows, face_cols = (stencil[0], stencil[1])
    top_rows = deflation[:, CX - 1::CX]
    bottom_rows = deflation[:, 0::CX]
    shifted_rows = jnp.concatenate([jnp.zeros_like(top_rows[:, :1]), top_rows[:, :-1]], axis=1)
    weighted_rows = bottom_rows * face_rows[0:NX:CX][None]
    weighted_rows = weighted_rows.reshape(K, N_GX, N_GY, CY, NZ)
    shifted_rows = shifted_rows.reshape(K, N_GX, N_GY, CY, NZ)
    below_rows = -jnp.einsum('kabcz,labcz->abkl', weighted_rows, shifted_rows, precision=highest)
    top_cols = deflation[:, :, CY - 1::CY]
    bottom_cols = deflation[:, :, 0::CY]
    shifted_cols = jnp.concatenate([jnp.zeros_like(top_cols[:, :, :1]), top_cols[:, :, :-1]], axis=2)
    weighted_cols = bottom_cols * face_cols[:, 0:NY:CY][None]
    weighted_cols = weighted_cols.reshape(K, N_GX, CX, N_GY, NZ)
    shifted_cols = shifted_cols.reshape(K, N_GX, CX, N_GY, NZ)
    below_cols = -jnp.einsum('kacbz,lacbz->abkl', weighted_cols, shifted_cols, precision=highest)
    return (below_rows.reshape(N_GX * N_GY, K, K), below_cols.reshape(N_GX * N_GY, K, K))

def place(selector, blocks):
    return selector.astype(jnp.float32)[:, None, :, None] * blocks[:, :, None, :]

def place_mirror(selector, blocks):
    return selector.astype(jnp.float32)[:, None, :, None] * jnp.transpose(blocks, (2, 0, 1))[None]

def block_masks(block_count, across):
    positions = jnp.arange(block_count, dtype=jnp.int32)
    row_ids = positions[:, None]
    col_ids = positions[None, :]
    self_mask = row_ids == col_ids
    below_rows = col_ids == row_ids - across
    below_cols = (col_ids == row_ids - 1) & (row_ids % across != 0)
    above_rows = col_ids == row_ids + across
    above_cols = (col_ids == row_ids + 1) & (col_ids % across != 0)
    return (self_mask, below_rows, below_cols, above_rows, above_cols)

def restrict(deflation, values):

    def per_vector(vector):
        return (vector * values).reshape(N_GX, CX, N_GY, CY, NZ).sum(axis=(1, 3, 4))
    sums = lax.map(per_vector, deflation)
    return jnp.transpose(sums, (1, 2, 0)).reshape(-1)

def prolong(deflation, coarse_values):
    grid = jnp.transpose(coarse_values.reshape(N_GX, N_GY, K), (2, 0, 1))

    def add_one(carry, pair):
        vector, amounts = pair
        spread = vector.reshape(N_GX, CX, N_GY, CY, NZ) * amounts[:, None, :, None, None]
        return (carry + spread.reshape(NX, NY, NZ), None)
    summed, ignored = lax.scan(add_one, jnp.zeros((NX, NY, NZ), jnp.float32), (deflation, grid))
    return summed

def reference(right_side, start_field, coef, deflation):
    stencil = coefficients(coef)
    diagonal = stencil[3]
    diag_blocks = diagonal_blocks(deflation, stencil)
    below_rows, below_cols = lower_blocks(deflation, stencil)
    block_count = N_GX * N_GY
    self_mask, mask_below_rows, mask_below_cols, mask_above_rows, mask_above_cols = block_masks(block_count, N_GY)
    matrix = place(self_mask, diag_blocks) + place(mask_below_rows, below_rows) + place(mask_below_cols, below_cols)
    matrix = matrix + place_mirror(mask_above_rows, below_rows) + place_mirror(mask_above_cols, below_cols)
    matrix = matrix.reshape(block_count * K, block_count * K)
    factor = jnp.linalg.cholesky(matrix)

    def coarse(values):
        solved = jax.scipy.linalg.cho_solve((factor, True), restrict(deflation, values))
        return prolong(deflation, solved)
    solution = start_field + coarse(right_side - operate(start_field, stencil))
    residual = right_side - operate(solution, stencil)
    precond = residual / diagonal
    inner_now = jnp.sum(residual * precond)
    direction = precond - coarse(operate(precond, stencil))
    for iteration in range(ITERS):
        applied = operate(direction, stencil)
        step_size = inner_now / jnp.sum(direction * applied)
        solution = solution + step_size * direction
        residual = residual - step_size * applied
        precond = residual / diagonal
        inner_next = jnp.sum(residual * precond)
        direction = precond + inner_next / inner_now * direction - coarse(operate(precond, stencil))
        inner_now = inner_next
    return (solution, residual, direction)
```

```python
import functools
import jax, jax.numpy as jnp
from jax import lax
from jax.experimental import pallas as pl
from jax.experimental.pallas import tpu as pltpu
from jax.sharding import PartitionSpec as P

F32 = jnp.float32
BF = jnp.bfloat16


def iota(shape, dim):
    return lax.broadcasted_iota(jnp.int32, shape, dim)


def split3(v):
    high = v.astype(BF)
    rest = v - high.astype(F32)
    mid = rest.astype(BF)
    low = (rest - mid.astype(F32)).astype(BF)
    return high, mid, low


def mm(left, right):
    lh, lm, ll = left
    rh, rm, rl = right
    d = lambda p, q: jnp.dot(p, q, preferred_element_type=F32)
    return d(lh, rh) + (d(lh, rm) + d(lm, rh)) + (d(lm, rm) + d(lh, rl) + d(ll, rh))


def invert_pairs(m_ref, count):
    lane = iota((8, 128), 1)
    sub = iota((8, 128), 0)
    half = lane // 64 * 64

    def panel(p, carry):
        start = pl.multiple_of(p * 8, 8)
        in_panel = (lane - half) // 8 == p
        ident = (lane - half - p * 8) == sub
        for s in range(count):
            rows = m_ref[s, pl.ds(start, 8), :]
            piv = [jnp.take_along_axis(rows, half + p * 8 + j, axis=1) for j in range(8)]
            cols = [
                [jnp.take_along_axis(m_ref[s, 8 * v : 8 * v + 8, :], half + p * 8 + j, axis=1) for j in range(8)]
                for v in range(8)
            ]
            rows = jnp.where(in_panel, jnp.where(ident, 1.0, 0.0), rows)
            for t in range(8):
                scale = 1.0 / piv[t][t : t + 1, :]
                own = sub == t
                row = rows[t : t + 1, :] * scale
                mult = piv[t]
                rows = jnp.where(own, row, rows - mult * row)
                for j in range(t + 1, 8):
                    prow = piv[j][t : t + 1, :] * scale
                    piv[j] = jnp.where(own, prow, piv[j] - mult * prow)
            for v in range(8):
                block = jnp.where(in_panel, 0.0, m_ref[s, 8 * v : 8 * v + 8, :])
                terms = [cols[v][j] * rows[j : j + 1, :] for j in range(8)]
                while len(terms) > 1:
                    terms = [terms[i] + terms[i + 1] for i in range(0, len(terms), 2)]
                m_ref[s, 8 * v : 8 * v + 8, :] = block - terms[0]
            m_ref[s, pl.ds(start, 8), :] = rows
        return carry

    lax.fori_loop(0, 8, panel, 0)


def factor(tiles, d_ref, lu_ref, w_ref, y_ref, m_ref, x_ref, xt_ref, a, b, na, nb):
    lane = iota((64, 128), 1)
    rowi = iota((64, 128), 0)
    low = lane < 64
    group = lane // 8
    within = lane % 8
    own = (b * na + a) * 8
    target = jnp.where(group == 0, own, -4096)
    target = jnp.where((group == 1) & (a > 0), own - 8, target)
    target = jnp.where((group == 2) & (a < na - 1), own + 8, target)
    target = jnp.where((group == 3) & (b > 0), own - 64, target)
    target = jnp.where((group == 4) & (b < nb - 1), own + 64, target)
    target = target + within
    for j in range(nb):
        tile = tiles[j]
        d_ref[j] = tile
        y_ref[j] = jnp.where(rowi + 64 * j == target, 1.0, 0.0)
    for j in range(nb):
        left = pltpu.roll(tiles[j], 64, 1)
        if j < nb - 1:
            up = jnp.transpose(tiles[j + 1])[64:128, :]
            up = jnp.concatenate([jnp.zeros((64, 64), F32), up], axis=1)
        else:
            up = jnp.zeros((64, 128), F32)
        left = jnp.where(low, left, 0.0) if j > 0 else jnp.zeros((64, 128), F32)
        lu_ref[j] = jnp.where(low, left, up)

    def invert(lines):
        slots = (len(lines) + 1) // 2
        for s in range(slots):
            first = d_ref[lines[2 * s]]
            second = d_ref[lines[min(2 * s + 1, len(lines) - 1)]]
            m_ref[s] = jnp.where(low, first, pltpu.roll(second, 64, 1))
        invert_pairs(m_ref, slots)
        out = []
        for i in range(len(lines)):
            v = m_ref[i // 2]
            out.append(v[:, :64] if i % 2 == 0 else pltpu.roll(v, 64, 1)[:, :64])
        return out

    step = 1
    levels = []
    while step < nb:
        lines = list(range(step, nb, 2 * step))
        inverses = invert(lines)
        for j, inv in zip(lines, inverses):
            right = jnp.concatenate([lu_ref[j], y_ref[j]], axis=1)
            lut = jnp.transpose(lu_ref[j])
            w = mm(split3(inv), split3(right))
            w_ref[j] = w
            p = mm(split3(lut), split3(w))
            i, k = j - step, j + step
            d_ref[i] = d_ref[i] - p[:64, :128]
            y_ref[i] = y_ref[i] - p[:64, 128:]
            lu_ref[i] = jnp.where(low, lu_ref[i], -p[:64, :128])
            if k < nb:
                d_ref[k] = d_ref[k] - pltpu.roll(p[64:, :128], 64, 1)
                y_ref[k] = y_ref[k] - p[64:, 128:]
                lu_ref[k] = jnp.where(low, -p[64:, :128], lu_ref[k])
        levels.append((step, lines))
        step *= 2
    inv = invert([0])[0]
    x_ref[0:64] = mm(split3(inv), split3(y_ref[0]))
    for step, lines in reversed(levels):
        for j in lines:
            i, k = j - step, j + step
            below = x_ref[64 * i : 64 * i + 64]
            above = x_ref[64 * k : 64 * k + 64] if k < nb else jnp.zeros((64, 128), F32)
            both = jnp.concatenate([below, above], axis=0)
            w = w_ref[j]
            x_ref[64 * j : 64 * j + 64] = w[:, 128:] - mm(split3(w[:, :128]), split3(both))
    for k in range(8):
        xt_ref[k] = jnp.transpose(x_ref[pl.ds(k, na * nb, stride=8), :])[:40, :]


def total_rows(accs):
    sub = iota((8, 128), 0)
    out = jnp.zeros((8, 128), F32)
    for i, acc in enumerate(accs):
        out = jnp.where(sub == i, jnp.sum(acc, axis=0, keepdims=True), out)
    return jnp.broadcast_to(jnp.sum(out, axis=1, keepdims=True), (8, 128))


def fold(value):
    rows, cols = value.shape
    pieces = [value[8 * i : 8 * i + 8, 128 * j : 128 * j + 128] for i in range(rows // 8) for j in range(cols // 128)]
    while len(pieces) > 1:
        pieces = [pieces[i] + pieces[i + 1] if i + 1 < len(pieces) else pieces[i] for i in range(0, len(pieces), 2)]
    return pieces[0]


def face_of(lower, upper):
    summed = lower + upper
    return jnp.where((lower > 0.0) & (upper > 0.0), 2.0 * lower * upper / summed, summed)


def body(na, nb, rhs_hbm, x0_hbm, c_hbm, z_hbm, sol_hbm, res_hbm, dir_hbm, *scratch):
    (zf, az, cf, xf, rf, vf, wf, pf, qf, fx, fyl, fyh, fzl, fzh, dg, rd,
     wx, wy, hxz, hyz, hxc, hyc, hxx, hyx, hxv, hyv, pyz, pyc, pyx, pyv, nx, ny, fcx, fcy,
     cc, ge, s1, gb, tb,
     d_ref, lu_ref, w_ref, y_ref, m_ref, x_ref, xt_ref,
     ld_sem, st_sem, hs_sem, hr_sem, es_sem, er_sem, gs_sem, gr_sem) = scratch
    cx, cy, nz = cf.shape
    nk = zf.shape[0]
    a = lax.axis_index("gx")
    b = lax.axis_index("gy")
    mesh_id = pl.DeviceIdType.MESH
    loads = [
        pltpu.make_async_copy(c_hbm, cf, ld_sem.at[0]),
        pltpu.make_async_copy(x0_hbm, xf, ld_sem.at[1]),
        pltpu.make_async_copy(rhs_hbm, rf, ld_sem.at[2]),
        pltpu.make_async_copy(z_hbm, zf, ld_sem.at[3]),
    ]
    for load in loads:
        load.start()
    barrier = pltpu.get_barrier_semaphore()
    for o in range(1, na):
        pl.semaphore_signal(barrier, inc=1, device_id=(lax.rem(a + o, na), b), device_id_type=mesh_id)
    for o in range(1, nb):
        pl.semaphore_signal(barrier, inc=1, device_id=(a, lax.rem(b + o, nb)), device_id_type=mesh_id)

    has = [a > 0, a < na - 1, b > 0, b < nb - 1]
    peers = [(a - 1, b), (a + 1, b), (a, b - 1), (a, b + 1)]

    def halo(slot, sources, targets):
        def copy(s):
            return pltpu.make_async_remote_copy(
                src_ref=sources[s], dst_ref=targets[s ^ 1],
                send_sem=hs_sem.at[slot, s], recv_sem=hr_sem.at[slot, s ^ 1],
                device_id=peers[s], device_id_type=mesh_id)

        def start():
            for s in range(4):
                @pl.when(has[s])
                def _():
                    copy(s).start()

        def wait_recv():
            for s in range(4):
                @pl.when(has[s])
                def _():
                    pltpu.make_async_remote_copy(
                        src_ref=sources[s], dst_ref=targets[s],
                        send_sem=hs_sem.at[slot, s], recv_sem=hr_sem.at[slot, s],
                        device_id=peers[s], device_id_type=mesh_id).wait_recv()

        def wait_send():
            for s in range(4):
                @pl.when(has[s])
                def _():
                    copy(s).wait_send()

        return start, wait_recv, wait_send

    row0 = iota((cy, nz), 0) == 0
    rowl = iota((cy, nz), 0) == cy - 1
    lan0 = iota((cy, nz), 1) == 0
    lanl = iota((cy, nz), 1) == nz - 1

    for s in range(2):
        @pl.when(jnp.logical_not(has[s]))
        def _():
            hxz[s] = jnp.zeros(hxz.shape[1:], F32)
            hxc[s] = jnp.zeros(hxc.shape[1:], F32)
            hxx[s] = jnp.zeros(hxx.shape[1:], F32)
            for i in range(2):
                hxv[i, s] = jnp.zeros(hxv.shape[2:], F32)

        @pl.when(jnp.logical_not(has[2 + s]))
        def _():
            hyz[s] = jnp.zeros(hyz.shape[1:], F32)
            hyc[s] = jnp.zeros(hyc.shape[1:], F32)
            hyx[s] = jnp.zeros(hyx.shape[1:], F32)
            for i in range(2):
                hyv[i, s] = jnp.zeros(hyv.shape[2:], F32)

    loads[0].wait()
    loads[1].wait()

    def pack(x, carry):
        pyc[0, pl.ds(x, 1), :] = cf[x, 0:1, :]
        pyc[1, pl.ds(x, 1), :] = cf[x, cy - 1 : cy, :]
        pyx[0, pl.ds(x, 1), :] = xf[x, 0:1, :]
        pyx[1, pl.ds(x, 1), :] = xf[x, cy - 1 : cy, :]
        return carry

    lax.fori_loop(0, cx, pack, 0)
    pl.semaphore_wait(barrier, na + nb - 2)
    coef_halo = halo(0, [cf.at[0], cf.at[cx - 1], pyc.at[0], pyc.at[1]], [hxc.at[0], hxc.at[1], hyc.at[0], hyc.at[1]])
    coef_halo[0]()
    x_halo = halo(1, [xf.at[0], xf.at[cx - 1], pyx.at[0], pyx.at[1]], [hxx.at[0], hxx.at[1], hyx.at[0], hyx.at[1]])
    x_halo[0]()
    loads[3].wait()

    def packz(x, carry):
        for k in range(nk):
            pyz[0, k, pl.ds(x, 1), :] = zf[k, x, 0:1, :]
            pyz[1, k, pl.ds(x, 1), :] = zf[k, x, cy - 1 : cy, :]
        return carry

    lax.fori_loop(0, cx, packz, 0)
    z_halo = halo(2, [zf.at[:, 0], zf.at[:, cx - 1], pyz.at[0], pyz.at[1]], [hxz.at[0], hxz.at[1], hyz.at[0], hyz.at[1]])
    z_halo[0]()
    coef_halo[1]()

    fx[0] = jnp.zeros((cy, nz), F32)
    fx[cx] = jnp.zeros((cy, nz), F32)
    wx[0] = face_of(cf[0], hxc[0])
    wx[1] = face_of(cf[cx - 1], hxc[1])

    def faces_x(x, carry):
        fx[x] = face_of(cf[x - 1], cf[x])
        return carry

    lax.fori_loop(1, cx, faces_x, 0)

    def faces(x, carry):
        c = cf[x]
        yl = face_of(jnp.where(row0, hyc[0, pl.ds(x, 1), :], pltpu.roll(c, 1, 0)), c)
        yh = face_of(c, jnp.where(rowl, hyc[1, pl.ds(x, 1), :], pltpu.roll(c, cy - 1, 0)))
        zl = face_of(jnp.where(lan0, 0.0, pltpu.roll(c, 1, 1)), c)
        zh = face_of(c, jnp.where(lanl, 0.0, pltpu.roll(c, nz - 1, 1)))
        wy[0, pl.ds(x, 1), :] = yl[0:1, :]
        wy[1, pl.ds(x, 1), :] = yh[cy - 1 : cy, :]
        xl = jnp.where(x == 0, wx[0], fx[x])
        xh = jnp.where(x == cx - 1, wx[1], fx[x + 1])
        total = xl + xh + yl + yh + zl + zh
        dg[x] = total
        rd[x] = 1.0 / total
        fyl[x] = jnp.where(row0, 0.0, yl)
        fyh[x] = jnp.where(rowl, 0.0, yh)
        fzl[x] = jnp.where(lan0, 0.0, zl)
        fzh[x] = jnp.where(lanl, 0.0, zh)
        return carry

    lax.fori_loop(0, cx, faces, 0)

    def inner_apply(v, before, after, x):
        near = fx[x] * before + fx[x + 1] * after
        near = near + fyl[x] * pltpu.roll(v, 1, 0) + fyh[x] * pltpu.roll(v, cy - 1, 0)
        near = near + fzl[x] * pltpu.roll(v, 1, 1) + fzh[x] * pltpu.roll(v, nz - 1, 1)
        return dg[x] * v - near

    def below(x):
        return jnp.maximum(x - 1, 0)

    def above(x):
        return jnp.minimum(x + 1, cx - 1)

    def make_az(x, carry):
        for k in range(nk):
            az[k, x] = inner_apply(zf[k, x], zf[k, below(x)], zf[k, above(x)], x)
        return carry

    lax.fori_loop(0, cx, make_az, 0)

    pairs = [(k, l) for k in range(nk) for l in range(k, nk)]

    def gram(x, accs):
        accs = list(accs)
        for i in range(cy // 8):
            for j in range(nz // 128):
                zs = [zf[k, x, 8 * i : 8 * i + 8, 128 * j : 128 * j + 128] for k in range(nk)]
                for l in range(nk):
                    w = az[l, x, 8 * i : 8 * i + 8, 128 * j : 128 * j + 128]
                    for k in range(l + 1):
                        n = pairs.index((k, l))
                        accs[n] = accs[n] + zs[k] * w
        return tuple(accs)

    diag = lax.fori_loop(0, cx, gram, tuple(jnp.zeros((8, 128), F32) for _ in pairs))

    x_halo[1]()
    loads[2].wait()

    def minus_faces(v, x, hx, hy):
        v = v + jnp.where(row0, wy[0, pl.ds(x, 1), :] * hy[0, pl.ds(x, 1), :], 0.0)
        return v + jnp.where(rowl, wy[1, pl.ds(x, 1), :] * hy[1, pl.ds(x, 1), :], 0.0)

    def first(x, accs):
        ax = inner_apply(xf[x], xf[below(x)], xf[above(x)], x)
        r = minus_faces(rf[x] - ax, x, hxx, hyx)
        r = r + jnp.where(x == 0, wx[0] * hxx[0], 0.0) + jnp.where(x == cx - 1, wx[1] * hxx[1], 0.0)
        rf[x] = r
        return tuple(accs[k] + fold(zf[k, x] * r) for k in range(nk))

    rest = lax.fori_loop(0, cx, first, tuple(jnp.zeros((8, 128), F32) for _ in range(nk)))

    z_halo[1]()
    for s in range(2):
        for k in range(nk):
            nx[s, k] = -(wx[s] * hxz[s, k])
            ny[s, k] = -(wy[s] * hyz[s, k])

    lane = iota((8, 128), 1)
    sub = iota((8, 128), 0)
    tile = jnp.zeros((8, 128), F32)
    for l in range(nk):
        v = total_rows([diag[pairs.index((min(k, l), max(k, l)))] for k in range(nk)])
        tile = tile + jnp.where(lane == 8 * a + l, v, 0.0)
    tb[0] = tile

    def off_blocks(l, carry):
        out = tb[0]
        for s in range(2):
            v = total_rows([fold(zf[k, s * (cx - 1)] * nx[s, l]) for k in range(nk)])
            at = 8 * (a + 2 * s - 1) + l
            out = out + jnp.where((lane == at) & (lane < 64), v, 0.0)
        v = total_rows([fold(pyz[0, k] * ny[0, l]) for k in range(nk)])
        tb[0] = out + jnp.where(lane == 64 + 8 * a + l, v, 0.0)
        return carry

    lax.fori_loop(0, nk, off_blocks, 0)

    ge[b, pl.ds(pl.multiple_of(8 * a, 8), 8), :] = tb[0]

    def spread(buf_at, own, count, peer_of, ssem, rsem):
        for o in range(1, count):
            pltpu.make_async_remote_copy(
                src_ref=own, dst_ref=own, send_sem=ssem, recv_sem=rsem,
                device_id=peer_of(o), device_id_type=mesh_id).start()

    def wait_bytes(ref, sem):
        pltpu.make_async_copy(ref, ref, sem).wait()

    gx_peer = lambda o: (lax.rem(a + o, na), b)
    gy_peer = lambda o: (a, lax.rem(b + o, nb))

    def message_rows(groups):
        out = jnp.zeros((1, 128), F32)
        for q, accs in groups:
            v = total_rows(accs)
            out = out + jnp.sum(jnp.where(lane == 8 * q + sub, v, 0.0), axis=0, keepdims=True)
        return jnp.where(sub == a, out, 0.0)

    def send_first(phase, groups):
        s1[phase, a] = message_rows(groups)
        spread(None, s1.at[phase, a], na, gx_peer, gs_sem.at[phase, 0], gr_sem.at[phase, 0])

    def send_second(phase):
        wait_bytes(s1.at[phase, pl.ds(0, na - 1)], gr_sem.at[phase, 0])
        t = s1[phase, 0]
        for i in range(1, na):
            t = t + s1[phase, i]
        gb[phase, b] = t
        spread(None, gb.at[phase, b], nb, gy_peer, gs_sem.at[phase, 1], gr_sem.at[phase, 1])

    def receive(phase):
        wait_bytes(gb.at[phase, pl.ds(0, nb - 1)], gr_sem.at[phase, 1])
        return jnp.transpose(gb[phase].reshape(na * nb, 128))

    mine = ge.at[b, pl.ds(pl.multiple_of(8 * a, 8), 8), :]
    spread(None, mine, na, gx_peer, es_sem.at[0], er_sem.at[0])
    send_first(0, [(0, list(rest))])
    wait_bytes(ge.at[0, pl.ds(0, 8 * (na - 1)), :], er_sem.at[0])
    spread(None, ge.at[b], nb, gy_peer, es_sem.at[1], er_sem.at[1])
    send_second(0)
    wait_bytes(ge.at[pl.ds(0, nb - 1)], er_sem.at[1])

    factor([ge[j] for j in range(nb)], d_ref, lu_ref, w_ref, y_ref, m_ref, x_ref, xt_ref, a, b, na, nb)

    def coarse(got):
        g = got[0:8]
        g = g + pltpu.roll(got[8:16], na * nb - 1, 1) + pltpu.roll(got[16:24], 1, 1)
        g = g + pltpu.roll(got[24:32], na * nb - na, 1) + pltpu.roll(got[32:40], na, 1)
        c = xt_ref[0] * g[0:1, :]
        for k in range(1, nk):
            c = c + xt_ref[k] * g[k : k + 1, :]
        c = jnp.sum(c, axis=1, keepdims=True)
        cc[...] = jnp.broadcast_to(c, (40, nz))
        for s in range(2):
            u = nx[s, 0] * cc[8 * s + 8 : 8 * s + 9, :]
            v = ny[s, 0] * cc[8 * s + 24 : 8 * s + 25, :]
            for k in range(1, nk):
                u = u + nx[s, k] * cc[8 * s + 8 + k : 8 * s + 9 + k, :]
                v = v + ny[s, k] * cc[8 * s + 24 + k : 8 * s + 25 + k, :]
            fcx[s] = u
            fcy[s] = v

    def span(vectors, x):
        out = vectors[0, x] * cc[0:1, :]
        for k in range(1, nk):
            out = out + vectors[k, x] * cc[k : k + 1, :]
        return out

    def image(x):
        out = span(az, x)
        out = out + jnp.where(row0, fcy[0, pl.ds(x, 1), :], 0.0) + jnp.where(rowl, fcy[1, pl.ds(x, 1), :], 0.0)
        return out + jnp.where(x == 0, fcx[0], 0.0) + jnp.where(x == cx - 1, fcx[1], 0.0)

    def scalar(got, row):
        return jnp.sum(got[row : row + 1, :], axis=1, keepdims=True)

    zero = jnp.zeros((8, 128), F32)

    def restrict_slab(x, r, slot, accs):
        v = r * rd[x]
        vf[x] = v
        pyv[slot, 0, pl.ds(x, 1), :] = v[0:1, :]
        pyv[slot, 1, pl.ds(x, 1), :] = v[cy - 1 : cy, :]
        return tuple(accs[k] + fold(az[k, x] * v) for k in range(nk)) + (accs[nk] + fold(r * v),)

    def finish_groups(slot, accs):
        groups = [(0, list(accs[:nk])), (5, [accs[nk]])]
        for s in range(2):
            groups.append((1 + s, [fold(nx[s, k] * vf[s * (cx - 1)]) for k in range(nk)]))
            groups.append((3 + s, [fold(ny[s, k] * pyv[slot, s]) for k in range(nk)]))
        return groups

    v_halos = [
        halo(3 + i, [vf.at[0], vf.at[cx - 1], pyv.at[i, 0], pyv.at[i, 1]],
             [hxv.at[i, 0], hxv.at[i, 1], hyv.at[i, 0], hyv.at[i, 1]])
        for i in range(2)
    ]

    got = receive(0)
    coarse(got)

    def deflate(x, accs):
        xf[x] = xf[x] + span(zf, x)
        r = rf[x] - image(x)
        rf[x] = r
        return restrict_slab(x, r, 0, accs)

    x_halo[2]()
    accs = lax.fori_loop(0, cx, deflate, (zero,) * (nk + 1))
    inner = None
    beta = None
    for it in range(3):
        if it < 2:
            v_halos[it][0]()
        send_first(1 + 2 * it, finish_groups(min(it, 1), accs))
        send_second(1 + 2 * it)
        if it < 2:
            v_halos[it][1]()
            hx, hy = hxv.at[it], hyv.at[it]

            def image_v(x, carry):
                w = inner_apply(vf[x], vf[below(x)], vf[above(x)], x)
                w = w - jnp.where(row0, wy[0, pl.ds(x, 1), :] * hy[0, pl.ds(x, 1), :], 0.0)
                w = w - jnp.where(rowl, wy[1, pl.ds(x, 1), :] * hy[1, pl.ds(x, 1), :], 0.0)
                w = w - jnp.where(x == 0, wx[0] * hx[0], 0.0) - jnp.where(x == cx - 1, wx[1] * hx[1], 0.0)
                wf[x] = w
                return carry

            lax.fori_loop(0, cx, image_v, 0)
        got = receive(1 + 2 * it)
        coarse(got)
        new = scalar(got, 40)
        beta = None if it == 0 else new / inner
        inner = new
        if it == 2:
            def last(x, carry):
                pf[x] = vf[x] + beta * pf[x] - span(zf, x)
                return carry

            lax.fori_loop(0, cx, last, 0)
            break

        def direction(x, acc):
            p = vf[x] - span(zf, x)
            q = wf[x] - image(x)
            if beta is not None:
                p = p + beta * pf[x]
                q = q + beta * qf[x]
            pf[x] = p
            qf[x] = q
            return acc + fold(p * q)

        acc = lax.fori_loop(0, cx, direction, zero)
        send_first(2 + 2 * it, [(0, [acc])])
        send_second(2 + 2 * it)
        got = receive(2 + 2 * it)
        step = inner / scalar(got, 0)
        v_halos[it][2]()

        def update(x, accs):
            xf[x] = xf[x] + step * pf[x]
            r = rf[x] - step * qf[x]
            rf[x] = r
            return restrict_slab(x, r, 1, accs)

        accs = lax.fori_loop(0, cx, update, (zero,) * (nk + 1))
        if it == 1:
            stores = [pltpu.make_async_copy(xf, sol_hbm, st_sem.at[0]), pltpu.make_async_copy(rf, res_hbm, st_sem.at[1])]
            for store in stores:
                store.start()
    store = pltpu.make_async_copy(pf, dir_hbm, st_sem.at[2])
    store.start()
    for h in (coef_halo, z_halo):
        h[2]()
    wait_bytes(ge.at[0, pl.ds(0, 8 * (na - 1)), :], es_sem.at[0])
    wait_bytes(ge.at[pl.ds(0, nb - 1)], es_sem.at[1])
    for phase in range(6):
        wait_bytes(s1.at[phase, pl.ds(0, na - 1)], gs_sem.at[phase, 0])
        wait_bytes(gb.at[phase, pl.ds(0, nb - 1)], gs_sem.at[phase, 1])
    for s in stores + [store]:
        s.wait()


def solution(mesh):
    na, nb = mesh.shape["gx"], mesh.shape["gy"]

    def per_device(right_side, start_field, coef, deflation):
        nk, cx, cy, nz = deflation.shape
        vm = lambda *shape: pltpu.VMEM(shape, F32)
        dma = lambda *shape: pltpu.SemaphoreType.DMA(shape)
        field = (cx, cy, nz)
        scratch = [
            vm(nk, *field), vm(nk, *field), vm(*field), vm(*field), vm(*field), vm(*field), vm(*field), vm(*field),
            vm(*field), vm(cx + 1, cy, nz), vm(*field), vm(*field), vm(*field), vm(*field), vm(*field), vm(*field),
            vm(2, cy, nz), vm(2, cx, nz),
            vm(2, nk, cy, nz), vm(2, nk, cx, nz), vm(2, cy, nz), vm(2, cx, nz), vm(2, cy, nz), vm(2, cx, nz),
            vm(2, 2, cy, nz), vm(2, 2, cx, nz),
            vm(2, nk, cx, nz), vm(2, cx, nz), vm(2, cx, nz), vm(2, 2, cx, nz),
            vm(2, nk, cy, nz), vm(2, nk, cx, nz), vm(2, cy, nz), vm(2, cx, nz),
            vm(40, nz), vm(nb, 64, 128), vm(6, na, 8, 128), vm(6, nb, 8, 128), vm(1, 8, 128),
            vm(nb, 64, 128), vm(nb, 64, 128), vm(nb, 64, 256), vm(nb, 64, 128), vm((nb // 2 + 1) // 2, 64, 128),
            vm(nb * 64, 128), vm(8, 40, 128),
            dma(4), dma(3), dma(5, 4), dma(5, 4), dma(2), dma(2), dma(6, 2), dma(6, 2),
        ]
        out = jax.ShapeDtypeStruct(field, F32)
        return pl.pallas_call(
            functools.partial(body, na, nb),
            out_shape=(out, out, out),
            in_specs=[pl.BlockSpec(memory_space=pl.ANY)] * 4,
            out_specs=(pl.BlockSpec(memory_space=pl.ANY),) * 3,
            scratch_shapes=scratch,
            compiler_params=pltpu.CompilerParams(
                collective_id=0, has_side_effects=True, vmem_limit_bytes=60000 * 1024),
            name="deflated_cg",
        )(right_side, start_field, coef, deflation)

    spec = P("gx", "gy", None)
    return jax.shard_map(
        per_device, mesh=mesh, in_specs=(spec, spec, spec, P(None, "gx", "gy", None)),
        out_specs=(spec, spec, spec), check_vma=False)
```

```python
import functools
import jax, jax.numpy as jnp
from jax import lax
from jax.experimental import pallas as pl
from jax.experimental.pallas import tpu as pltpu
from jax.sharding import PartitionSpec as P

F32 = jnp.float32
BF = jnp.bfloat16


def iota(shape, dim):
    return lax.broadcasted_iota(jnp.int32, shape, dim)


def split3(v):
    high = v.astype(BF)
    rest = v - high.astype(F32)
    mid = rest.astype(BF)
    low = (rest - mid.astype(F32)).astype(BF)
    return high, mid, low


def mm(left, right):
    lh, lm, ll = left
    rh, rm, rl = right
    d = lambda p, q: jnp.dot(p, q, preferred_element_type=F32)
    return d(lh, rh) + (d(lh, rm) + d(lm, rh)) + (d(lm, rm) + d(lh, rl) + d(ll, rh))


def invert_pairs(m_ref, count):
    lane = iota((8, 128), 1)
    sub = iota((8, 128), 0)
    half = lane // 64 * 64

    def panel(p, carry):
        start = pl.multiple_of(p * 8, 8)
        in_panel = (lane - half) // 8 == p
        ident = (lane - half - p * 8) == sub
        index = [half + p * 8 + j for j in range(8)]
        rows, piv = [], []
        for s in range(count):
            r = m_ref[s, pl.ds(start, 8), :]
            piv.append([jnp.take_along_axis(r, index[j], axis=1) for j in range(8)])
            rows.append(jnp.where(in_panel, jnp.where(ident, 1.0, 0.0), r))
        for t in range(8):
            own = sub == t
            for s in range(count):
                mult = piv[s][t]
                scale = 1.0 / mult[t : t + 1, :]
                row = rows[s][t : t + 1, :] * scale
                rows[s] = jnp.where(own, row, rows[s] - mult * row)
                for j in range(t + 1, 8):
                    prow = piv[s][j][t : t + 1, :] * scale
                    piv[s][j] = jnp.where(own, prow, piv[s][j] - mult * prow)
        for s in range(count):
            for v in range(8):
                block = m_ref[s, 8 * v : 8 * v + 8, :]
                terms = [jnp.take_along_axis(block, index[j], axis=1) * rows[s][j : j + 1, :] for j in range(8)]
                while len(terms) > 1:
                    terms = [terms[i] + terms[i + 1] for i in range(0, len(terms), 2)]
                m_ref[s, 8 * v : 8 * v + 8, :] = jnp.where(in_panel, 0.0, block) - terms[0]
        for s in range(count):
            m_ref[s, pl.ds(start, 8), :] = rows[s]
        return carry

    lax.fori_loop(0, 8, panel, 0)


def factor(tiles, d_ref, lu_ref, w_ref, y_ref, m_ref, x_ref, xt_ref, a, b, na, nb):
    lane = iota((64, 128), 1)
    rowi = iota((64, 128), 0)
    low = lane < 64
    group = lane // 8
    within = lane % 8
    own = (b * na + a) * 8
    target = jnp.where(group == 0, own, -4096)
    target = jnp.where((group == 1) & (a > 0), own - 8, target)
    target = jnp.where((group == 2) & (a < na - 1), own + 8, target)
    target = jnp.where((group == 3) & (b > 0), own - 64, target)
    target = jnp.where((group == 4) & (b < nb - 1), own + 64, target)
    target = target + within
    for j in range(nb):
        tile = tiles[j]
        d_ref[j] = tile
        y_ref[j] = jnp.where(rowi + 64 * j == target, 1.0, 0.0)
    for j in range(nb):
        left = pltpu.roll(tiles[j], 64, 1)
        if j < nb - 1:
            up = jnp.transpose(tiles[j + 1])[64:128, :]
            up = jnp.concatenate([jnp.zeros((64, 64), F32), up], axis=1)
        else:
            up = jnp.zeros((64, 128), F32)
        left = jnp.where(low, left, 0.0) if j > 0 else jnp.zeros((64, 128), F32)
        lu_ref[j] = jnp.where(low, left, up)

    def invert(lines):
        slots = (len(lines) + 1) // 2
        for s in range(slots):
            first = d_ref[lines[2 * s]]
            second = d_ref[lines[min(2 * s + 1, len(lines) - 1)]]
            m_ref[s] = jnp.where(low, first, pltpu.roll(second, 64, 1))
        invert_pairs(m_ref, slots)
        out = []
        for i in range(len(lines)):
            v = m_ref[i // 2]
            out.append(v[:, :64] if i % 2 == 0 else pltpu.roll(v, 64, 1)[:, :64])
        return out

    step = 1
    levels = []
    while step < nb:
        lines = list(range(step, nb, 2 * step))
        inverses = invert(lines)
        for j, inv in zip(lines, inverses):
            right = jnp.concatenate([lu_ref[j], y_ref[j]], axis=1)
            lut = jnp.transpose(lu_ref[j])
            w = mm(split3(inv), split3(right))
            w_ref[j] = w
            p = mm(split3(lut), split3(w))
            i, k = j - step, j + step
            d_ref[i] = d_ref[i] - p[:64, :128]
            y_ref[i] = y_ref[i] - p[:64, 128:]
            lu_ref[i] = jnp.where(low, lu_ref[i], -p[:64, :128])
            if k < nb:
                d_ref[k] = d_ref[k] - pltpu.roll(p[64:, :128], 64, 1)
                y_ref[k] = y_ref[k] - p[64:, 128:]
                lu_ref[k] = jnp.where(low, -p[64:, :128], lu_ref[k])
        levels.append((step, lines))
        step *= 2
    inv = invert([0])[0]
    x_ref[0:64] = mm(split3(inv), split3(y_ref[0]))
    for step, lines in reversed(levels):
        for j in lines:
            i, k = j - step, j + step
            below = x_ref[64 * i : 64 * i + 64]
            above = x_ref[64 * k : 64 * k + 64] if k < nb else jnp.zeros((64, 128), F32)
            both = jnp.concatenate([below, above], axis=0)
            w = w_ref[j]
            x_ref[64 * j : 64 * j + 64] = w[:, 128:] - mm(split3(w[:, :128]), split3(both))
    for k in range(8):
        xt_ref[k] = jnp.transpose(x_ref[pl.ds(k, na * nb, stride=8), :])[:40, :]


def total_rows(accs):
    sub = iota((8, 128), 0)
    out = jnp.zeros((8, 128), F32)
    for i, acc in enumerate(accs):
        out = jnp.where(sub == i, jnp.sum(acc, axis=0, keepdims=True), out)
    return jnp.broadcast_to(jnp.sum(out, axis=1, keepdims=True), (8, 128))


def fold(value):
    rows, cols = value.shape
    pieces = [value[8 * i : 8 * i + 8, 128 * j : 128 * j + 128] for i in range(rows // 8) for j in range(cols // 128)]
    while len(pieces) > 1:
        pieces = [pieces[i] + pieces[i + 1] if i + 1 < len(pieces) else pieces[i] for i in range(0, len(pieces), 2)]
    return pieces[0]


def face_of(lower, upper):
    summed = lower + upper
    return jnp.where((lower > 0.0) & (upper > 0.0), 2.0 * lower * upper / summed, summed)


def body(na, nb, rhs_hbm, x0_hbm, c_hbm, z_hbm, sol_hbm, res_hbm, dir_hbm, *scratch):
    (zf, az, cf, xf, rf, vf, wf, uf, tf, pf, qf, ph, qh, fx, fyl, fyh, fzl, fzh, dg, rd,
     wx, wy, hxz, hyz, hxc, hyc, hxx, hyx, hxv, hyv, pyz, pyc, pyx, pyv, nx, ny, fcx, fcy,
     cc, ge, es, et, s1, gb, tb,
     d_ref, lu_ref, w_ref, y_ref, m_ref, x_ref, xt_ref,
     ld_sem, st_sem, hs_sem, hr_sem, es_sem, er_sem, gs_sem, gr_sem) = scratch
    cx, cy, nz = cf.shape
    nk = zf.shape[0]
    a = lax.axis_index("gx")
    b = lax.axis_index("gy")
    mesh_id = pl.DeviceIdType.MESH
    loads = [
        pltpu.make_async_copy(c_hbm, cf, ld_sem.at[0]),
        pltpu.make_async_copy(x0_hbm, xf, ld_sem.at[1]),
        pltpu.make_async_copy(rhs_hbm, rf, ld_sem.at[2]),
        pltpu.make_async_copy(z_hbm, zf, ld_sem.at[3]),
    ]
    for load in loads:
        load.start()
    barrier = pltpu.get_barrier_semaphore()
    for o in range(1, na):
        pl.semaphore_signal(barrier, inc=1, device_id=(lax.rem(a + o, na), b), device_id_type=mesh_id)
    for o in range(1, nb):
        pl.semaphore_signal(barrier, inc=1, device_id=(a, lax.rem(b + o, nb)), device_id_type=mesh_id)

    has = [a > 0, a < na - 1, b > 0, b < nb - 1]
    peers = [(a - 1, b), (a + 1, b), (a, b - 1), (a, b + 1)]

    def halo(slot, sources, targets):
        def copy(s):
            return pltpu.make_async_remote_copy(
                src_ref=sources[s], dst_ref=targets[s ^ 1],
                send_sem=hs_sem.at[slot, s], recv_sem=hr_sem.at[slot, s ^ 1],
                device_id=peers[s], device_id_type=mesh_id)

        def start():
            for s in range(4):
                @pl.when(has[s])
                def _():
                    copy(s).start()

        def wait_recv():
            for s in range(4):
                @pl.when(has[s])
                def _():
                    pltpu.make_async_remote_copy(
                        src_ref=sources[s], dst_ref=targets[s],
                        send_sem=hs_sem.at[slot, s], recv_sem=hr_sem.at[slot, s],
                        device_id=peers[s], device_id_type=mesh_id).wait_recv()

        def wait_send():
            for s in range(4):
                @pl.when(has[s])
                def _():
                    copy(s).wait_send()

        return start, wait_recv, wait_send

    row0 = iota((cy, nz), 0) == 0
    rowl = iota((cy, nz), 0) == cy - 1
    lan0 = iota((cy, nz), 1) == 0
    lanl = iota((cy, nz), 1) == nz - 1

    for s in range(2):
        @pl.when(jnp.logical_not(has[s]))
        def _():
            hxz[s] = jnp.zeros(hxz.shape[1:], F32)
            hxc[s] = jnp.zeros(hxc.shape[1:], F32)
            hxx[s] = jnp.zeros(hxx.shape[1:], F32)
            for i in range(2):
                hxv[i, s] = jnp.zeros(hxv.shape[2:], F32)

        @pl.when(jnp.logical_not(has[2 + s]))
        def _():
            hyz[s] = jnp.zeros(hyz.shape[1:], F32)
            hyc[s] = jnp.zeros(hyc.shape[1:], F32)
            hyx[s] = jnp.zeros(hyx.shape[1:], F32)
            for i in range(2):
                hyv[i, s] = jnp.zeros(hyv.shape[2:], F32)

    loads[0].wait()

    def pack(x, carry):
        pyc[0, pl.ds(x, 1), :] = cf[x, 0:1, :]
        pyc[1, pl.ds(x, 1), :] = cf[x, cy - 1 : cy, :]
        return carry

    lax.fori_loop(0, cx, pack, 0)

    fx[0] = jnp.zeros((cy, nz), F32)
    fx[cx] = jnp.zeros((cy, nz), F32)

    def faces_x(x, carry):
        fx[x] = face_of(cf[x - 1], cf[x])
        return carry

    lax.fori_loop(1, cx, faces_x, 0)

    def faces(x, carry):
        c = cf[x]
        yl = jnp.where(row0, 0.0, face_of(pltpu.roll(c, 1, 0), c))
        yh = jnp.where(rowl, 0.0, face_of(c, pltpu.roll(c, cy - 1, 0)))
        zl = jnp.where(lan0, c, face_of(pltpu.roll(c, 1, 1), c))
        zh = jnp.where(lanl, c, face_of(c, pltpu.roll(c, nz - 1, 1)))
        dg[x] = fx[x] + fx[x + 1] + yl + yh + zl + zh
        fyl[x] = yl
        fyh[x] = yh
        fzl[x] = jnp.where(lan0, 0.0, zl)
        fzh[x] = jnp.where(lanl, 0.0, zh)
        return carry

    lax.fori_loop(0, cx, faces, 0)

    pl.semaphore_wait(barrier, na + nb - 2)
    coef_halo = halo(0, [cf.at[0], cf.at[cx - 1], pyc.at[0], pyc.at[1]], [hxc.at[0], hxc.at[1], hyc.at[0], hyc.at[1]])
    coef_halo[0]()
    loads[3].wait()

    def packz(x, carry):
        for k in range(nk):
            pyz[0, k, pl.ds(x, 1), :] = zf[k, x, 0:1, :]
            pyz[1, k, pl.ds(x, 1), :] = zf[k, x, cy - 1 : cy, :]
        return carry

    lax.fori_loop(0, cx, packz, 0)
    z_halo = halo(2, [zf.at[:, 0], zf.at[:, cx - 1], pyz.at[0], pyz.at[1]], [hxz.at[0], hxz.at[1], hyz.at[0], hyz.at[1]])
    z_halo[0]()
    loads[1].wait()

    def packx(x, carry):
        pyx[0, pl.ds(x, 1), :] = xf[x, 0:1, :]
        pyx[1, pl.ds(x, 1), :] = xf[x, cy - 1 : cy, :]
        return carry

    lax.fori_loop(0, cx, packx, 0)
    x_halo = halo(1, [xf.at[0], xf.at[cx - 1], pyx.at[0], pyx.at[1]], [hxx.at[0], hxx.at[1], hyx.at[0], hyx.at[1]])
    x_halo[0]()

    def inner_apply(v, before, after, x):
        near = fx[x] * before + fx[x + 1] * after
        near = near + fyl[x] * pltpu.roll(v, 1, 0) + fyh[x] * pltpu.roll(v, cy - 1, 0)
        near = near + fzl[x] * pltpu.roll(v, 1, 1) + fzh[x] * pltpu.roll(v, nz - 1, 1)
        return dg[x] * v - near

    def below(x):
        return jnp.maximum(x - 1, 0)

    def above(x):
        return jnp.minimum(x + 1, cx - 1)

    def make_az(x, carry):
        for k in range(nk):
            az[k, x] = inner_apply(zf[k, x], zf[k, below(x)], zf[k, above(x)], x)
        return carry

    lax.fori_loop(0, cx, make_az, 0)

    coef_halo[1]()
    for s in range(2):
        wx[s] = face_of(cf[s * (cx - 1)], hxc[s])
        wy[s] = face_of(pyc[s], hyc[s])
        dg[s * (cx - 1)] = dg[s * (cx - 1)] + wx[s]
        for k in range(nk):
            az[k, s * (cx - 1)] = az[k, s * (cx - 1)] + wx[s] * zf[k, s * (cx - 1)]
    top8 = iota((8, nz), 0) == 0
    bot8 = iota((8, nz), 0) == 7

    def fix(x, carry):
        lo = jnp.where(top8, wy[0, pl.ds(x, 1), :], 0.0)
        hi = jnp.where(bot8, wy[1, pl.ds(x, 1), :], 0.0)
        dg[x, 0:8, :] = dg[x, 0:8, :] + lo
        dg[x, cy - 8 : cy, :] = dg[x, cy - 8 : cy, :] + hi
        for k in range(nk):
            az[k, x, 0:8, :] = az[k, x, 0:8, :] + lo * zf[k, x, 0:8, :]
            az[k, x, cy - 8 : cy, :] = az[k, x, cy - 8 : cy, :] + hi * zf[k, x, cy - 8 : cy, :]
        rd[x] = 1.0 / dg[x]
        return carry

    lax.fori_loop(0, cx, fix, 0)

    pairs = [(k, l) for k in range(nk) for l in range(k, nk)]

    def gram(x, accs):
        accs = list(accs)
        for i in range(cy // 8):
            for j in range(nz // 128):
                zs = [zf[k, x, 8 * i : 8 * i + 8, 128 * j : 128 * j + 128] for k in range(nk)]
                for l in range(nk):
                    w = az[l, x, 8 * i : 8 * i + 8, 128 * j : 128 * j + 128]
                    for k in range(l + 1):
                        n = pairs.index((k, l))
                        accs[n] = accs[n] + zs[k] * w
        return tuple(accs)

    diag = lax.fori_loop(0, cx, gram, tuple(jnp.zeros((8, 128), F32) for _ in pairs))

    z_halo[1]()
    for s in range(2):
        for k in range(nk):
            nx[s, k] = -(wx[s] * hxz[s, k])
            ny[s, k] = -(wy[s] * hyz[s, k])

    lane = iota((8, 128), 1)
    sub = iota((8, 128), 0)
    base = lax.rem(a, 4) * 32
    tile = jnp.zeros((8, 128), F32)
    for l in range(nk):
        v = total_rows([diag[pairs.index((min(k, l), max(k, l)))] for k in range(nk)])
        tile = tile + jnp.where(lane == base + 8 + l, v, 0.0)
    tb[0] = tile

    def off_blocks(l, carry):
        out = tb[0]
        for s in range(2):
            v = total_rows([fold(zf[k, s * (cx - 1)] * nx[s, l]) for k in range(nk)])
            out = out + jnp.where(lane == base + 16 * s + l, v, 0.0)
        v = total_rows([fold(pyz[0, k] * ny[0, l]) for k in range(nk)])
        tb[0] = out + jnp.where(lane == base + 24 + l, v, 0.0)
        return carry

    lax.fori_loop(0, nk, off_blocks, 0)

    es[a] = tb[0]

    def spread(buf_at, own, count, peer_of, ssem, rsem):
        for o in range(1, count):
            pltpu.make_async_remote_copy(
                src_ref=own, dst_ref=own, send_sem=ssem, recv_sem=rsem,
                device_id=peer_of(o), device_id_type=mesh_id).start()

    def wait_bytes(ref, sem):
        pltpu.make_async_copy(ref, ref, sem).wait()

    gx_peer = lambda o: (lax.rem(a + o, na), b)
    gy_peer = lambda o: (a, lax.rem(b + o, nb))

    def message_rows(groups):
        out = jnp.zeros((1, 128), F32)
        for q, accs in groups:
            v = total_rows(accs)
            out = out + jnp.sum(jnp.where(lane == 8 * q + sub, v, 0.0), axis=0, keepdims=True)
        return jnp.where(sub == a, out, 0.0)

    def send_first(phase, groups):
        s1[phase, a] = message_rows(groups)
        spread(None, s1.at[phase, a], na, gx_peer, gs_sem.at[phase, 0], gr_sem.at[phase, 0])

    def send_second(phase):
        wait_bytes(s1.at[phase, pl.ds(0, na - 1)], gr_sem.at[phase, 0])
        t = s1[phase, 0]
        for i in range(1, na):
            t = t + s1[phase, i]
        gb[phase, b] = t
        spread(None, gb.at[phase, b], nb, gy_peer, gs_sem.at[phase, 1], gr_sem.at[phase, 1])

    def receive(phase):
        wait_bytes(gb.at[phase, pl.ds(0, nb - 1)], gr_sem.at[phase, 1])
        return jnp.transpose(gb[phase].reshape(na * nb, 128))

    spread(None, es.at[a], na, gx_peer, es_sem.at[0], er_sem.at[0])
    x_halo[1]()
    loads[2].wait()

    def minus_faces(v, x, hx, hy):
        v = v + jnp.where(row0, wy[0, pl.ds(x, 1), :] * hy[0, pl.ds(x, 1), :], 0.0)
        return v + jnp.where(rowl, wy[1, pl.ds(x, 1), :] * hy[1, pl.ds(x, 1), :], 0.0)

    def first(x, accs):
        ax = inner_apply(xf[x], xf[below(x)], xf[above(x)], x)
        r = minus_faces(rf[x] - ax, x, hxx, hyx)
        r = r + jnp.where(x == 0, wx[0] * hxx[0], 0.0) + jnp.where(x == cx - 1, wx[1] * hxx[1], 0.0)
        rf[x] = r
        return tuple(accs[k] + fold(zf[k, x] * r) for k in range(nk))

    rest = lax.fori_loop(0, cx, first, tuple(jnp.zeros((8, 128), F32) for _ in range(nk)))

    send_first(0, [(0, list(rest))])
    wait_bytes(es.at[pl.ds(0, na - 1)], er_sem.at[0])
    et[b, 0:8, :] = es[0] + es[1] + es[2] + es[3]
    et[b, 8:16, :] = es[4] + es[5] + es[6] + es[7]
    spread(None, et.at[b], nb, gy_peer, es_sem.at[1], er_sem.at[1])
    send_second(0)
    wait_bytes(et.at[pl.ds(0, nb - 1)], er_sem.at[1])

    def expand(j, carry):
        for i in range(na):
            packed = et[j, 8 * (i // 4) : 8 * (i // 4) + 8, :]
            at = 32 * (i % 4)
            near = pltpu.roll(packed, (8 * i - 8 - at) % 128, 1)
            side = pltpu.roll(packed, (40 + 8 * i - at) % 128, 1)
            out = jnp.where((lane >= 64 + 8 * i) & (lane < 72 + 8 * i), side, 0.0)
            out = jnp.where((lane >= 8 * i - 8) & (lane < 8 * i + 16) & (lane < 64), near, out)
            ge[j, 8 * i : 8 * i + 8, :] = out
        return carry

    lax.fori_loop(0, nb, expand, 0)

    factor([ge[j] for j in range(nb)], d_ref, lu_ref, w_ref, y_ref, m_ref, x_ref, xt_ref, a, b, na, nb)

    def coarse_of(got):
        g = got[0:8]
        g = g + pltpu.roll(got[8:16], na * nb - 1, 1) + pltpu.roll(got[16:24], 1, 1)
        g = g + pltpu.roll(got[24:32], na * nb - na, 1) + pltpu.roll(got[32:40], na, 1)
        c = xt_ref[0] * g[0:1, :]
        for k in range(1, nk):
            c = c + xt_ref[k] * g[k : k + 1, :]
        return jnp.broadcast_to(jnp.sum(c, axis=1, keepdims=True), (40, nz))

    def keep(c):
        cc[...] = c
        for s in range(2):
            u = nx[s, 0] * cc[8 * s + 8 : 8 * s + 9, :]
            v = ny[s, 0] * cc[8 * s + 24 : 8 * s + 25, :]
            for k in range(1, nk):
                u = u + nx[s, k] * cc[8 * s + 8 + k : 8 * s + 9 + k, :]
                v = v + ny[s, k] * cc[8 * s + 24 + k : 8 * s + 25 + k, :]
            fcx[s] = u
            fcy[s] = v

    def span(vectors, x):
        out = vectors[0, x] * cc[0:1, :]
        for k in range(1, nk):
            out = out + vectors[k, x] * cc[k : k + 1, :]
        return out

    def image(x):
        out = span(az, x)
        out = out + jnp.where(row0, fcy[0, pl.ds(x, 1), :], 0.0) + jnp.where(rowl, fcy[1, pl.ds(x, 1), :], 0.0)
        return out + jnp.where(x == 0, fcx[0], 0.0) + jnp.where(x == cx - 1, fcx[1], 0.0)

    def scalar(got, row):
        return jnp.sum(got[row : row + 1, :], axis=1, keepdims=True)

    zero = jnp.zeros((8, 128), F32)

    def restrict_slab(x, v, field, slot, accs):
        field[x] = v
        pyv[slot, 0, pl.ds(x, 1), :] = v[0:1, :]
        pyv[slot, 1, pl.ds(x, 1), :] = v[cy - 1 : cy, :]
        return tuple(accs[k] + fold(az[k, x] * v) for k in range(nk))

    def finish_groups(field, slot, accs):
        groups = [(0, list(accs[:nk])), (5, list(accs[nk:]))]
        for s in range(2):
            groups.append((1 + s, [fold(nx[s, k] * field[s * (cx - 1)]) for k in range(nk)]))
            groups.append((3 + s, [fold(ny[s, k] * pyv[slot, s]) for k in range(nk)]))
        return groups

    fields = [vf, uf]
    v_halos = [
        halo(3 + i, [fields[i].at[0], fields[i].at[cx - 1], pyv.at[i, 0], pyv.at[i, 1]],
             [hxv.at[i, 0], hxv.at[i, 1], hyv.at[i, 0], hyv.at[i, 1]])
        for i in range(2)
    ]

    def apply_all(i, out):
        field, hx, hy = fields[i], hxv.at[i], hyv.at[i]

        def slab(x, carry):
            w = inner_apply(field[x], field[below(x)], field[above(x)], x)
            w = w - jnp.where(row0, wy[0, pl.ds(x, 1), :] * hy[0, pl.ds(x, 1), :], 0.0)
            w = w - jnp.where(rowl, wy[1, pl.ds(x, 1), :] * hy[1, pl.ds(x, 1), :], 0.0)
            out[x] = w - jnp.where(x == 0, wx[0] * hx[0], 0.0) - jnp.where(x == cx - 1, wx[1] * hx[1], 0.0)
            return carry

        lax.fori_loop(0, cx, slab, 0)

    keep(coarse_of(receive(0)))
    x_halo[2]()

    def deflate(x, accs):
        xf[x] = xf[x] + span(zf, x)
        r = rf[x] - image(x)
        rf[x] = r
        v = r * rd[x]
        return restrict_slab(x, v, vf, 0, accs) + (accs[nk] + fold(r * v),)

    accs = lax.fori_loop(0, cx, deflate, (zero,) * (nk + 1))
    v_halos[0][0]()
    send_first(1, finish_groups(vf, 0, accs))
    send_second(1)
    v_halos[0][1]()
    apply_all(0, wf)
    got = receive(1)
    keep(coarse_of(got))
    inner = scalar(got, 40)

    def sums(x, p, q, v, slot, accs):
        u = q * rd[x]
        more = (accs[nk] + fold(p * q), accs[nk + 1] + fold(q * v), accs[nk + 2] + fold(q * u))
        return restrict_slab(x, u, uf, slot, accs) + more

    def direction(x, accs):
        v = vf[x]
        p = v - span(zf, x)
        q = wf[x] - image(x)
        pf[x] = p
        qf[x] = q
        return sums(x, p, q, v, 1, accs)

    accs = lax.fori_loop(0, cx, direction, (zero,) * (nk + 3))
    v_halos[1][0]()
    send_first(2, finish_groups(uf, 1, accs))
    send_second(2)
    v_halos[0][2]()
    v_halos[1][1]()
    apply_all(1, tf)

    def advance(got, inner):
        step = inner / scalar(got, 40)
        new = inner - 2.0 * step * scalar(got, 41) + step * step * scalar(got, 42)
        keep(cc[...] - step * coarse_of(got))
        return step, new, new / inner

    got = receive(2)
    step, inner, beta = advance(got, inner)
    v_halos[1][2]()

    def next_direction(x, accs):
        v = vf[x] - step * uf[x]
        vf[x] = v
        p = v + beta * pf[x] - span(zf, x)
        q = wf[x] - step * tf[x] + beta * qf[x] - image(x)
        ph[x] = p
        qh[x] = q
        return sums(x, p, q, v, 2, accs)

    accs = lax.fori_loop(0, cx, next_direction, (zero,) * (nk + 3))
    send_first(3, finish_groups(uf, 2, accs))
    send_second(3)

    def move(x, carry):
        xf[x] = xf[x] + step * pf[x]
        rf[x] = rf[x] - step * qf[x]
        return carry

    lax.fori_loop(0, cx, move, 0)
    got = receive(3)
    last_step, inner, beta = advance(got, inner)

    def last_move(x, carry):
        xf[x] = xf[x] + last_step * ph[x]
        rf[x] = rf[x] - last_step * qh[x]
        return carry

    def last(x, carry):
        pf[x] = vf[x] - last_step * uf[x] + beta * ph[x] - span(zf, x)
        return carry

    lax.fori_loop(0, cx, last_move, 0)
    stores = [
        pltpu.make_async_copy(xf, sol_hbm, st_sem.at[0]),
        pltpu.make_async_copy(rf, res_hbm, st_sem.at[1]),
        pltpu.make_async_copy(pf, dir_hbm, st_sem.at[2]),
    ]
    stores[0].start()
    stores[1].start()
    lax.fori_loop(0, cx, last, 0)
    stores[2].start()
    for h in (coef_halo, z_halo):
        h[2]()
    wait_bytes(es.at[pl.ds(0, na - 1)], es_sem.at[0])
    wait_bytes(et.at[pl.ds(0, nb - 1)], es_sem.at[1])
    for phase in range(4):
        wait_bytes(s1.at[phase, pl.ds(0, na - 1)], gs_sem.at[phase, 0])
        wait_bytes(gb.at[phase, pl.ds(0, nb - 1)], gs_sem.at[phase, 1])
    for store in stores:
        store.wait()


def solution(mesh):
    na, nb = mesh.shape["gx"], mesh.shape["gy"]

    def per_device(right_side, start_field, coef, deflation):
        nk, cx, cy, nz = deflation.shape
        vm = lambda *shape: pltpu.VMEM(shape, F32)
        dma = lambda *shape: pltpu.SemaphoreType.DMA(shape)
        field = (cx, cy, nz)
        scratch = [
            vm(nk, *field), vm(nk, *field)] + [vm(*field) for _ in range(11)] + [
            vm(cx + 1, cy, nz), vm(*field), vm(*field), vm(*field), vm(*field), vm(*field), vm(*field),
            vm(2, cy, nz), vm(2, cx, nz),
            vm(2, nk, cy, nz), vm(2, nk, cx, nz), vm(2, cy, nz), vm(2, cx, nz), vm(2, cy, nz), vm(2, cx, nz),
            vm(2, 2, cy, nz), vm(2, 2, cx, nz),
            vm(2, nk, cx, nz), vm(2, cx, nz), vm(2, cx, nz), vm(3, 2, cx, nz),
            vm(2, nk, cy, nz), vm(2, nk, cx, nz), vm(2, cy, nz), vm(2, cx, nz),
            vm(40, nz), vm(nb, 64, 128), vm(na, 8, 128), vm(nb, 16, 128), vm(4, na, 8, 128), vm(4, nb, 8, 128), vm(1, 8, 128),
            vm(nb, 64, 128), vm(nb, 64, 128), vm(nb, 64, 256), vm(nb, 64, 128), vm((nb // 2 + 1) // 2, 64, 128),
            vm(nb * 64, 128), vm(8, 40, 128),
            dma(4), dma(3), dma(5, 4), dma(5, 4), dma(2), dma(2), dma(4, 2), dma(4, 2),
        ]
        out = jax.ShapeDtypeStruct(field, F32)
        return pl.pallas_call(
            functools.partial(body, na, nb),
            out_shape=(out, out, out),
            in_specs=[pl.BlockSpec(memory_space=pl.ANY)] * 4,
            out_specs=(pl.BlockSpec(memory_space=pl.ANY),) * 3,
            scratch_shapes=scratch,
            compiler_params=pltpu.CompilerParams(
                collective_id=0, has_side_effects=True, vmem_limit_bytes=60000 * 1024),
            name="deflated_cg",
        )(right_side, start_field, coef, deflation)

    spec = P("gx", "gy", None)
    return jax.shard_map(
        per_device, mesh=mesh, in_specs=(spec, spec, spec, P(None, "gx", "gy", None)),
        out_specs=(spec, spec, spec), check_vma=False)
```

```python
import functools
import jax, jax.numpy as jnp
from jax import lax
from jax.experimental import pallas as pl
from jax.experimental.pallas import tpu as pltpu
from jax.sharding import PartitionSpec as P

F32 = jnp.float32
BF = jnp.bfloat16


def iota(shape, dim):
    return lax.broadcasted_iota(jnp.int32, shape, dim)


def split3(v):
    high = v.astype(BF)
    rest = v - high.astype(F32)
    mid = rest.astype(BF)
    low = (rest - mid.astype(F32)).astype(BF)
    return high, mid, low


def mm(left, right):
    lh, lm, ll = left
    rh, rm, rl = right
    d = lambda p, q: jnp.dot(p, q, preferred_element_type=F32)
    return d(lh, rh) + (d(lh, rm) + d(lm, rh)) + (d(lm, rm) + d(lh, rl) + d(ll, rh))


def invert_pairs(m_ref, count):
    lane = iota((8, 128), 1)
    sub = iota((8, 128), 0)
    half = lane // 64 * 64
    left = lane < 64

    def panel(p, carry):
        start = pl.multiple_of(p * 8, 8)
        in_panel = (lane - half) // 8 == p
        done = (lane - half) // 8 < p
        ident = (lane - half - p * 8) == sub
        index = [half + p * 8 + j for j in range(8)]
        rows, piv, cols = [], [], []
        for s in range(count):
            r = m_ref[s, pl.ds(start, 8), :]
            piv.append([jnp.take_along_axis(r, index[j], axis=1) for j in range(8)])
            rows.append(jnp.where(in_panel, jnp.where(ident, 1.0, 0.0), r))
            if count > 1:
                flip = jnp.where(done, -r, r)
                c = jnp.concatenate([flip[:, :64], pltpu.roll(flip, 64, 1)[:, :64]], axis=0)
                ch, cm, cl = split3(c)
                cols.append(jnp.transpose(jnp.concatenate([ch, ch, cm, cm, ch, cl], axis=0).astype(F32)).astype(BF))
        for t in range(8):
            own = sub == t
            for s in range(count):
                mult = piv[s][t]
                scale = 1.0 / mult[t : t + 1, :]
                row = rows[s][t : t + 1, :] * scale
                rows[s] = jnp.where(own, row, rows[s] - mult * row)
                for j in range(t + 1, 8):
                    prow = piv[s][j][t : t + 1, :] * scale
                    piv[s][j] = jnp.where(own, prow, piv[s][j] - mult * prow)
        if count > 1:
            wide = iota((64, 128), 1)
            wide_panel = (wide - wide // 64 * 64) // 8 == p
            for s in range(count):
                r = jnp.concatenate([jnp.where(left, rows[s], 0.0), jnp.where(left, 0.0, rows[s])], axis=0)
                rh, rm, rl = split3(r)
                right = jnp.concatenate([rh, rm, rh, rm, rl, rh], axis=0)
                m_ref[s] = jnp.where(wide_panel, 0.0, m_ref[s]) - jnp.dot(cols[s], right, preferred_element_type=F32)
        else:
            for s in range(count):
                for v in range(8):
                    block = m_ref[s, 8 * v : 8 * v + 8, :]
                    terms = [jnp.take_along_axis(block, index[j], axis=1) * rows[s][j : j + 1, :] for j in range(8)]
                    while len(terms) > 1:
                        terms = [terms[i] + terms[i + 1] for i in range(0, len(terms), 2)]
                    m_ref[s, 8 * v : 8 * v + 8, :] = jnp.where(in_panel, 0.0, block) - terms[0]
        for s in range(count):
            m_ref[s, pl.ds(start, 8), :] = rows[s]
        return carry

    lax.fori_loop(0, 8, panel, 0)


def factor(tiles, d_ref, lu_ref, w_ref, y_ref, m_ref, x_ref, xt_ref, a, b, na, nb):
    lane = iota((64, 128), 1)
    rowi = iota((64, 128), 0)
    low = lane < 64
    group = lane // 8
    within = lane % 8
    own = (b * na + a) * 8
    target = jnp.where(group == 0, own, -4096)
    target = jnp.where((group == 1) & (a > 0), own - 8, target)
    target = jnp.where((group == 2) & (a < na - 1), own + 8, target)
    target = jnp.where((group == 3) & (b > 0), own - 64, target)
    target = jnp.where((group == 4) & (b < nb - 1), own + 64, target)
    target = target + within
    for j in range(nb):
        tile = tiles[j]
        d_ref[j] = tile
        y_ref[j] = jnp.where(rowi + 64 * j == target, 1.0, 0.0)
    for j in range(nb):
        left = pltpu.roll(tiles[j], 64, 1)
        if j < nb - 1:
            up = jnp.transpose(tiles[j + 1])[64:128, :]
            up = jnp.concatenate([jnp.zeros((64, 64), F32), up], axis=1)
        else:
            up = jnp.zeros((64, 128), F32)
        left = jnp.where(low, left, 0.0) if j > 0 else jnp.zeros((64, 128), F32)
        lu_ref[j] = jnp.where(low, left, up)

    def invert(lines):
        slots = (len(lines) + 1) // 2
        for s in range(slots):
            first = d_ref[lines[2 * s]]
            second = d_ref[lines[min(2 * s + 1, len(lines) - 1)]]
            m_ref[s] = jnp.where(low, first, pltpu.roll(second, 64, 1))
        invert_pairs(m_ref, slots)
        out = []
        for i in range(len(lines)):
            v = m_ref[i // 2]
            out.append(v[:, :64] if i % 2 == 0 else pltpu.roll(v, 64, 1)[:, :64])
        return out

    step = 1
    levels = []
    while step < nb:
        lines = list(range(step, nb, 2 * step))
        inverses = invert(lines)
        for j, inv in zip(lines, inverses):
            right = jnp.concatenate([lu_ref[j], y_ref[j]], axis=1)
            lut = jnp.transpose(lu_ref[j])
            w = mm(split3(inv), split3(right))
            w_ref[j] = w
            p = mm(split3(lut), split3(w))
            i, k = j - step, j + step
            d_ref[i] = d_ref[i] - p[:64, :128]
            y_ref[i] = y_ref[i] - p[:64, 128:]
            lu_ref[i] = jnp.where(low, lu_ref[i], -p[:64, :128])
            if k < nb:
                d_ref[k] = d_ref[k] - pltpu.roll(p[64:, :128], 64, 1)
                y_ref[k] = y_ref[k] - p[64:, 128:]
                lu_ref[k] = jnp.where(low, -p[64:, :128], lu_ref[k])
        levels.append((step, lines))
        step *= 2
    inv = invert([0])[0]
    x_ref[0:64] = mm(split3(inv), split3(y_ref[0]))
    for step, lines in reversed(levels):
        for j in lines:
            i, k = j - step, j + step
            below = x_ref[64 * i : 64 * i + 64]
            above = x_ref[64 * k : 64 * k + 64] if k < nb else jnp.zeros((64, 128), F32)
            both = jnp.concatenate([below, above], axis=0)
            w = w_ref[j]
            x_ref[64 * j : 64 * j + 64] = w[:, 128:] - mm(split3(w[:, :128]), split3(both))
    for k in range(8):
        xt_ref[k] = jnp.transpose(x_ref[pl.ds(k, na * nb, stride=8), :])[:40, :]


def total_rows(accs):
    sub = iota((8, 128), 0)
    out = jnp.zeros((8, 128), F32)
    for i, acc in enumerate(accs):
        out = jnp.where(sub == i, jnp.sum(acc, axis=0, keepdims=True), out)
    return jnp.broadcast_to(jnp.sum(out, axis=1, keepdims=True), (8, 128))


def fold(value):
    rows, cols = value.shape
    pieces = [value[8 * i : 8 * i + 8, 128 * j : 128 * j + 128] for i in range(rows // 8) for j in range(cols // 128)]
    while len(pieces) > 1:
        pieces = [pieces[i] + pieces[i + 1] if i + 1 < len(pieces) else pieces[i] for i in range(0, len(pieces), 2)]
    return pieces[0]


def face_of(lower, upper):
    summed = lower + upper
    return jnp.where((lower > 0.0) & (upper > 0.0), 2.0 * lower * upper / summed, summed)


def body(na, nb, rhs_hbm, x0_hbm, c_hbm, z_hbm, sol_hbm, res_hbm, dir_hbm, *scratch):
    (zf, az, cf, xf, rf, vf, wf, uf, tf, pf, qf, ph, qh, fx, fyl, fyh, fzl, fzh, dg, rd,
     wx, wy, hxz, hyz, hxc, hyc, hxx, hyx, hxv, hyv, pyz, pyc, pyx, pyv, nx, ny, fcx, fcy,
     cc, ge, es, et, gb, tb,
     d_ref, lu_ref, w_ref, y_ref, m_ref, x_ref, xt_ref,
     ld_sem, st_sem, hs_sem, hr_sem, es_sem, er_sem, gs_sem, gr_sem) = scratch
    cx, cy, nz = cf.shape
    nk = zf.shape[0]
    a = lax.axis_index("gx")
    b = lax.axis_index("gy")
    mesh_id = pl.DeviceIdType.MESH
    loads = [
        pltpu.make_async_copy(c_hbm, cf, ld_sem.at[0]),
        pltpu.make_async_copy(x0_hbm, xf, ld_sem.at[1]),
        pltpu.make_async_copy(rhs_hbm, rf, ld_sem.at[2]),
        pltpu.make_async_copy(z_hbm, zf, ld_sem.at[3]),
    ]
    for load in loads:
        load.start()
    barrier = pltpu.get_barrier_semaphore()
    for o in range(1, na):
        pl.semaphore_signal(barrier, inc=1, device_id=(lax.rem(a + o, na), b), device_id_type=mesh_id)
    for o in range(1, nb):
        pl.semaphore_signal(barrier, inc=1, device_id=(a, lax.rem(b + o, nb)), device_id_type=mesh_id)

    has = [a > 0, a < na - 1, b > 0, b < nb - 1]
    peers = [(a - 1, b), (a + 1, b), (a, b - 1), (a, b + 1)]

    def halo(slot, sources, targets):
        def copy(s):
            return pltpu.make_async_remote_copy(
                src_ref=sources[s], dst_ref=targets[s ^ 1],
                send_sem=hs_sem.at[slot, s], recv_sem=hr_sem.at[slot, s ^ 1],
                device_id=peers[s], device_id_type=mesh_id)

        def start():
            for s in range(4):
                @pl.when(has[s])
                def _():
                    copy(s).start()

        def wait_recv():
            for s in range(4):
                @pl.when(has[s])
                def _():
                    pltpu.make_async_remote_copy(
                        src_ref=sources[s], dst_ref=targets[s],
                        send_sem=hs_sem.at[slot, s], recv_sem=hr_sem.at[slot, s],
                        device_id=peers[s], device_id_type=mesh_id).wait_recv()

        def wait_send():
            for s in range(4):
                @pl.when(has[s])
                def _():
                    copy(s).wait_send()

        return start, wait_recv, wait_send

    row0 = iota((cy, nz), 0) == 0
    rowl = iota((cy, nz), 0) == cy - 1
    lan0 = iota((cy, nz), 1) == 0
    lanl = iota((cy, nz), 1) == nz - 1

    for s in range(2):
        @pl.when(jnp.logical_not(has[s]))
        def _():
            hxz[s] = jnp.zeros(hxz.shape[1:], F32)
            hxc[s] = jnp.zeros(hxc.shape[1:], F32)
            hxx[s] = jnp.zeros(hxx.shape[1:], F32)
            for i in range(2):
                hxv[i, s] = jnp.zeros(hxv.shape[2:], F32)

        @pl.when(jnp.logical_not(has[2 + s]))
        def _():
            hyz[s] = jnp.zeros(hyz.shape[1:], F32)
            hyc[s] = jnp.zeros(hyc.shape[1:], F32)
            hyx[s] = jnp.zeros(hyx.shape[1:], F32)
            for i in range(2):
                hyv[i, s] = jnp.zeros(hyv.shape[2:], F32)

    loads[0].wait()

    def pack(x, carry):
        pyc[0, pl.ds(x, 1), :] = cf[x, 0:1, :]
        pyc[1, pl.ds(x, 1), :] = cf[x, cy - 1 : cy, :]
        return carry

    lax.fori_loop(0, cx, pack, 0)

    fx[0] = jnp.zeros((cy, nz), F32)
    fx[cx] = jnp.zeros((cy, nz), F32)

    def faces_x(x, carry):
        fx[x] = face_of(cf[x - 1], cf[x])
        return carry

    lax.fori_loop(1, cx, faces_x, 0)

    def faces(x, carry):
        c = cf[x]
        yl = jnp.where(row0, 0.0, face_of(pltpu.roll(c, 1, 0), c))
        yh = jnp.where(rowl, 0.0, face_of(c, pltpu.roll(c, cy - 1, 0)))
        zl = jnp.where(lan0, c, face_of(pltpu.roll(c, 1, 1), c))
        zh = jnp.where(lanl, c, face_of(c, pltpu.roll(c, nz - 1, 1)))
        dg[x] = fx[x] + fx[x + 1] + yl + yh + zl + zh
        fyl[x] = yl
        fyh[x] = yh
        fzl[x] = jnp.where(lan0, 0.0, zl)
        fzh[x] = jnp.where(lanl, 0.0, zh)
        return carry

    lax.fori_loop(0, cx, faces, 0)

    pl.semaphore_wait(barrier, na + nb - 2)
    coef_halo = halo(0, [cf.at[0], cf.at[cx - 1], pyc.at[0], pyc.at[1]], [hxc.at[0], hxc.at[1], hyc.at[0], hyc.at[1]])
    coef_halo[0]()
    loads[3].wait()

    def packz(x, carry):
        for k in range(nk):
            pyz[0, k, pl.ds(x, 1), :] = zf[k, x, 0:1, :]
            pyz[1, k, pl.ds(x, 1), :] = zf[k, x, cy - 1 : cy, :]
        return carry

    lax.fori_loop(0, cx, packz, 0)
    z_halo = halo(2, [zf.at[:, 0], zf.at[:, cx - 1], pyz.at[0], pyz.at[1]], [hxz.at[0], hxz.at[1], hyz.at[0], hyz.at[1]])
    z_halo[0]()
    loads[1].wait()

    def packx(x, carry):
        pyx[0, pl.ds(x, 1), :] = xf[x, 0:1, :]
        pyx[1, pl.ds(x, 1), :] = xf[x, cy - 1 : cy, :]
        return carry

    lax.fori_loop(0, cx, packx, 0)
    x_halo = halo(1, [xf.at[0], xf.at[cx - 1], pyx.at[0], pyx.at[1]], [hxx.at[0], hxx.at[1], hyx.at[0], hyx.at[1]])
    x_halo[0]()

    def inner_apply(v, before, after, x):
        near = fx[x] * before + fx[x + 1] * after
        near = near + fyl[x] * pltpu.roll(v, 1, 0) + fyh[x] * pltpu.roll(v, cy - 1, 0)
        near = near + fzl[x] * pltpu.roll(v, 1, 1) + fzh[x] * pltpu.roll(v, nz - 1, 1)
        return dg[x] * v - near

    def below(x):
        return jnp.maximum(x - 1, 0)

    def above(x):
        return jnp.minimum(x + 1, cx - 1)

    def make_az(x, carry):
        for k in range(nk):
            az[k, x] = inner_apply(zf[k, x], zf[k, below(x)], zf[k, above(x)], x)
        return carry

    lax.fori_loop(0, cx, make_az, 0)

    coef_halo[1]()
    for s in range(2):
        wx[s] = face_of(cf[s * (cx - 1)], hxc[s])
        wy[s] = face_of(pyc[s], hyc[s])
        dg[s * (cx - 1)] = dg[s * (cx - 1)] + wx[s]
        for k in range(nk):
            az[k, s * (cx - 1)] = az[k, s * (cx - 1)] + wx[s] * zf[k, s * (cx - 1)]
    top8 = iota((8, nz), 0) == 0
    bot8 = iota((8, nz), 0) == 7

    def fix(x, carry):
        lo = jnp.where(top8, wy[0, pl.ds(x, 1), :], 0.0)
        hi = jnp.where(bot8, wy[1, pl.ds(x, 1), :], 0.0)
        dg[x, 0:8, :] = dg[x, 0:8, :] + lo
        dg[x, cy - 8 : cy, :] = dg[x, cy - 8 : cy, :] + hi
        for k in range(nk):
            az[k, x, 0:8, :] = az[k, x, 0:8, :] + lo * zf[k, x, 0:8, :]
            az[k, x, cy - 8 : cy, :] = az[k, x, cy - 8 : cy, :] + hi * zf[k, x, cy - 8 : cy, :]
        rd[x] = 1.0 / dg[x]
        return carry

    lax.fori_loop(0, cx, fix, 0)

    pairs = [(k, l) for k in range(nk) for l in range(k, nk)]

    def gram(x, accs):
        accs = list(accs)
        for i in range(cy // 8):
            for j in range(nz // 128):
                zs = [zf[k, x, 8 * i : 8 * i + 8, 128 * j : 128 * j + 128] for k in range(nk)]
                for l in range(nk):
                    w = az[l, x, 8 * i : 8 * i + 8, 128 * j : 128 * j + 128]
                    for k in range(l + 1):
                        n = pairs.index((k, l))
                        accs[n] = accs[n] + zs[k] * w
        return tuple(accs)

    diag = lax.fori_loop(0, cx, gram, tuple(jnp.zeros((8, 128), F32) for _ in pairs))

    z_halo[1]()
    for s in range(2):
        for k in range(nk):
            nx[s, k] = -(wx[s] * hxz[s, k])
            ny[s, k] = -(wy[s] * hyz[s, k])

    lane = iota((8, 128), 1)
    sub = iota((8, 128), 0)
    base = lax.rem(a, 4) * 32
    tile = jnp.zeros((8, 128), F32)
    for l in range(nk):
        v = total_rows([diag[pairs.index((min(k, l), max(k, l)))] for k in range(nk)])
        tile = tile + jnp.where(lane == base + 8 + l, v, 0.0)
    tb[0] = tile

    def off_blocks(l, carry):
        out = tb[0]
        for s in range(2):
            v = total_rows([fold(zf[k, s * (cx - 1)] * nx[s, l]) for k in range(nk)])
            out = out + jnp.where(lane == base + 16 * s + l, v, 0.0)
        v = total_rows([fold(pyz[0, k] * ny[0, l]) for k in range(nk)])
        tb[0] = out + jnp.where(lane == base + 24 + l, v, 0.0)
        return carry

    lax.fori_loop(0, nk, off_blocks, 0)

    es[a] = tb[0]

    def spread(buf_at, own, count, peer_of, ssem, rsem):
        for o in range(1, count):
            pltpu.make_async_remote_copy(
                src_ref=own, dst_ref=own, send_sem=ssem, recv_sem=rsem,
                device_id=peer_of(o), device_id_type=mesh_id).start()

    def wait_bytes(ref, sem):
        pltpu.make_async_copy(ref, ref, sem).wait()

    gx_peer = lambda o: (lax.rem(a + o, na), b)
    gy_peer = lambda o: (a, lax.rem(b + o, nb))

    def message_rows(groups):
        out = jnp.zeros((1, 128), F32)
        for q, accs in groups:
            v = total_rows(accs)
            out = out + jnp.sum(jnp.where(lane == 8 * q + sub, v, 0.0), axis=0, keepdims=True)
        return out

    half_y, half_z = na // 2, 4 if nb % 4 == 0 else 1
    side_x = nb // half_z
    hops = lambda d, n: min(d, n - d)
    offsets = sorted(
        [(i, j, k, 1 - c) for i in range(half_y) for j in range(half_z) for k in range(side_x) for c in range(2)],
        key=lambda o: -(hops(o[0], half_y) + hops(o[1], half_z) + hops(o[2], side_x)))
    me = b * na + a

    def send(phase, groups):
        gb[phase, pl.ds(me, 1), :] = message_rows(groups)
        row = gb.at[phase, pl.ds(me, 1)]
        for dy, dz, dx, dc in offsets:
            if (dy, dz, dx, dc) == (0, 0, 0, 0):
                continue
            to_a = 2 * lax.rem(a // 2 + dy, half_y) + (1 - lax.rem(a, 2) if dc else lax.rem(a, 2))
            to_b = side_x * lax.rem(b // side_x + dz, half_z) + lax.rem(lax.rem(b, side_x) + dx, side_x)
            pltpu.make_async_remote_copy(
                src_ref=row, dst_ref=row, send_sem=gs_sem.at[phase], recv_sem=gr_sem.at[phase],
                device_id=(to_a, to_b), device_id_type=mesh_id).start()

    def receive(phase):
        wait_bytes(gb.at[phase, pl.ds(0, na * nb - 1)], gr_sem.at[phase])
        return jnp.transpose(gb[phase])

    spread(None, es.at[a], na, gx_peer, es_sem.at[0], er_sem.at[0])
    x_halo[1]()
    loads[2].wait()

    def minus_faces(v, x, hx, hy):
        v = v + jnp.where(row0, wy[0, pl.ds(x, 1), :] * hy[0, pl.ds(x, 1), :], 0.0)
        return v + jnp.where(rowl, wy[1, pl.ds(x, 1), :] * hy[1, pl.ds(x, 1), :], 0.0)

    def first(x, accs):
        ax = inner_apply(xf[x], xf[below(x)], xf[above(x)], x)
        r = minus_faces(rf[x] - ax, x, hxx, hyx)
        r = r + jnp.where(x == 0, wx[0] * hxx[0], 0.0) + jnp.where(x == cx - 1, wx[1] * hxx[1], 0.0)
        rf[x] = r
        return tuple(accs[k] + fold(zf[k, x] * r) for k in range(nk))

    rest = lax.fori_loop(0, cx, first, tuple(jnp.zeros((8, 128), F32) for _ in range(nk)))

    wait_bytes(es.at[pl.ds(0, na - 1)], er_sem.at[0])
    et[b, 0:8, :] = es[0] + es[1] + es[2] + es[3]
    et[b, 8:16, :] = es[4] + es[5] + es[6] + es[7]
    spread(None, et.at[b], nb, gy_peer, es_sem.at[1], er_sem.at[1])
    wait_bytes(et.at[pl.ds(0, nb - 1)], er_sem.at[1])
    send(0, [(0, list(rest))])

    def expand(j, carry):
        for i in range(na):
            packed = et[j, 8 * (i // 4) : 8 * (i // 4) + 8, :]
            at = 32 * (i % 4)
            near = pltpu.roll(packed, (8 * i - 8 - at) % 128, 1)
            side = pltpu.roll(packed, (40 + 8 * i - at) % 128, 1)
            out = jnp.where((lane >= 64 + 8 * i) & (lane < 72 + 8 * i), side, 0.0)
            out = jnp.where((lane >= 8 * i - 8) & (lane < 8 * i + 16) & (lane < 64), near, out)
            ge[j, 8 * i : 8 * i + 8, :] = out
        return carry

    lax.fori_loop(0, nb, expand, 0)

    factor([ge[j] for j in range(nb)], d_ref, lu_ref, w_ref, y_ref, m_ref, x_ref, xt_ref, a, b, na, nb)

    def coarse_of(got):
        g = got[0:8]
        g = g + pltpu.roll(got[8:16], na * nb - 1, 1) + pltpu.roll(got[16:24], 1, 1)
        g = g + pltpu.roll(got[24:32], na * nb - na, 1) + pltpu.roll(got[32:40], na, 1)
        c = xt_ref[0] * g[0:1, :]
        for k in range(1, nk):
            c = c + xt_ref[k] * g[k : k + 1, :]
        return jnp.broadcast_to(jnp.sum(c, axis=1, keepdims=True), (40, nz))

    def keep(c):
        cc[...] = c
        for s in range(2):
            u = nx[s, 0] * cc[8 * s + 8 : 8 * s + 9, :]
            v = ny[s, 0] * cc[8 * s + 24 : 8 * s + 25, :]
            for k in range(1, nk):
                u = u + nx[s, k] * cc[8 * s + 8 + k : 8 * s + 9 + k, :]
                v = v + ny[s, k] * cc[8 * s + 24 + k : 8 * s + 25 + k, :]
            fcx[s] = u
            fcy[s] = v

    def span(vectors, x):
        out = vectors[0, x] * cc[0:1, :]
        for k in range(1, nk):
            out = out + vectors[k, x] * cc[k : k + 1, :]
        return out

    def image(x):
        out = span(az, x)
        out = out + jnp.where(row0, fcy[0, pl.ds(x, 1), :], 0.0) + jnp.where(rowl, fcy[1, pl.ds(x, 1), :], 0.0)
        return out + jnp.where(x == 0, fcx[0], 0.0) + jnp.where(x == cx - 1, fcx[1], 0.0)

    def scalar(got, row):
        return jnp.sum(got[row : row + 1, :], axis=1, keepdims=True)

    zero = jnp.zeros((8, 128), F32)

    def restrict_slab(x, v, field, slot, accs):
        field[x] = v
        pyv[slot, 0, pl.ds(x, 1), :] = v[0:1, :]
        pyv[slot, 1, pl.ds(x, 1), :] = v[cy - 1 : cy, :]
        return tuple(accs[k] + fold(az[k, x] * v) for k in range(nk))

    def finish_groups(field, slot, accs):
        groups = [(0, list(accs[:nk])), (5, list(accs[nk:]))]
        for s in range(2):
            groups.append((1 + s, [fold(nx[s, k] * field[s * (cx - 1)]) for k in range(nk)]))
            groups.append((3 + s, [fold(ny[s, k] * pyv[slot, s]) for k in range(nk)]))
        return groups

    fields = [vf, uf]
    v_halos = [
        halo(3 + i, [fields[i].at[0], fields[i].at[cx - 1], pyv.at[i, 0], pyv.at[i, 1]],
             [hxv.at[i, 0], hxv.at[i, 1], hyv.at[i, 0], hyv.at[i, 1]])
        for i in range(2)
    ]

    def apply_all(i, out):
        field, hx, hy = fields[i], hxv.at[i], hyv.at[i]

        def slab(x, carry):
            w = inner_apply(field[x], field[below(x)], field[above(x)], x)
            w = w - jnp.where(row0, wy[0, pl.ds(x, 1), :] * hy[0, pl.ds(x, 1), :], 0.0)
            w = w - jnp.where(rowl, wy[1, pl.ds(x, 1), :] * hy[1, pl.ds(x, 1), :], 0.0)
            out[x] = w - jnp.where(x == 0, wx[0] * hx[0], 0.0) - jnp.where(x == cx - 1, wx[1] * hx[1], 0.0)
            return carry

        lax.fori_loop(0, cx, slab, 0)

    keep(coarse_of(receive(0)))
    x_halo[2]()

    def deflate(x, accs):
        xf[x] = xf[x] + span(zf, x)
        r = rf[x] - image(x)
        rf[x] = r
        v = r * rd[x]
        return restrict_slab(x, v, vf, 0, accs) + (accs[nk] + fold(r * v),)

    accs = lax.fori_loop(0, cx, deflate, (zero,) * (nk + 1))
    v_halos[0][0]()
    send(1, finish_groups(vf, 0, accs))
    v_halos[0][1]()
    apply_all(0, wf)
    got = receive(1)
    keep(coarse_of(got))
    inner = scalar(got, 40)

    def sums(x, p, q, v, slot, accs):
        u = q * rd[x]
        more = (accs[nk] + fold(p * q), accs[nk + 1] + fold(q * v), accs[nk + 2] + fold(q * u))
        return restrict_slab(x, u, uf, slot, accs) + more

    def direction(x, accs):
        v = vf[x]
        p = v - span(zf, x)
        q = wf[x] - image(x)
        pf[x] = p
        qf[x] = q
        return sums(x, p, q, v, 1, accs)

    accs = lax.fori_loop(0, cx, direction, (zero,) * (nk + 3))
    v_halos[1][0]()
    send(2, finish_groups(uf, 1, accs))
    v_halos[0][2]()
    v_halos[1][1]()
    apply_all(1, tf)

    def advance(got, inner):
        step = inner / scalar(got, 40)
        new = inner - 2.0 * step * scalar(got, 41) + step * step * scalar(got, 42)
        keep(cc[...] - step * coarse_of(got))
        return step, new, new / inner

    got = receive(2)
    step, inner, beta = advance(got, inner)
    v_halos[1][2]()

    def next_direction(x, accs):
        v = vf[x] - step * uf[x]
        vf[x] = v
        p = v + beta * pf[x] - span(zf, x)
        q = wf[x] - step * tf[x] + beta * qf[x] - image(x)
        ph[x] = p
        qh[x] = q
        return sums(x, p, q, v, 2, accs)

    accs = lax.fori_loop(0, cx, next_direction, (zero,) * (nk + 3))
    send(3, finish_groups(uf, 2, accs))

    def move(x, carry):
        xf[x] = xf[x] + step * pf[x]
        rf[x] = rf[x] - step * qf[x]
        return carry

    lax.fori_loop(0, cx, move, 0)
    got = receive(3)
    last_step, inner, beta = advance(got, inner)

    def last_move(x, carry):
        xf[x] = xf[x] + last_step * ph[x]
        rf[x] = rf[x] - last_step * qh[x]
        return carry

    def last(x, carry):
        pf[x] = vf[x] - last_step * uf[x] + beta * ph[x] - span(zf, x)
        return carry

    lax.fori_loop(0, cx, last_move, 0)
    stores = [
        pltpu.make_async_copy(xf, sol_hbm, st_sem.at[0]),
        pltpu.make_async_copy(rf, res_hbm, st_sem.at[1]),
        pltpu.make_async_copy(pf, dir_hbm, st_sem.at[2]),
    ]
    stores[0].start()
    stores[1].start()
    lax.fori_loop(0, cx, last, 0)
    stores[2].start()
    for h in (coef_halo, z_halo):
        h[2]()
    wait_bytes(es.at[pl.ds(0, na - 1)], es_sem.at[0])
    wait_bytes(et.at[pl.ds(0, nb - 1)], es_sem.at[1])
    for phase in range(4):
        wait_bytes(gb.at[phase, pl.ds(0, na * nb - 1)], gs_sem.at[phase])
    for store in stores:
        store.wait()


def solution(mesh):
    na, nb = mesh.shape["gx"], mesh.shape["gy"]

    def per_device(right_side, start_field, coef, deflation):
        nk, cx, cy, nz = deflation.shape
        vm = lambda *shape: pltpu.VMEM(shape, F32)
        dma = lambda *shape: pltpu.SemaphoreType.DMA(shape)
        field = (cx, cy, nz)
        scratch = [
            vm(nk, *field), vm(nk, *field)] + [vm(*field) for _ in range(11)] + [
            vm(cx + 1, cy, nz), vm(*field), vm(*field), vm(*field), vm(*field), vm(*field), vm(*field),
            vm(2, cy, nz), vm(2, cx, nz),
            vm(2, nk, cy, nz), vm(2, nk, cx, nz), vm(2, cy, nz), vm(2, cx, nz), vm(2, cy, nz), vm(2, cx, nz),
            vm(2, 2, cy, nz), vm(2, 2, cx, nz),
            vm(2, nk, cx, nz), vm(2, cx, nz), vm(2, cx, nz), vm(3, 2, cx, nz),
            vm(2, nk, cy, nz), vm(2, nk, cx, nz), vm(2, cy, nz), vm(2, cx, nz),
            vm(40, nz), vm(nb, 64, 128), vm(na, 8, 128), vm(nb, 16, 128), vm(4, na * nb, 128), vm(1, 8, 128),
            vm(nb, 64, 128), vm(nb, 64, 128), vm(nb, 64, 256), vm(nb, 64, 128), vm((nb // 2 + 1) // 2, 64, 128),
            vm(nb * 64, 128), vm(8, 40, 128),
            dma(4), dma(3), dma(5, 4), dma(5, 4), dma(2), dma(2), dma(4), dma(4),
        ]
        out = jax.ShapeDtypeStruct(field, F32)
        return pl.pallas_call(
            functools.partial(body, na, nb),
            out_shape=(out, out, out),
            in_specs=[pl.BlockSpec(memory_space=pl.ANY)] * 4,
            out_specs=(pl.BlockSpec(memory_space=pl.ANY),) * 3,
            scratch_shapes=scratch,
            compiler_params=pltpu.CompilerParams(
                collective_id=0, has_side_effects=True, vmem_limit_bytes=60000 * 1024),
            name="deflated_cg",
        )(right_side, start_field, coef, deflation)

    spec = P("gx", "gy", None)
    return jax.shard_map(
        per_device, mesh=mesh, in_specs=(spec, spec, spec, P(None, "gx", "gy", None)),
        out_specs=(spec, spec, spec), check_vma=False)
```

```python
import functools
import jax, jax.numpy as jnp
from jax import lax
from jax.experimental import pallas as pl
from jax.experimental.pallas import tpu as pltpu
from jax.sharding import PartitionSpec as P

F32 = jnp.float32
BF = jnp.bfloat16


def iota(shape, dim):
    return lax.broadcasted_iota(jnp.int32, shape, dim)


def split3(v):
    high = v.astype(BF)
    rest = v - high.astype(F32)
    mid = rest.astype(BF)
    low = (rest - mid.astype(F32)).astype(BF)
    return high, mid, low


def mm(left, right):
    lh, lm, ll = left
    rh, rm, rl = right
    d = lambda p, q: jnp.dot(p, q, preferred_element_type=F32)
    return d(lh, rh) + (d(lh, rm) + d(lm, rh)) + (d(lm, rm) + d(lh, rl) + d(ll, rh))


def invert_pairs(m_ref, count):
    lane = iota((8, 128), 1)
    sub = iota((8, 128), 0)
    half = lane // 64 * 64
    left = lane < 64

    def panel(p, carry):
        start = pl.multiple_of(p * 8, 8)
        in_panel = (lane - half) // 8 == p
        done = (lane - half) // 8 < p
        ident = (lane - half - p * 8) == sub
        index = [half + p * 8 + j for j in range(8)]
        rows, piv, cols = [], [], []
        for s in range(count):
            r = m_ref[s, pl.ds(start, 8), :]
            piv.append([jnp.take_along_axis(r, index[j], axis=1) for j in range(8)])
            rows.append(jnp.where(in_panel, jnp.where(ident, 1.0, 0.0), r))
            if count > 1:
                flip = jnp.where(done, -r, r)
                c = jnp.concatenate([flip[:, :64], pltpu.roll(flip, 64, 1)[:, :64]], axis=0)
                ch, cm, cl = split3(c)
                cols.append(jnp.transpose(jnp.concatenate([ch, ch, cm, cm, ch, cl], axis=0).astype(F32)).astype(BF))
        for t in range(8):
            own = sub == t
            for s in range(count):
                mult = piv[s][t]
                scale = 1.0 / mult[t : t + 1, :]
                row = rows[s][t : t + 1, :] * scale
                rows[s] = jnp.where(own, row, rows[s] - mult * row)
                for j in range(t + 1, 8):
                    prow = piv[s][j][t : t + 1, :] * scale
                    piv[s][j] = jnp.where(own, prow, piv[s][j] - mult * prow)
        if count > 1:
            wide = iota((64, 128), 1)
            wide_panel = (wide - wide // 64 * 64) // 8 == p
            for s in range(count):
                r = jnp.concatenate([jnp.where(left, rows[s], 0.0), jnp.where(left, 0.0, rows[s])], axis=0)
                rh, rm, rl = split3(r)
                right = jnp.concatenate([rh, rm, rh, rm, rl, rh], axis=0)
                m_ref[s] = jnp.where(wide_panel, 0.0, m_ref[s]) - jnp.dot(cols[s], right, preferred_element_type=F32)
        else:
            for s in range(count):
                for v in range(8):
                    block = m_ref[s, 8 * v : 8 * v + 8, :]
                    terms = [jnp.take_along_axis(block, index[j], axis=1) * rows[s][j : j + 1, :] for j in range(8)]
                    while len(terms) > 1:
                        terms = [terms[i] + terms[i + 1] for i in range(0, len(terms), 2)]
                    m_ref[s, 8 * v : 8 * v + 8, :] = jnp.where(in_panel, 0.0, block) - terms[0]
        for s in range(count):
            m_ref[s, pl.ds(start, 8), :] = rows[s]
        return carry

    lax.fori_loop(0, 8, panel, 0)


def factor(tiles, d_ref, lu_ref, w_ref, y_ref, m_ref, x_ref, xt_ref, a, b, na, nb):
    lane = iota((64, 128), 1)
    rowi = iota((64, 128), 0)
    low = lane < 64
    group = lane // 8
    within = lane % 8
    own = (b * na + a) * 8
    target = jnp.where(group == 0, own, -4096)
    target = jnp.where((group == 1) & (a > 0), own - 8, target)
    target = jnp.where((group == 2) & (a < na - 1), own + 8, target)
    target = jnp.where((group == 3) & (b > 0), own - 64, target)
    target = jnp.where((group == 4) & (b < nb - 1), own + 64, target)
    target = target + within
    for j in range(nb):
        tile = tiles[j]
        d_ref[j] = tile
        y_ref[j] = jnp.where(rowi + 64 * j == target, 1.0, 0.0)
    for j in range(nb):
        left = pltpu.roll(tiles[j], 64, 1)
        if j < nb - 1:
            up = jnp.transpose(tiles[j + 1])[64:128, :]
            up = jnp.concatenate([jnp.zeros((64, 64), F32), up], axis=1)
        else:
            up = jnp.zeros((64, 128), F32)
        left = jnp.where(low, left, 0.0) if j > 0 else jnp.zeros((64, 128), F32)
        lu_ref[j] = jnp.where(low, left, up)

    def invert(lines):
        slots = (len(lines) + 1) // 2
        for s in range(slots):
            first = d_ref[lines[2 * s]]
            second = d_ref[lines[min(2 * s + 1, len(lines) - 1)]]
            m_ref[s] = jnp.where(low, first, pltpu.roll(second, 64, 1))
        invert_pairs(m_ref, slots)
        out = []
        for i in range(len(lines)):
            v = m_ref[i // 2]
            out.append(v[:, :64] if i % 2 == 0 else pltpu.roll(v, 64, 1)[:, :64])
        return out

    step = 1
    levels = []
    while step < nb:
        lines = list(range(step, nb, 2 * step))
        inverses = invert(lines)
        for j, inv in zip(lines, inverses):
            right = jnp.concatenate([lu_ref[j], y_ref[j]], axis=1)
            lut = jnp.transpose(lu_ref[j])
            w = mm(split3(inv), split3(right))
            w_ref[j] = w
            p = mm(split3(lut), split3(w))
            i, k = j - step, j + step
            d_ref[i] = d_ref[i] - p[:64, :128]
            y_ref[i] = y_ref[i] - p[:64, 128:]
            lu_ref[i] = jnp.where(low, lu_ref[i], -p[:64, :128])
            if k < nb:
                d_ref[k] = d_ref[k] - pltpu.roll(p[64:, :128], 64, 1)
                y_ref[k] = y_ref[k] - p[64:, 128:]
                lu_ref[k] = jnp.where(low, -p[64:, :128], lu_ref[k])
        levels.append((step, lines))
        step *= 2
    inv = invert([0])[0]
    x_ref[0:64] = mm(split3(inv), split3(y_ref[0]))
    for step, lines in reversed(levels):
        for j in lines:
            i, k = j - step, j + step
            below = x_ref[64 * i : 64 * i + 64]
            above = x_ref[64 * k : 64 * k + 64] if k < nb else jnp.zeros((64, 128), F32)
            both = jnp.concatenate([below, above], axis=0)
            w = w_ref[j]
            x_ref[64 * j : 64 * j + 64] = w[:, 128:] - mm(split3(w[:, :128]), split3(both))
    for k in range(8):
        xt_ref[k] = jnp.transpose(x_ref[pl.ds(k, na * nb, stride=8), :])[:40, :]


def total_rows(accs):
    sub = iota((8, 128), 0)
    out = jnp.zeros((8, 128), F32)
    for i, acc in enumerate(accs):
        out = jnp.where(sub == i, jnp.sum(acc, axis=0, keepdims=True), out)
    return jnp.broadcast_to(jnp.sum(out, axis=1, keepdims=True), (8, 128))


def fold(value):
    rows, cols = value.shape
    pieces = [value[8 * i : 8 * i + 8, 128 * j : 128 * j + 128] for i in range(rows // 8) for j in range(cols // 128)]
    while len(pieces) > 1:
        pieces = [pieces[i] + pieces[i + 1] if i + 1 < len(pieces) else pieces[i] for i in range(0, len(pieces), 2)]
    return pieces[0]


def face_of(lower, upper):
    summed = lower + upper
    return jnp.where((lower > 0.0) & (upper > 0.0), 2.0 * lower * upper / summed, summed)


def body(na, nb, rhs_hbm, x0_hbm, c_hbm, z_hbm, sol_hbm, res_hbm, dir_hbm, *scratch):
    (zf, az, cf, xf, rf, vf, wf, uf, tf, pf, qf, ph, qh, fx, fyl, fyh, fzl, fzh, dg, rd,
     wx, wy, hxz, hyz, hxc, hyc, hxx, hyx, hxv, hyv, pyz, pyc, pyx, pyv, nx, ny, fcx, fcy,
     cc, ge, et, gb, tb,
     d_ref, lu_ref, w_ref, y_ref, m_ref, x_ref, xt_ref,
     ld_sem, st_sem, hs_sem, hr_sem, es_sem, er_sem, gs_sem, gr_sem, all_sem) = scratch
    cx, cy, nz = cf.shape
    nk = zf.shape[0]
    a = lax.axis_index("gx")
    b = lax.axis_index("gy")
    mesh_id = pl.DeviceIdType.MESH
    loads = [
        pltpu.make_async_copy(c_hbm, cf, ld_sem.at[0]),
        pltpu.make_async_copy(x0_hbm, xf, ld_sem.at[1]),
        pltpu.make_async_copy(rhs_hbm, rf, ld_sem.at[2]),
        pltpu.make_async_copy(z_hbm, zf, ld_sem.at[3]),
    ]
    for load in loads:
        load.start()
    barrier = pltpu.get_barrier_semaphore()
    for o in range(1, na):
        pl.semaphore_signal(barrier, inc=1, device_id=(lax.rem(a + o, na), b), device_id_type=mesh_id)
    for o in range(1, nb):
        pl.semaphore_signal(barrier, inc=1, device_id=(a, lax.rem(b + o, nb)), device_id_type=mesh_id)

    has = [a > 0, a < na - 1, b > 0, b < nb - 1]
    peers = [(a - 1, b), (a + 1, b), (a, b - 1), (a, b + 1)]

    def halo(slot, sources, targets):
        def copy(s):
            return pltpu.make_async_remote_copy(
                src_ref=sources[s], dst_ref=targets[s ^ 1],
                send_sem=hs_sem.at[slot, s], recv_sem=hr_sem.at[slot, s ^ 1],
                device_id=peers[s], device_id_type=mesh_id)

        def start():
            for s in range(4):
                @pl.when(has[s])
                def _():
                    copy(s).start()

        def wait_recv():
            for s in range(4):
                @pl.when(has[s])
                def _():
                    pltpu.make_async_remote_copy(
                        src_ref=sources[s], dst_ref=targets[s],
                        send_sem=hs_sem.at[slot, s], recv_sem=hr_sem.at[slot, s],
                        device_id=peers[s], device_id_type=mesh_id).wait_recv()

        def wait_send():
            for s in range(4):
                @pl.when(has[s])
                def _():
                    copy(s).wait_send()

        return start, wait_recv, wait_send

    row0 = iota((cy, nz), 0) == 0
    rowl = iota((cy, nz), 0) == cy - 1
    lan0 = iota((cy, nz), 1) == 0
    lanl = iota((cy, nz), 1) == nz - 1

    for s in range(2):
        @pl.when(jnp.logical_not(has[s]))
        def _():
            hxz[s] = jnp.zeros(hxz.shape[1:], F32)
            hxc[s] = jnp.zeros(hxc.shape[1:], F32)
            hxx[s] = jnp.zeros(hxx.shape[1:], F32)
            for i in range(2):
                hxv[i, s] = jnp.zeros(hxv.shape[2:], F32)

        @pl.when(jnp.logical_not(has[2 + s]))
        def _():
            hyz[s] = jnp.zeros(hyz.shape[1:], F32)
            hyc[s] = jnp.zeros(hyc.shape[1:], F32)
            hyx[s] = jnp.zeros(hyx.shape[1:], F32)
            for i in range(2):
                hyv[i, s] = jnp.zeros(hyv.shape[2:], F32)

    loads[0].wait()

    def pack(x, carry):
        pyc[0, pl.ds(x, 1), :] = cf[x, 0:1, :]
        pyc[1, pl.ds(x, 1), :] = cf[x, cy - 1 : cy, :]
        return carry

    lax.fori_loop(0, cx, pack, 0)

    fx[0] = jnp.zeros((cy, nz), F32)
    fx[cx] = jnp.zeros((cy, nz), F32)

    def faces_x(x, carry):
        fx[x] = face_of(cf[x - 1], cf[x])
        return carry

    lax.fori_loop(1, cx, faces_x, 0)

    def faces(x, carry):
        c = cf[x]
        yl = jnp.where(row0, 0.0, face_of(pltpu.roll(c, 1, 0), c))
        yh = jnp.where(rowl, 0.0, face_of(c, pltpu.roll(c, cy - 1, 0)))
        zl = jnp.where(lan0, c, face_of(pltpu.roll(c, 1, 1), c))
        zh = jnp.where(lanl, c, face_of(c, pltpu.roll(c, nz - 1, 1)))
        dg[x] = fx[x] + fx[x + 1] + yl + yh + zl + zh
        fyl[x] = yl
        fyh[x] = yh
        fzl[x] = jnp.where(lan0, 0.0, zl)
        fzh[x] = jnp.where(lanl, 0.0, zh)
        return carry

    lax.fori_loop(0, cx, faces, 0)

    pl.semaphore_wait(barrier, na + nb - 2)
    for o in range(1, nb):
        pl.semaphore_signal(all_sem, inc=1, device_id=(a, lax.rem(b + o, nb)), device_id_type=mesh_id)
    coef_halo = halo(0, [cf.at[0], cf.at[cx - 1], pyc.at[0], pyc.at[1]], [hxc.at[0], hxc.at[1], hyc.at[0], hyc.at[1]])
    coef_halo[0]()
    loads[3].wait()

    def packz(x, carry):
        for k in range(nk):
            pyz[0, k, pl.ds(x, 1), :] = zf[k, x, 0:1, :]
            pyz[1, k, pl.ds(x, 1), :] = zf[k, x, cy - 1 : cy, :]
        return carry

    lax.fori_loop(0, cx, packz, 0)
    z_halo = halo(2, [zf.at[:, 0], zf.at[:, cx - 1], pyz.at[0], pyz.at[1]], [hxz.at[0], hxz.at[1], hyz.at[0], hyz.at[1]])
    z_halo[0]()
    loads[1].wait()

    def packx(x, carry):
        pyx[0, pl.ds(x, 1), :] = xf[x, 0:1, :]
        pyx[1, pl.ds(x, 1), :] = xf[x, cy - 1 : cy, :]
        return carry

    lax.fori_loop(0, cx, packx, 0)
    x_halo = halo(1, [xf.at[0], xf.at[cx - 1], pyx.at[0], pyx.at[1]], [hxx.at[0], hxx.at[1], hyx.at[0], hyx.at[1]])
    x_halo[0]()

    def inner_apply(v, before, after, x):
        near = fx[x] * before + fx[x + 1] * after
        near = near + fyl[x] * pltpu.roll(v, 1, 0) + fyh[x] * pltpu.roll(v, cy - 1, 0)
        near = near + fzl[x] * pltpu.roll(v, 1, 1) + fzh[x] * pltpu.roll(v, nz - 1, 1)
        return dg[x] * v - near

    def below(x):
        return jnp.maximum(x - 1, 0)

    def above(x):
        return jnp.minimum(x + 1, cx - 1)

    def make_az(x, carry):
        for k in range(nk):
            az[k, x] = inner_apply(zf[k, x], zf[k, below(x)], zf[k, above(x)], x)
        return carry

    lax.fori_loop(0, cx, make_az, 0)

    coef_halo[1]()
    for s in range(2):
        wx[s] = face_of(cf[s * (cx - 1)], hxc[s])
        wy[s] = face_of(pyc[s], hyc[s])
        dg[s * (cx - 1)] = dg[s * (cx - 1)] + wx[s]
        for k in range(nk):
            az[k, s * (cx - 1)] = az[k, s * (cx - 1)] + wx[s] * zf[k, s * (cx - 1)]
    top8 = iota((8, nz), 0) == 0
    bot8 = iota((8, nz), 0) == 7

    def fix(x, carry):
        lo = jnp.where(top8, wy[0, pl.ds(x, 1), :], 0.0)
        hi = jnp.where(bot8, wy[1, pl.ds(x, 1), :], 0.0)
        dg[x, 0:8, :] = dg[x, 0:8, :] + lo
        dg[x, cy - 8 : cy, :] = dg[x, cy - 8 : cy, :] + hi
        for k in range(nk):
            az[k, x, 0:8, :] = az[k, x, 0:8, :] + lo * zf[k, x, 0:8, :]
            az[k, x, cy - 8 : cy, :] = az[k, x, cy - 8 : cy, :] + hi * zf[k, x, cy - 8 : cy, :]
        rd[x] = 1.0 / dg[x]
        return carry

    lax.fori_loop(0, cx, fix, 0)

    pairs = [(k, l) for k in range(nk) for l in range(k, nk)]

    def gram(x, accs):
        accs = list(accs)
        for i in range(cy // 8):
            for j in range(nz // 128):
                zs = [zf[k, x, 8 * i : 8 * i + 8, 128 * j : 128 * j + 128] for k in range(nk)]
                for l in range(nk):
                    w = az[l, x, 8 * i : 8 * i + 8, 128 * j : 128 * j + 128]
                    for k in range(l + 1):
                        n = pairs.index((k, l))
                        accs[n] = accs[n] + zs[k] * w
        return tuple(accs)

    diag = lax.fori_loop(0, cx, gram, tuple(jnp.zeros((8, 128), F32) for _ in pairs))

    z_halo[1]()
    for s in range(2):
        for k in range(nk):
            nx[s, k] = -(wx[s] * hxz[s, k])
            ny[s, k] = -(wy[s] * hyz[s, k])

    lane = iota((8, 128), 1)
    sub = iota((8, 128), 0)
    tile = jnp.zeros((8, 128), F32)
    for l in range(nk):
        v = total_rows([diag[pairs.index((min(k, l), max(k, l)))] for k in range(nk)])
        tile = tile + jnp.where(lane == 8 + l, v, 0.0)
    tb[0] = tile

    def off_blocks(l, carry):
        out = tb[0]
        for s in range(2):
            v = total_rows([fold(zf[k, s * (cx - 1)] * nx[s, l]) for k in range(nk)])
            out = out + jnp.where(lane == 16 * s + l, v, 0.0)
        v = total_rows([fold(pyz[0, k] * ny[0, l]) for k in range(nk)])
        tb[0] = out + jnp.where(lane == 24 + l, v, 0.0)
        return carry

    lax.fori_loop(0, nk, off_blocks, 0)
    tile = jnp.take_along_axis(tb[0], lane % 32, axis=1)
    tile = jnp.where(lane // 32 == sub % 4, tile, 0.0)
    upper = jnp.sum(jnp.where(sub < 4, tile, 0.0), axis=0, keepdims=True)
    lower = jnp.sum(jnp.where(sub < 4, 0.0, tile), axis=0, keepdims=True)


    def wait_bytes(ref, sem):
        pltpu.make_async_copy(ref, ref, sem).wait()

    def message_rows(groups):
        out = jnp.zeros((1, 128), F32)
        for q, accs in groups:
            v = total_rows(accs)
            out = out + jnp.sum(jnp.where(lane == 8 * q + sub, v, 0.0), axis=0, keepdims=True)
        return out

    half_y, half_z = na // 2, 4 if nb % 4 == 0 else 1
    side_x = nb // half_z
    hops = lambda d, n: min(d, n - d)
    offsets = sorted(
        [(i, j, k, 1 - c) for i in range(half_y) for j in range(half_z) for k in range(side_x) for c in range(2)],
        key=lambda o: -(hops(o[0], half_y) + hops(o[1], half_z) + hops(o[2], side_x)))
    me = b * na + a

    def spread(own, ssem, rsem):
        for dy, dz, dx, dc in offsets:
            if (dy, dz, dx, dc) == (0, 0, 0, 0):
                continue
            to_a = 2 * lax.rem(a // 2 + dy, half_y) + (1 - lax.rem(a, 2) if dc else lax.rem(a, 2))
            to_b = side_x * lax.rem(b // side_x + dz, half_z) + lax.rem(lax.rem(b, side_x) + dx, side_x)
            pltpu.make_async_remote_copy(
                src_ref=own, dst_ref=own, send_sem=ssem, recv_sem=rsem,
                device_id=(to_a, to_b), device_id_type=mesh_id).start()

    def send(phase, groups):
        gb[phase, pl.ds(me, 1), :] = message_rows(groups)
        spread(gb.at[phase, pl.ds(me, 1)], gs_sem.at[phase], gr_sem.at[phase])

    def receive(phase):
        wait_bytes(gb.at[phase, pl.ds(0, na * nb - 1)], gr_sem.at[phase])
        return jnp.transpose(gb[phase])

    et[pl.ds(2 * me, 1), :] = upper
    et[pl.ds(2 * me + 1, 1), :] = lower
    pl.semaphore_wait(all_sem, nb - 1)
    spread(et.at[pl.ds(pl.multiple_of(2 * me, 2), 2)], es_sem.at[0], er_sem.at[0])
    x_halo[1]()
    loads[2].wait()

    def minus_faces(v, x, hx, hy):
        v = v + jnp.where(row0, wy[0, pl.ds(x, 1), :] * hy[0, pl.ds(x, 1), :], 0.0)
        return v + jnp.where(rowl, wy[1, pl.ds(x, 1), :] * hy[1, pl.ds(x, 1), :], 0.0)

    def first(x, accs):
        ax = inner_apply(xf[x], xf[below(x)], xf[above(x)], x)
        r = minus_faces(rf[x] - ax, x, hxx, hyx)
        r = r + jnp.where(x == 0, wx[0] * hxx[0], 0.0) + jnp.where(x == cx - 1, wx[1] * hxx[1], 0.0)
        rf[x] = r
        return tuple(accs[k] + fold(zf[k, x] * r) for k in range(nk))

    rest = lax.fori_loop(0, cx, first, tuple(jnp.zeros((8, 128), F32) for _ in range(nk)))

    wait_bytes(et.at[pl.ds(0, 2 * (na * nb - 1))], er_sem.at[0])
    send(0, [(0, list(rest))])

    def expand(j, carry):
        start = pl.multiple_of(2 * na * j, 2 * na)
        for i in range(na):
            packed = jnp.where(sub < 4, et[pl.ds(start + 2 * i, 1), :], et[pl.ds(start + 2 * i + 1, 1), :])
            side = lane >= 64
            at = jnp.where(side, lane - 64 - 8 * i, lane + 8 - 8 * i)
            good = (at >= 0) & (at < jnp.where(side, 8, 24))
            source = 32 * (sub % 4) + jnp.where(good, at, 0) + jnp.where(side, 24, 0)
            ge[j, 8 * i : 8 * i + 8, :] = jnp.where(good, jnp.take_along_axis(packed, source, axis=1), 0.0)
        return carry

    lax.fori_loop(0, nb, expand, 0)

    factor([ge[j] for j in range(nb)], d_ref, lu_ref, w_ref, y_ref, m_ref, x_ref, xt_ref, a, b, na, nb)

    def coarse_of(got):
        g = got[0:8]
        g = g + pltpu.roll(got[8:16], na * nb - 1, 1) + pltpu.roll(got[16:24], 1, 1)
        g = g + pltpu.roll(got[24:32], na * nb - na, 1) + pltpu.roll(got[32:40], na, 1)
        c = xt_ref[0] * g[0:1, :]
        for k in range(1, nk):
            c = c + xt_ref[k] * g[k : k + 1, :]
        return jnp.broadcast_to(jnp.sum(c, axis=1, keepdims=True), (40, nz))

    def keep(c):
        cc[...] = c
        for s in range(2):
            u = nx[s, 0] * cc[8 * s + 8 : 8 * s + 9, :]
            v = ny[s, 0] * cc[8 * s + 24 : 8 * s + 25, :]
            for k in range(1, nk):
                u = u + nx[s, k] * cc[8 * s + 8 + k : 8 * s + 9 + k, :]
                v = v + ny[s, k] * cc[8 * s + 24 + k : 8 * s + 25 + k, :]
            fcx[s] = u
            fcy[s] = v

    def span(vectors, x):
        out = vectors[0, x] * cc[0:1, :]
        for k in range(1, nk):
            out = out + vectors[k, x] * cc[k : k + 1, :]
        return out

    def image(x):
        out = span(az, x)
        out = out + jnp.where(row0, fcy[0, pl.ds(x, 1), :], 0.0) + jnp.where(rowl, fcy[1, pl.ds(x, 1), :], 0.0)
        return out + jnp.where(x == 0, fcx[0], 0.0) + jnp.where(x == cx - 1, fcx[1], 0.0)

    def scalar(got, row):
        return jnp.sum(got[row : row + 1, :], axis=1, keepdims=True)

    zero = jnp.zeros((8, 128), F32)

    def restrict_slab(x, v, field, slot, accs):
        field[x] = v
        pyv[slot, 0, pl.ds(x, 1), :] = v[0:1, :]
        pyv[slot, 1, pl.ds(x, 1), :] = v[cy - 1 : cy, :]
        return tuple(accs[k] + fold(az[k, x] * v) for k in range(nk))

    def finish_groups(field, slot, accs):
        groups = [(0, list(accs[:nk])), (5, list(accs[nk:]))]
        for s in range(2):
            groups.append((1 + s, [fold(nx[s, k] * field[s * (cx - 1)]) for k in range(nk)]))
            groups.append((3 + s, [fold(ny[s, k] * pyv[slot, s]) for k in range(nk)]))
        return groups

    fields = [vf, uf]
    v_halos = [
        halo(3 + i, [fields[i].at[0], fields[i].at[cx - 1], pyv.at[i, 0], pyv.at[i, 1]],
             [hxv.at[i, 0], hxv.at[i, 1], hyv.at[i, 0], hyv.at[i, 1]])
        for i in range(2)
    ]

    def apply_all(i, out):
        field, hx, hy = fields[i], hxv.at[i], hyv.at[i]

        def slab(x, carry):
            w = inner_apply(field[x], field[below(x)], field[above(x)], x)
            w = w - jnp.where(row0, wy[0, pl.ds(x, 1), :] * hy[0, pl.ds(x, 1), :], 0.0)
            w = w - jnp.where(rowl, wy[1, pl.ds(x, 1), :] * hy[1, pl.ds(x, 1), :], 0.0)
            out[x] = w - jnp.where(x == 0, wx[0] * hx[0], 0.0) - jnp.where(x == cx - 1, wx[1] * hx[1], 0.0)
            return carry

        lax.fori_loop(0, cx, slab, 0)

    keep(coarse_of(receive(0)))
    x_halo[2]()

    def deflate(x, accs):
        xf[x] = xf[x] + span(zf, x)
        r = rf[x] - image(x)
        rf[x] = r
        v = r * rd[x]
        return restrict_slab(x, v, vf, 0, accs) + (accs[nk] + fold(r * v),)

    accs = lax.fori_loop(0, cx, deflate, (zero,) * (nk + 1))
    v_halos[0][0]()
    send(1, finish_groups(vf, 0, accs))
    v_halos[0][1]()
    apply_all(0, wf)
    got = receive(1)
    keep(coarse_of(got))
    inner = scalar(got, 40)

    def sums(x, p, q, v, slot, accs):
        u = q * rd[x]
        more = (accs[nk] + fold(p * q), accs[nk + 1] + fold(q * v), accs[nk + 2] + fold(q * u))
        return restrict_slab(x, u, uf, slot, accs) + more

    def direction(x, accs):
        v = vf[x]
        p = v - span(zf, x)
        q = wf[x] - image(x)
        pf[x] = p
        qf[x] = q
        return sums(x, p, q, v, 1, accs)

    accs = lax.fori_loop(0, cx, direction, (zero,) * (nk + 3))
    v_halos[1][0]()
    send(2, finish_groups(uf, 1, accs))
    v_halos[0][2]()
    v_halos[1][1]()
    apply_all(1, tf)

    def advance(got, inner):
        step = inner / scalar(got, 40)
        new = inner - 2.0 * step * scalar(got, 41) + step * step * scalar(got, 42)
        keep(cc[...] - step * coarse_of(got))
        return step, new, new / inner

    got = receive(2)
    step, inner, beta = advance(got, inner)
    v_halos[1][2]()

    def next_direction(x, accs):
        v = vf[x] - step * uf[x]
        vf[x] = v
        p = v + beta * pf[x] - span(zf, x)
        q = wf[x] - step * tf[x] + beta * qf[x] - image(x)
        ph[x] = p
        qh[x] = q
        return sums(x, p, q, v, 2, accs)

    accs = lax.fori_loop(0, cx, next_direction, (zero,) * (nk + 3))
    send(3, finish_groups(uf, 2, accs))

    def move(x, carry):
        xf[x] = xf[x] + step * pf[x]
        rf[x] = rf[x] - step * qf[x]
        return carry

    lax.fori_loop(0, cx, move, 0)
    got = receive(3)
    last_step, inner, beta = advance(got, inner)

    def last_move(x, carry):
        xf[x] = xf[x] + last_step * ph[x]
        rf[x] = rf[x] - last_step * qh[x]
        return carry

    def last(x, carry):
        pf[x] = vf[x] - last_step * uf[x] + beta * ph[x] - span(zf, x)
        return carry

    lax.fori_loop(0, cx, last_move, 0)
    stores = [
        pltpu.make_async_copy(xf, sol_hbm, st_sem.at[0]),
        pltpu.make_async_copy(rf, res_hbm, st_sem.at[1]),
        pltpu.make_async_copy(pf, dir_hbm, st_sem.at[2]),
    ]
    stores[0].start()
    stores[1].start()
    lax.fori_loop(0, cx, last, 0)
    stores[2].start()
    for h in (coef_halo, z_halo):
        h[2]()
    wait_bytes(et.at[pl.ds(0, 2 * (na * nb - 1))], es_sem.at[0])
    for phase in range(4):
        wait_bytes(gb.at[phase, pl.ds(0, na * nb - 1)], gs_sem.at[phase])
    for store in stores:
        store.wait()


def hand_over(count, *refs):
    ins, outs, held = refs[:3], refs[3:6], refs[6:9]
    load_sem, store_sem = refs[9:]
    piece = ins[0].shape[0] // count
    every = [(i, j) for j in range(count) for i in range(3)]

    def load(i, j):
        part = pl.ds(j * piece, piece)
        return pltpu.make_async_copy(ins[i].at[part], held[i].at[part], load_sem.at[i, j])

    def store(i, j):
        part = pl.ds(j * piece, piece)
        return pltpu.make_async_copy(held[i].at[part], outs[i].at[part], store_sem.at[i, j])

    for i, j in every:
        load(i, j).start()
    for i, j in every:
        load(i, j).wait()
        store(i, j).start()
    for i, j in every:
        store(i, j).wait()


def solution(mesh):
    na, nb = mesh.shape["gx"], mesh.shape["gy"]

    def per_device(right_side, start_field, coef, deflation):
        nk, cx, cy, nz = deflation.shape
        vm = lambda *shape: pltpu.VMEM(shape, F32)
        dma = lambda *shape: pltpu.SemaphoreType.DMA(shape)
        field = (cx, cy, nz)
        scratch = [
            vm(nk, *field), vm(nk, *field)] + [vm(*field) for _ in range(11)] + [
            vm(cx + 1, cy, nz), vm(*field), vm(*field), vm(*field), vm(*field), vm(*field), vm(*field),
            vm(2, cy, nz), vm(2, cx, nz),
            vm(2, nk, cy, nz), vm(2, nk, cx, nz), vm(2, cy, nz), vm(2, cx, nz), vm(2, cy, nz), vm(2, cx, nz),
            vm(2, 2, cy, nz), vm(2, 2, cx, nz),
            vm(2, nk, cx, nz), vm(2, cx, nz), vm(2, cx, nz), vm(3, 2, cx, nz),
            vm(2, nk, cy, nz), vm(2, nk, cx, nz), vm(2, cy, nz), vm(2, cx, nz),
            vm(40, nz), vm(nb, 64, 128), vm(2 * na * nb, 128), vm(4, na * nb, 128), vm(1, 8, 128),
            vm(nb, 64, 128), vm(nb, 64, 128), vm(nb, 64, 256), vm(nb, 64, 128), vm((nb // 2 + 1) // 2, 64, 128),
            vm(nb * 64, 128), vm(8, 40, 128),
            dma(4), dma(3), dma(5, 4), dma(5, 4), dma(1), dma(1), dma(4), dma(4), pltpu.SemaphoreType.REGULAR,
        ]
        out = jax.ShapeDtypeStruct(field, F32)
        results = pl.pallas_call(
            functools.partial(body, na, nb),
            out_shape=(out, out, out),
            in_specs=[pl.BlockSpec(memory_space=pl.ANY)] * 4,
            out_specs=(pl.BlockSpec(memory_space=pl.ANY),) * 3,
            scratch_shapes=scratch,
            compiler_params=pltpu.CompilerParams(
                collective_id=0, has_side_effects=True, vmem_limit_bytes=60000 * 1024),
            name="deflated_cg",
        )(right_side, start_field, coef, deflation)
        return pl.pallas_call(
            functools.partial(hand_over, 2),
            out_shape=(out, out, out),
            in_specs=[pl.BlockSpec(memory_space=pl.ANY)] * 3,
            out_specs=(pl.BlockSpec(memory_space=pl.ANY),) * 3,
            scratch_shapes=[vm(*field), vm(*field), vm(*field), dma(3, 2), dma(3, 2)],
            name="hand_over",
        )(*results)

    spec = P("gx", "gy", None)
    return jax.shard_map(
        per_device, mesh=mesh, in_specs=(spec, spec, spec, P(None, "gx", "gy", None)),
        out_specs=(spec, spec, spec), check_vma=False)
```

```python
import functools
import jax, jax.numpy as jnp
from jax import lax
from jax.experimental import pallas as pl
from jax.experimental.pallas import tpu as pltpu
from jax.sharding import PartitionSpec as P

F32 = jnp.float32
BF = jnp.bfloat16


def iota(shape, dim):
    return lax.broadcasted_iota(jnp.int32, shape, dim)


def split3(v):
    high = v.astype(BF)
    rest = v - high.astype(F32)
    mid = rest.astype(BF)
    low = (rest - mid.astype(F32)).astype(BF)
    return high, mid, low


def mm(left, right):
    lh, lm, ll = left
    rh, rm, rl = right
    if lh.shape[1] < 128:
        d = lambda p, q: jnp.dot(p, q, preferred_element_type=F32)
        return d(lh, rh) + (d(lh, rm) + d(lm, rh)) + (d(lm, rm) + d(lh, rl) + d(ll, rh))
    return jnp.dot(
        jnp.concatenate([lh, lh, lm, lm, lh, ll], axis=1),
        jnp.concatenate([rh, rm, rh, rm, rl, rh], axis=0), preferred_element_type=F32)


def invert_pairs(m_ref, count):
    lane = iota((8, 128), 1)
    sub = iota((8, 128), 0)
    half = lane // 64 * 64
    left = lane < 64
    wide_panel = iota((64, 128), 1) % 64 // 8
    ahead = [m_ref[s, 0:8, :] for s in range(count)]
    for p in range(8):
        in_panel = (lane - half) // 8 == p
        done = (lane - half) // 8 < p
        ident = (lane - half - p * 8) == sub
        index = [half + p * 8 + j for j in range(8)]
        rows, piv, cols, near = [], [], [], []
        for s in range(count):
            r = ahead[s]
            piv.append([jnp.take_along_axis(r, index[j], axis=1) for j in range(8)])
            rows.append(jnp.where(in_panel, jnp.where(ident, 1.0, 0.0), r))
            flip = jnp.where(done, -r, r)
            c = jnp.concatenate([flip[:, :64], pltpu.roll(flip, 64, 1)[:, :64]], axis=0)
            ch, cm, cl = split3(c)
            cols.append(jnp.transpose(jnp.concatenate([ch, ch, cm, cm, ch, cl], axis=0).astype(F32)).astype(BF))
            if p < 7:
                raw = m_ref[s, 8 * p + 8 : 8 * p + 16, :]
                near.append([jnp.take_along_axis(raw, index[j], axis=1) for j in range(8)])
                ahead[s] = jnp.where(in_panel, 0.0, raw)
        for t in range(8):
            own = sub == t
            for s in range(count):
                mult = piv[s][t]
                scale = 1.0 / mult[t : t + 1, :]
                row = rows[s][t : t + 1, :]
                rows[s] = jnp.where(own, row * scale, rows[s] - (mult * row) * scale)
                for j in range(t + 1, 8):
                    prow = piv[s][j][t : t + 1, :]
                    piv[s][j] = jnp.where(own, prow * scale, piv[s][j] - (mult * prow) * scale)
        for s in range(count):
            if p < 7:
                terms = [near[s][j] * rows[s][j : j + 1, :] for j in range(8)]
                while len(terms) > 1:
                    terms = [terms[i] + terms[i + 1] for i in range(0, len(terms), 2)]
                ahead[s] = ahead[s] - terms[0]
            r = jnp.concatenate([jnp.where(left, rows[s], 0.0), jnp.where(left, 0.0, rows[s])], axis=0)
            rh, rm, rl = split3(r)
            right = jnp.concatenate([rh, rm, rh, rm, rl, rh], axis=0)
            new = jnp.where(wide_panel == p, 0.0, m_ref[s]) - jnp.dot(cols[s], right, preferred_element_type=F32)
            for v in range(8):
                m_ref[s, 8 * v : 8 * v + 8, :] = rows[s] if v == p else new[8 * v : 8 * v + 8, :]


def invert_chains(m_ref, count):
    lane = iota((8, 128), 1)
    sub = iota((8, 128), 0)
    half = lane // 64 * 64
    block = lane % 64 // 8
    left = lane < 64
    wide_block = iota((64, 128), 1) % 64 // 8
    gone = []
    for together in ([1, 3, 5, 7], [2, 6], [4], [0]):
        done = functools.reduce(jnp.logical_or, [block == q for q in gone], lane < 0)
        keys = [(s, p) for s in range(count) for p in together]
        rows, piv, cols = {}, {}, []
        for s, p in keys:
            r = m_ref[s, 8 * p : 8 * p + 8, :]
            piv[s, p] = [jnp.take_along_axis(r, half + p * 8 + j, axis=1) for j in range(8)]
            rows[s, p] = jnp.where(block == p, jnp.where(lane - half - p * 8 == sub, 1.0, 0.0), r)
        for s in range(count):
            flips = [jnp.where(done, -m_ref[s, 8 * p : 8 * p + 8, :], m_ref[s, 8 * p : 8 * p + 8, :]) for p in together]
            c = jnp.concatenate([f[:, :64] for f in flips] + [pltpu.roll(f, 64, 1)[:, :64] for f in flips], axis=0)
            ch, cm, cl = split3(c)
            cols.append(jnp.transpose(jnp.concatenate([ch, ch, cm, cm, ch, cl], axis=0).astype(F32)).astype(BF))
        for t in range(8):
            own = sub == t
            for key in keys:
                mult = piv[key][t]
                scale = 1.0 / mult[t : t + 1, :]
                row = rows[key][t : t + 1, :]
                rows[key] = jnp.where(own, row * scale, rows[key] - (mult * row) * scale)
                for j in range(t + 1, 8):
                    prow = piv[key][j][t : t + 1, :]
                    piv[key][j] = jnp.where(own, prow * scale, piv[key][j] - (mult * prow) * scale)
        cleared = functools.reduce(jnp.logical_or, [wide_block == p for p in together])
        for s in range(count):
            r = jnp.concatenate(
                [jnp.where(left, rows[s, p], 0.0) for p in together]
                + [jnp.where(left, 0.0, rows[s, p]) for p in together], axis=0)
            rh, rm, rl = split3(r)
            right = jnp.concatenate([rh, rm, rh, rm, rl, rh], axis=0)
            new = jnp.where(cleared, 0.0, m_ref[s]) - jnp.dot(cols[s], right, preferred_element_type=F32)
            for v in range(8):
                m_ref[s, 8 * v : 8 * v + 8, :] = rows[s, v] if v in together else new[8 * v : 8 * v + 8, :]
        gone = gone + together


def unit_columns(y_ref, a, b, na, nb):
    lane = iota((64, 128), 1)
    rowi = iota((64, 128), 0)
    group = lane // 8
    own = (b * na + a) * 8
    target = jnp.where(group == 0, own, -4096)
    target = jnp.where((group == 1) & (a > 0), own - 8, target)
    target = jnp.where((group == 2) & (a < na - 1), own + 8, target)
    target = jnp.where((group == 3) & (b > 0), own - 64, target)
    target = jnp.where((group == 4) & (b < nb - 1), own + 64, target)
    target = target + lane % 8
    for j in range(nb):
        y_ref[j] = jnp.where(rowi + 64 * j == target, 1.0, 0.0)


def factor(tiles, d_ref, lu_ref, w_ref, y_ref, m_ref, x_ref, xt_ref, a, b, na, nb):
    lane = iota((64, 128), 1)
    low = lane < 64
    for j in range(nb):
        d_ref[j] = tiles[j]
    for j in range(nb):
        left = pltpu.roll(tiles[j], 64, 1)
        if j < nb - 1:
            up = jnp.transpose(tiles[j + 1])[64:128, :]
            up = jnp.concatenate([jnp.zeros((64, 64), F32), up], axis=1)
        else:
            up = jnp.zeros((64, 128), F32)
        left = jnp.where(low, left, 0.0) if j > 0 else jnp.zeros((64, 128), F32)
        lu_ref[j] = jnp.where(low, left, up)

    def invert(lines, step):
        slots = (len(lines) + 1) // 2
        for s in range(slots):
            first = d_ref[lines[2 * s]]
            second = d_ref[lines[min(2 * s + 1, len(lines) - 1)]]
            m_ref[s] = jnp.where(low, first, pltpu.roll(second, 64, 1))
        (invert_chains if step == 1 and len(lines) > 1 else invert_pairs)(m_ref, slots)
        out = []
        for i in range(len(lines)):
            v = m_ref[i // 2]
            out.append(v[:, :64] if i % 2 == 0 else pltpu.roll(v, 64, 1)[:, :64])
        return out

    step = 1
    levels = []
    while step < nb:
        lines = list(range(step, nb, 2 * step))
        inverses = invert(lines, step)
        for j, inv in zip(lines, inverses):
            right = jnp.concatenate([lu_ref[j], y_ref[j]], axis=1)
            lut = jnp.transpose(lu_ref[j])
            w = mm(split3(inv), split3(right))
            w_ref[j] = w
            p = mm(split3(lut), split3(w))
            i, k = j - step, j + step
            d_ref[i] = d_ref[i] - p[:64, :128]
            y_ref[i] = y_ref[i] - p[:64, 128:]
            lu_ref[i] = jnp.where(low, lu_ref[i], -p[:64, :128])
            if k < nb:
                d_ref[k] = d_ref[k] - pltpu.roll(p[64:, :128], 64, 1)
                y_ref[k] = y_ref[k] - p[64:, 128:]
                lu_ref[k] = jnp.where(low, -p[64:, :128], lu_ref[k])
        levels.append((step, lines))
        step *= 2
    inv = invert([0], step)[0]
    x_ref[0:64] = mm(split3(inv), split3(y_ref[0]))
    for step, lines in reversed(levels):
        for j in lines:
            i, k = j - step, j + step
            below = x_ref[64 * i : 64 * i + 64]
            above = x_ref[64 * k : 64 * k + 64] if k < nb else jnp.zeros((64, 128), F32)
            both = jnp.concatenate([below, above], axis=0)
            w = w_ref[j]
            x_ref[64 * j : 64 * j + 64] = w[:, 128:] - mm(split3(w[:, :128]), split3(both))
    for k in range(8):
        xt_ref[k] = jnp.transpose(x_ref[pl.ds(k, na * nb, stride=8), :])[:40, :]


def total_rows(accs):
    sub = iota((8, 128), 0)
    out = jnp.zeros((8, 128), F32)
    for i, acc in enumerate(accs):
        out = jnp.where(sub == i, jnp.sum(acc, axis=0, keepdims=True), out)
    return jnp.broadcast_to(jnp.sum(out, axis=1, keepdims=True), (8, 128))


def fold(value):
    rows, cols = value.shape
    pieces = [value[8 * i : 8 * i + 8, 128 * j : 128 * j + 128] for i in range(rows // 8) for j in range(cols // 128)]
    while len(pieces) > 1:
        pieces = [pieces[i] + pieces[i + 1] if i + 1 < len(pieces) else pieces[i] for i in range(0, len(pieces), 2)]
    return pieces[0]


def face_of(lower, upper):
    summed = lower + upper
    return jnp.where((lower > 0.0) & (upper > 0.0), 2.0 * lower * upper / summed, summed)


def body(na, nb, rhs_hbm, x0_hbm, c_hbm, z_hbm, sol_hbm, res_hbm, dir_hbm, *scratch):
    (zf, az, cf, xf, rf, vf, wf, uf, tf, pf, qf, ph, qh, fx, fyl, fyh, fzl, fzh, dg, rd,
     wx, wy, hxz, hyz, hxc, hyc, hxx, hyx, hxv, hyv, pyz, pyc, pyx, pyv, nx, ny, fcx, fcy,
     cc, ge, et, gb, tb,
     d_ref, lu_ref, w_ref, y_ref, m_ref, x_ref, xt_ref,
     ld_sem, st_sem, hs_sem, hr_sem, es_sem, er_sem, gs_sem, gr_sem, all_sem) = scratch
    cx, cy, nz = cf.shape
    nk = zf.shape[0]
    a = lax.axis_index("gx")
    b = lax.axis_index("gy")
    mesh_id = pl.DeviceIdType.MESH
    loads = [
        pltpu.make_async_copy(c_hbm, cf, ld_sem.at[0]),
        pltpu.make_async_copy(x0_hbm, xf, ld_sem.at[1]),
        pltpu.make_async_copy(rhs_hbm, rf, ld_sem.at[2]),
        pltpu.make_async_copy(z_hbm, zf, ld_sem.at[3]),
    ]
    for i in (0, 3, 1, 2):
        loads[i].start()
    barrier = pltpu.get_barrier_semaphore()
    for o in range(1, na):
        pl.semaphore_signal(barrier, inc=1, device_id=(lax.rem(a + o, na), b), device_id_type=mesh_id)
    for o in range(1, nb):
        pl.semaphore_signal(barrier, inc=1, device_id=(a, lax.rem(b + o, nb)), device_id_type=mesh_id)

    has = [a > 0, a < na - 1, b > 0, b < nb - 1]
    peers = [(a - 1, b), (a + 1, b), (a, b - 1), (a, b + 1)]

    def halo(slot, sources, targets):
        def copy(s):
            return pltpu.make_async_remote_copy(
                src_ref=sources[s], dst_ref=targets[s ^ 1],
                send_sem=hs_sem.at[slot, s], recv_sem=hr_sem.at[slot, s ^ 1],
                device_id=peers[s], device_id_type=mesh_id)

        def start():
            for s in range(4):
                @pl.when(has[s])
                def _():
                    copy(s).start()

        def wait_recv():
            for s in range(4):
                @pl.when(has[s])
                def _():
                    pltpu.make_async_remote_copy(
                        src_ref=sources[s], dst_ref=targets[s],
                        send_sem=hs_sem.at[slot, s], recv_sem=hr_sem.at[slot, s],
                        device_id=peers[s], device_id_type=mesh_id).wait_recv()

        def wait_send():
            for s in range(4):
                @pl.when(has[s])
                def _():
                    copy(s).wait_send()

        return start, wait_recv, wait_send

    row0 = iota((cy, nz), 0) == 0
    rowl = iota((cy, nz), 0) == cy - 1
    lan0 = iota((cy, nz), 1) == 0
    lanl = iota((cy, nz), 1) == nz - 1

    for s in range(2):
        @pl.when(jnp.logical_not(has[s]))
        def _():
            hxz[s] = jnp.zeros(hxz.shape[1:], F32)
            hxc[s] = jnp.zeros(hxc.shape[1:], F32)
            hxx[s] = jnp.zeros(hxx.shape[1:], F32)
            for i in range(2):
                hxv[i, s] = jnp.zeros(hxv.shape[2:], F32)

        @pl.when(jnp.logical_not(has[2 + s]))
        def _():
            hyz[s] = jnp.zeros(hyz.shape[1:], F32)
            hyc[s] = jnp.zeros(hyc.shape[1:], F32)
            hyx[s] = jnp.zeros(hyx.shape[1:], F32)
            for i in range(2):
                hyv[i, s] = jnp.zeros(hyv.shape[2:], F32)

    loads[0].wait()

    def pack(x, carry):
        pyc[0, pl.ds(x, 1), :] = cf[x, 0:1, :]
        pyc[1, pl.ds(x, 1), :] = cf[x, cy - 1 : cy, :]
        return carry

    lax.fori_loop(0, cx, pack, 0)

    fx[0] = jnp.zeros((cy, nz), F32)
    fx[cx] = jnp.zeros((cy, nz), F32)

    def faces_x(x, carry):
        fx[x] = face_of(cf[x - 1], cf[x])
        return carry

    lax.fori_loop(1, cx, faces_x, 0)

    def faces(x, carry):
        c = cf[x]
        yl = jnp.where(row0, 0.0, face_of(pltpu.roll(c, 1, 0), c))
        yh = jnp.where(rowl, 0.0, face_of(c, pltpu.roll(c, cy - 1, 0)))
        zl = jnp.where(lan0, c, face_of(pltpu.roll(c, 1, 1), c))
        zh = jnp.where(lanl, c, face_of(c, pltpu.roll(c, nz - 1, 1)))
        dg[x] = fx[x] + fx[x + 1] + yl + yh + zl + zh
        fyl[x] = yl
        fyh[x] = yh
        fzl[x] = jnp.where(lan0, 0.0, zl)
        fzh[x] = jnp.where(lanl, 0.0, zh)
        return carry

    lax.fori_loop(0, cx, faces, 0)

    pl.semaphore_wait(barrier, na + nb - 2)
    for o in range(1, nb):
        pl.semaphore_signal(all_sem, inc=1, device_id=(a, lax.rem(b + o, nb)), device_id_type=mesh_id)
    coef_halo = halo(0, [cf.at[0], cf.at[cx - 1], pyc.at[0], pyc.at[1]], [hxc.at[0], hxc.at[1], hyc.at[0], hyc.at[1]])
    coef_halo[0]()
    loads[3].wait()

    def packz(x, carry):
        for k in range(nk):
            pyz[0, k, pl.ds(x, 1), :] = zf[k, x, 0:1, :]
            pyz[1, k, pl.ds(x, 1), :] = zf[k, x, cy - 1 : cy, :]
        return carry

    lax.fori_loop(0, cx, packz, 0)
    z_halo = halo(2, [zf.at[:, 0], zf.at[:, cx - 1], pyz.at[0], pyz.at[1]], [hxz.at[0], hxz.at[1], hyz.at[0], hyz.at[1]])
    z_halo[0]()
    loads[1].wait()

    def packx(x, carry):
        pyx[0, pl.ds(x, 1), :] = xf[x, 0:1, :]
        pyx[1, pl.ds(x, 1), :] = xf[x, cy - 1 : cy, :]
        return carry

    lax.fori_loop(0, cx, packx, 0)
    x_halo = halo(1, [xf.at[0], xf.at[cx - 1], pyx.at[0], pyx.at[1]], [hxx.at[0], hxx.at[1], hyx.at[0], hyx.at[1]])
    x_halo[0]()

    def inner_apply(v, before, after, x):
        near = fx[x] * before + fx[x + 1] * after
        near = near + fyl[x] * pltpu.roll(v, 1, 0) + fyh[x] * pltpu.roll(v, cy - 1, 0)
        near = near + fzl[x] * pltpu.roll(v, 1, 1) + fzh[x] * pltpu.roll(v, nz - 1, 1)
        return dg[x] * v - near

    def below(x):
        return jnp.maximum(x - 1, 0)

    def above(x):
        return jnp.minimum(x + 1, cx - 1)

    def make_az(x, carry):
        for k in range(nk):
            az[k, x] = inner_apply(zf[k, x], zf[k, below(x)], zf[k, above(x)], x)
        return carry

    lax.fori_loop(0, cx, make_az, 0)

    coef_halo[1]()
    for s in range(2):
        wx[s] = face_of(cf[s * (cx - 1)], hxc[s])
        wy[s] = face_of(pyc[s], hyc[s])
        dg[s * (cx - 1)] = dg[s * (cx - 1)] + wx[s]
        for k in range(nk):
            az[k, s * (cx - 1)] = az[k, s * (cx - 1)] + wx[s] * zf[k, s * (cx - 1)]
    top8 = iota((8, nz), 0) == 0
    bot8 = iota((8, nz), 0) == 7

    def fix(x, carry):
        lo = jnp.where(top8, wy[0, pl.ds(x, 1), :], 0.0)
        hi = jnp.where(bot8, wy[1, pl.ds(x, 1), :], 0.0)
        dg[x, 0:8, :] = dg[x, 0:8, :] + lo
        dg[x, cy - 8 : cy, :] = dg[x, cy - 8 : cy, :] + hi
        for k in range(nk):
            az[k, x, 0:8, :] = az[k, x, 0:8, :] + lo * zf[k, x, 0:8, :]
            az[k, x, cy - 8 : cy, :] = az[k, x, cy - 8 : cy, :] + hi * zf[k, x, cy - 8 : cy, :]
        rd[x] = 1.0 / dg[x]
        return carry

    lax.fori_loop(0, cx, fix, 0)

    pairs = [(k, l) for k in range(nk) for l in range(k, nk)]

    def gram(x, accs):
        accs = list(accs)
        for i in range(cy // 8):
            for j in range(nz // 128):
                zs = [zf[k, x, 8 * i : 8 * i + 8, 128 * j : 128 * j + 128] for k in range(nk)]
                for l in range(nk):
                    w = az[l, x, 8 * i : 8 * i + 8, 128 * j : 128 * j + 128]
                    for k in range(l + 1):
                        n = pairs.index((k, l))
                        accs[n] = accs[n] + zs[k] * w
        return tuple(accs)

    diag = lax.fori_loop(0, cx, gram, tuple(jnp.zeros((8, 128), F32) for _ in pairs))

    z_halo[1]()
    for s in range(2):
        for k in range(nk):
            nx[s, k] = -(wx[s] * hxz[s, k])
            ny[s, k] = -(wy[s] * hyz[s, k])

    lane = iota((8, 128), 1)
    sub = iota((8, 128), 0)
    tile = jnp.zeros((8, 128), F32)
    for l in range(nk):
        v = total_rows([diag[pairs.index((min(k, l), max(k, l)))] for k in range(nk)])
        tile = tile + jnp.where(lane == 8 + l, v, 0.0)
    tb[0] = tile

    def off_blocks(l, carry):
        out = tb[0]
        for s in range(2):
            v = total_rows([fold(zf[k, s * (cx - 1)] * nx[s, l]) for k in range(nk)])
            out = out + jnp.where(lane == 16 * s + l, v, 0.0)
        v = total_rows([fold(pyz[0, k] * ny[0, l]) for k in range(nk)])
        tb[0] = out + jnp.where(lane == 24 + l, v, 0.0)
        return carry

    lax.fori_loop(0, nk, off_blocks, 0)
    tile = jnp.take_along_axis(tb[0], lane % 32, axis=1)
    tile = jnp.where(lane // 32 == sub % 4, tile, 0.0)
    upper = jnp.sum(jnp.where(sub < 4, tile, 0.0), axis=0, keepdims=True)
    lower = jnp.sum(jnp.where(sub < 4, 0.0, tile), axis=0, keepdims=True)


    def wait_bytes(ref, sem):
        pltpu.make_async_copy(ref, ref, sem).wait()

    def message_rows(groups):
        out = jnp.zeros((1, 128), F32)
        for q, accs in groups:
            v = total_rows(accs)
            out = out + jnp.sum(jnp.where(lane == 8 * q + sub, v, 0.0), axis=0, keepdims=True)
        return out

    half_y, half_z = na // 2, 4 if nb % 4 == 0 else 1
    side_x = nb // half_z
    hops = lambda d, n: min(d, n - d)
    offsets = sorted(
        [(i, j, k, 1 - c) for i in range(half_y) for j in range(half_z) for k in range(side_x) for c in range(2)],
        key=lambda o: -(hops(o[0], half_y) + hops(o[1], half_z) + hops(o[2], side_x)))
    me = b * na + a

    def spread(own, ssem, rsem):
        for dy, dz, dx, dc in offsets:
            if (dy, dz, dx, dc) == (0, 0, 0, 0):
                continue
            to_a = 2 * lax.rem(a // 2 + dy, half_y) + (1 - lax.rem(a, 2) if dc else lax.rem(a, 2))
            to_b = side_x * lax.rem(b // side_x + dz, half_z) + lax.rem(lax.rem(b, side_x) + dx, side_x)
            pltpu.make_async_remote_copy(
                src_ref=own, dst_ref=own, send_sem=ssem, recv_sem=rsem,
                device_id=(to_a, to_b), device_id_type=mesh_id).start()

    def send(phase, groups):
        gb[phase, pl.ds(me, 1), :] = message_rows(groups)
        spread(gb.at[phase, pl.ds(me, 1)], gs_sem.at[phase], gr_sem.at[phase])

    def receive(phase):
        wait_bytes(gb.at[phase, pl.ds(0, na * nb - 1)], gr_sem.at[phase])
        return jnp.transpose(gb[phase])

    et[pl.ds(2 * me, 1), :] = upper
    et[pl.ds(2 * me + 1, 1), :] = lower
    pl.semaphore_wait(all_sem, nb - 1)
    spread(et.at[pl.ds(pl.multiple_of(2 * me, 2), 2)], es_sem.at[0], er_sem.at[0])
    x_halo[1]()
    loads[2].wait()

    def minus_faces(v, x, hx, hy):
        v = v + jnp.where(row0, wy[0, pl.ds(x, 1), :] * hy[0, pl.ds(x, 1), :], 0.0)
        return v + jnp.where(rowl, wy[1, pl.ds(x, 1), :] * hy[1, pl.ds(x, 1), :], 0.0)

    def first(x, accs):
        ax = inner_apply(xf[x], xf[below(x)], xf[above(x)], x)
        r = minus_faces(rf[x] - ax, x, hxx, hyx)
        r = r + jnp.where(x == 0, wx[0] * hxx[0], 0.0) + jnp.where(x == cx - 1, wx[1] * hxx[1], 0.0)
        rf[x] = r
        return tuple(accs[k] + fold(zf[k, x] * r) for k in range(nk))

    rest = lax.fori_loop(0, cx, first, tuple(jnp.zeros((8, 128), F32) for _ in range(nk)))

    unit_columns(y_ref, a, b, na, nb)
    wait_bytes(et.at[pl.ds(0, 2 * (na * nb - 1))], er_sem.at[0])
    send(0, [(0, list(rest))])

    def expand(j, carry):
        start = pl.multiple_of(2 * na * j, 2 * na)
        for i in range(na):
            packed = jnp.where(sub < 4, et[pl.ds(start + 2 * i, 1), :], et[pl.ds(start + 2 * i + 1, 1), :])
            side = lane >= 64
            at = jnp.where(side, lane - 64 - 8 * i, lane + 8 - 8 * i)
            good = (at >= 0) & (at < jnp.where(side, 8, 24))
            source = 32 * (sub % 4) + jnp.where(good, at, 0) + jnp.where(side, 24, 0)
            ge[j, 8 * i : 8 * i + 8, :] = jnp.where(good, jnp.take_along_axis(packed, source, axis=1), 0.0)
        return carry

    lax.fori_loop(0, nb, expand, 0)

    factor([ge[j] for j in range(nb)], d_ref, lu_ref, w_ref, y_ref, m_ref, x_ref, xt_ref, a, b, na, nb)

    def coarse_of(got):
        g = got[0:8]
        g = g + pltpu.roll(got[8:16], na * nb - 1, 1) + pltpu.roll(got[16:24], 1, 1)
        g = g + pltpu.roll(got[24:32], na * nb - na, 1) + pltpu.roll(got[32:40], na, 1)
        c = xt_ref[0] * g[0:1, :]
        for k in range(1, nk):
            c = c + xt_ref[k] * g[k : k + 1, :]
        return jnp.broadcast_to(jnp.sum(c, axis=1, keepdims=True), (40, nz))

    def keep(c):
        cc[...] = c
        for s in range(2):
            u = nx[s, 0] * cc[8 * s + 8 : 8 * s + 9, :]
            v = ny[s, 0] * cc[8 * s + 24 : 8 * s + 25, :]
            for k in range(1, nk):
                u = u + nx[s, k] * cc[8 * s + 8 + k : 8 * s + 9 + k, :]
                v = v + ny[s, k] * cc[8 * s + 24 + k : 8 * s + 25 + k, :]
            fcx[s] = u
            fcy[s] = v

    def span(vectors, x):
        out = vectors[0, x] * cc[0:1, :]
        for k in range(1, nk):
            out = out + vectors[k, x] * cc[k : k + 1, :]
        return out

    def image(x):
        out = span(az, x)
        out = out + jnp.where(row0, fcy[0, pl.ds(x, 1), :], 0.0) + jnp.where(rowl, fcy[1, pl.ds(x, 1), :], 0.0)
        return out + jnp.where(x == 0, fcx[0], 0.0) + jnp.where(x == cx - 1, fcx[1], 0.0)

    def scalar(got, row):
        return jnp.sum(got[row : row + 1, :], axis=1, keepdims=True)

    zero = jnp.zeros((8, 128), F32)

    def restrict_slab(x, v, field, slot, accs):
        field[x] = v
        pyv[slot, 0, pl.ds(x, 1), :] = v[0:1, :]
        pyv[slot, 1, pl.ds(x, 1), :] = v[cy - 1 : cy, :]
        return tuple(accs[k] + fold(az[k, x] * v) for k in range(nk))

    def finish_groups(field, slot, accs):
        groups = [(0, list(accs[:nk])), (5, list(accs[nk:]))]
        for s in range(2):
            groups.append((1 + s, [fold(nx[s, k] * field[s * (cx - 1)]) for k in range(nk)]))
            groups.append((3 + s, [fold(ny[s, k] * pyv[slot, s]) for k in range(nk)]))
        return groups

    fields = [vf, uf]
    v_halos = [
        halo(3 + i, [fields[i].at[0], fields[i].at[cx - 1], pyv.at[i, 0], pyv.at[i, 1]],
             [hxv.at[i, 0], hxv.at[i, 1], hyv.at[i, 0], hyv.at[i, 1]])
        for i in range(2)
    ]

    def apply_all(i, out):
        field, hx, hy = fields[i], hxv.at[i], hyv.at[i]

        def slab(x, carry):
            w = inner_apply(field[x], field[below(x)], field[above(x)], x)
            w = w - jnp.where(row0, wy[0, pl.ds(x, 1), :] * hy[0, pl.ds(x, 1), :], 0.0)
            w = w - jnp.where(rowl, wy[1, pl.ds(x, 1), :] * hy[1, pl.ds(x, 1), :], 0.0)
            out[x] = w - jnp.where(x == 0, wx[0] * hx[0], 0.0) - jnp.where(x == cx - 1, wx[1] * hx[1], 0.0)
            return carry

        lax.fori_loop(0, cx, slab, 0)

    keep(coarse_of(receive(0)))
    x_halo[2]()

    def deflate(x, accs):
        xf[x] = xf[x] + span(zf, x)
        r = rf[x] - image(x)
        rf[x] = r
        v = r * rd[x]
        return restrict_slab(x, v, vf, 0, accs) + (accs[nk] + fold(r * v),)

    accs = lax.fori_loop(0, cx, deflate, (zero,) * (nk + 1))
    v_halos[0][0]()
    send(1, finish_groups(vf, 0, accs))
    v_halos[0][1]()
    apply_all(0, wf)
    got = receive(1)
    keep(coarse_of(got))
    inner = scalar(got, 40)

    def sums(x, p, q, v, slot, accs):
        u = q * rd[x]
        more = (accs[nk] + fold(p * q), accs[nk + 1] + fold(q * v), accs[nk + 2] + fold(q * u))
        return restrict_slab(x, u, uf, slot, accs) + more

    def direction(x, accs):
        v = vf[x]
        p = v - span(zf, x)
        q = wf[x] - image(x)
        pf[x] = p
        qf[x] = q
        return sums(x, p, q, v, 1, accs)

    accs = lax.fori_loop(0, cx, direction, (zero,) * (nk + 3))
    v_halos[1][0]()
    send(2, finish_groups(uf, 1, accs))
    v_halos[0][2]()
    v_halos[1][1]()
    apply_all(1, tf)

    def advance(got, inner):
        step = inner / scalar(got, 40)
        new = inner - 2.0 * step * scalar(got, 41) + step * step * scalar(got, 42)
        keep(cc[...] - step * coarse_of(got))
        return step, new, new / inner

    got = receive(2)
    step, inner, beta = advance(got, inner)
    v_halos[1][2]()

    def next_direction(x, accs):
        v = vf[x] - step * uf[x]
        vf[x] = v
        p = v + beta * pf[x] - span(zf, x)
        q = wf[x] - step * tf[x] + beta * qf[x] - image(x)
        ph[x] = p
        qh[x] = q
        return sums(x, p, q, v, 2, accs)

    accs = lax.fori_loop(0, cx, next_direction, (zero,) * (nk + 3))
    send(3, finish_groups(uf, 2, accs))

    def move(x, carry):
        xf[x] = xf[x] + step * pf[x]
        rf[x] = rf[x] - step * qf[x]
        return carry

    lax.fori_loop(0, cx, move, 0)
    got = receive(3)
    last_step, inner, beta = advance(got, inner)

    def last_move(x, carry):
        xf[x] = xf[x] + last_step * ph[x]
        rf[x] = rf[x] - last_step * qh[x]
        return carry

    def last(x, carry):
        pf[x] = vf[x] - last_step * uf[x] + beta * ph[x] - span(zf, x)
        return carry

    lax.fori_loop(0, cx, last_move, 0)
    stores = [
        pltpu.make_async_copy(xf, sol_hbm, st_sem.at[0]),
        pltpu.make_async_copy(rf, res_hbm, st_sem.at[1]),
        pltpu.make_async_copy(pf, dir_hbm, st_sem.at[2]),
    ]
    stores[0].start()
    stores[1].start()
    lax.fori_loop(0, cx, last, 0)
    stores[2].start()
    for h in (coef_halo, z_halo):
        h[2]()
    wait_bytes(et.at[pl.ds(0, 2 * (na * nb - 1))], es_sem.at[0])
    for phase in range(4):
        wait_bytes(gb.at[phase, pl.ds(0, na * nb - 1)], gs_sem.at[phase])
    for store in stores:
        store.wait()


def hand_over(count, *refs):
    ins, outs, held = refs[:3], refs[3:6], refs[6:9]
    load_sem, store_sem = refs[9:]
    piece = ins[0].shape[0] // count
    every = [(i, j) for j in range(count) for i in range(3)]

    def load(i, j):
        part = pl.ds(j * piece, piece)
        return pltpu.make_async_copy(ins[i].at[part], held[i].at[part], load_sem.at[i, j])

    def store(i, j):
        part = pl.ds(j * piece, piece)
        return pltpu.make_async_copy(held[i].at[part], outs[i].at[part], store_sem.at[i, j])

    for i, j in every:
        load(i, j).start()
    for i, j in every:
        load(i, j).wait()
        store(i, j).start()
    for i, j in every:
        store(i, j).wait()


def solution(mesh):
    na, nb = mesh.shape["gx"], mesh.shape["gy"]

    def per_device(right_side, start_field, coef, deflation):
        nk, cx, cy, nz = deflation.shape
        vm = lambda *shape: pltpu.VMEM(shape, F32)
        dma = lambda *shape: pltpu.SemaphoreType.DMA(shape)
        field = (cx, cy, nz)
        scratch = [
            vm(nk, *field), vm(nk, *field)] + [vm(*field) for _ in range(11)] + [
            vm(cx + 1, cy, nz), vm(*field), vm(*field), vm(*field), vm(*field), vm(*field), vm(*field),
            vm(2, cy, nz), vm(2, cx, nz),
            vm(2, nk, cy, nz), vm(2, nk, cx, nz), vm(2, cy, nz), vm(2, cx, nz), vm(2, cy, nz), vm(2, cx, nz),
            vm(2, 2, cy, nz), vm(2, 2, cx, nz),
            vm(2, nk, cx, nz), vm(2, cx, nz), vm(2, cx, nz), vm(3, 2, cx, nz),
            vm(2, nk, cy, nz), vm(2, nk, cx, nz), vm(2, cy, nz), vm(2, cx, nz),
            vm(40, nz), vm(nb, 64, 128), vm(2 * na * nb, 128), vm(4, na * nb, 128), vm(1, 8, 128),
            vm(nb, 64, 128), vm(nb, 64, 128), vm(nb, 64, 256), vm(nb, 64, 128), vm((nb // 2 + 1) // 2, 64, 128),
            vm(nb * 64, 128), vm(8, 40, 128),
            dma(4), dma(3), dma(5, 4), dma(5, 4), dma(1), dma(1), dma(4), dma(4), pltpu.SemaphoreType.REGULAR,
        ]
        out = jax.ShapeDtypeStruct(field, F32)
        results = pl.pallas_call(
            functools.partial(body, na, nb),
            out_shape=(out, out, out),
            in_specs=[pl.BlockSpec(memory_space=pl.ANY)] * 4,
            out_specs=(pl.BlockSpec(memory_space=pl.ANY),) * 3,
            scratch_shapes=scratch,
            compiler_params=pltpu.CompilerParams(
                collective_id=0, has_side_effects=True, vmem_limit_bytes=60000 * 1024),
            name="deflated_cg",
        )(right_side, start_field, coef, deflation)
        return pl.pallas_call(
            functools.partial(hand_over, 2),
            out_shape=(out, out, out),
            in_specs=[pl.BlockSpec(memory_space=pl.ANY)] * 3,
            out_specs=(pl.BlockSpec(memory_space=pl.ANY),) * 3,
            scratch_shapes=[vm(*field), vm(*field), vm(*field), dma(3, 2), dma(3, 2)],
            name="hand_over",
        )(*results)

    spec = P("gx", "gy", None)
    return jax.shard_map(
        per_device, mesh=mesh, in_specs=(spec, spec, spec, P(None, "gx", "gy", None)),
        out_specs=(spec, spec, spec), check_vma=False)
```

```python
import functools
import jax, jax.numpy as jnp
from jax import lax
from jax.experimental import pallas as pl
from jax.experimental.pallas import tpu as pltpu
from jax.sharding import PartitionSpec as P

F32 = jnp.float32
BF = jnp.bfloat16


def iota(shape, dim):
    return lax.broadcasted_iota(jnp.int32, shape, dim)


def split3(v):
    high = v.astype(BF)
    rest = v - high.astype(F32)
    mid = rest.astype(BF)
    low = (rest - mid.astype(F32)).astype(BF)
    return high, mid, low


def mm(left, right):
    lh, lm, ll = left
    rh, rm, rl = right
    if lh.shape[1] < 128:
        d = lambda p, q: jnp.dot(p, q, preferred_element_type=F32)
        return d(lh, rh) + (d(lh, rm) + d(lm, rh)) + (d(lm, rm) + d(lh, rl) + d(ll, rh))
    return jnp.dot(
        jnp.concatenate([lh, lh, lm, lm, lh, ll], axis=1),
        jnp.concatenate([rh, rm, rh, rm, rl, rh], axis=0), preferred_element_type=F32)


def invert_pairs(m_ref, count):
    lane = iota((8, 128), 1)
    sub = iota((8, 128), 0)
    half = lane // 64 * 64
    left = lane < 64
    wide_panel = iota((64, 128), 1) % 64 // 8
    ahead = [m_ref[s, 0:8, :] for s in range(count)]
    for p in range(8):
        in_panel = (lane - half) // 8 == p
        done = (lane - half) // 8 < p
        ident = (lane - half - p * 8) == sub
        index = [half + p * 8 + j for j in range(8)]
        rows, piv, cols, near = [], [], [], []
        for s in range(count):
            r = ahead[s]
            piv.append([jnp.take_along_axis(r, index[j], axis=1) for j in range(8)])
            rows.append(jnp.where(in_panel, jnp.where(ident, 1.0, 0.0), r))
            flip = jnp.where(done, -r, r)
            c = jnp.concatenate([flip[:, :64], pltpu.roll(flip, 64, 1)[:, :64]], axis=0)
            ch, cm, cl = split3(c)
            cols.append(jnp.transpose(jnp.concatenate([ch, ch, cm, cm, ch, cl], axis=0).astype(F32)).astype(BF))
            if p < 7:
                raw = m_ref[s, 8 * p + 8 : 8 * p + 16, :]
                near.append([jnp.take_along_axis(raw, index[j], axis=1) for j in range(8)])
                ahead[s] = jnp.where(in_panel, 0.0, raw)
        for t in range(8):
            own = sub == t
            for s in range(count):
                mult = piv[s][t]
                scale = 1.0 / mult[t : t + 1, :]
                row = rows[s][t : t + 1, :]
                rows[s] = jnp.where(own, row * scale, rows[s] - (mult * row) * scale)
                for j in range(t + 1, 8):
                    prow = piv[s][j][t : t + 1, :]
                    piv[s][j] = jnp.where(own, prow * scale, piv[s][j] - (mult * prow) * scale)
        for s in range(count):
            if p < 7:
                terms = [near[s][j] * rows[s][j : j + 1, :] for j in range(8)]
                while len(terms) > 1:
                    terms = [terms[i] + terms[i + 1] for i in range(0, len(terms), 2)]
                ahead[s] = ahead[s] - terms[0]
            r = jnp.concatenate([jnp.where(left, rows[s], 0.0), jnp.where(left, 0.0, rows[s])], axis=0)
            rh, rm, rl = split3(r)
            right = jnp.concatenate([rh, rm, rh, rm, rl, rh], axis=0)
            new = jnp.where(wide_panel == p, 0.0, m_ref[s]) - jnp.dot(cols[s], right, preferred_element_type=F32)
            for v in range(8):
                m_ref[s, 8 * v : 8 * v + 8, :] = rows[s] if v == p else new[8 * v : 8 * v + 8, :]


def invert_chains(m_ref, count):
    lane = iota((8, 128), 1)
    sub = iota((8, 128), 0)
    half = lane // 64 * 64
    block = lane % 64 // 8
    left = lane < 64
    wide_block = iota((64, 128), 1) % 64 // 8
    gone = []
    for together in ([1, 3, 5, 7], [2, 6], [4], [0]):
        done = functools.reduce(jnp.logical_or, [block == q for q in gone], lane < 0)
        keys = [(s, p) for s in range(count) for p in together]
        rows, piv, cols = {}, {}, []
        for s, p in keys:
            r = m_ref[s, 8 * p : 8 * p + 8, :]
            piv[s, p] = [jnp.take_along_axis(r, half + p * 8 + j, axis=1) for j in range(8)]
            rows[s, p] = jnp.where(block == p, jnp.where(lane - half - p * 8 == sub, 1.0, 0.0), r)
        for s in range(count):
            flips = [jnp.where(done, -m_ref[s, 8 * p : 8 * p + 8, :], m_ref[s, 8 * p : 8 * p + 8, :]) for p in together]
            c = jnp.concatenate([f[:, :64] for f in flips] + [pltpu.roll(f, 64, 1)[:, :64] for f in flips], axis=0)
            ch, cm, cl = split3(c)
            cols.append(jnp.transpose(jnp.concatenate([ch, ch, cm, cm, ch, cl], axis=0).astype(F32)).astype(BF))
        for t in range(8):
            own = sub == t
            for key in keys:
                mult = piv[key][t]
                scale = 1.0 / mult[t : t + 1, :]
                row = rows[key][t : t + 1, :]
                rows[key] = jnp.where(own, row * scale, rows[key] - (mult * row) * scale)
                for j in range(t + 1, 8):
                    prow = piv[key][j][t : t + 1, :]
                    piv[key][j] = jnp.where(own, prow * scale, piv[key][j] - (mult * prow) * scale)
        cleared = functools.reduce(jnp.logical_or, [wide_block == p for p in together])
        for s in range(count):
            r = jnp.concatenate(
                [jnp.where(left, rows[s, p], 0.0) for p in together]
                + [jnp.where(left, 0.0, rows[s, p]) for p in together], axis=0)
            rh, rm, rl = split3(r)
            right = jnp.concatenate([rh, rm, rh, rm, rl, rh], axis=0)
            new = jnp.where(cleared, 0.0, m_ref[s]) - jnp.dot(cols[s], right, preferred_element_type=F32)
            for v in range(8):
                m_ref[s, 8 * v : 8 * v + 8, :] = rows[s, v] if v in together else new[8 * v : 8 * v + 8, :]
        gone = gone + together


def unit_columns(y_ref, a, b, na, nb):
    lane = iota((64, 128), 1)
    rowi = iota((64, 128), 0)
    group = lane // 8
    own = (b * na + a) * 8
    target = jnp.where(group == 0, own, -4096)
    target = jnp.where((group == 1) & (a > 0), own - 8, target)
    target = jnp.where((group == 2) & (a < na - 1), own + 8, target)
    target = jnp.where((group == 3) & (b > 0), own - 64, target)
    target = jnp.where((group == 4) & (b < nb - 1), own + 64, target)
    target = target + lane % 8
    for j in range(nb):
        y_ref[j] = jnp.where(rowi + 64 * j == target, 1.0, 0.0)


def factor(d_ref, lu_ref, w_ref, y_ref, m_ref, x_ref, xt_ref, a, b, na, nb):
    lane = iota((64, 128), 1)
    low = lane < 64
    for j in range(nb):
        left = pltpu.roll(d_ref[j], 64, 1)
        if j < nb - 1:
            up = jnp.transpose(d_ref[j + 1])[64:128, :]
            up = jnp.concatenate([jnp.zeros((64, 64), F32), up], axis=1)
        else:
            up = jnp.zeros((64, 128), F32)
        left = jnp.where(low, left, 0.0) if j > 0 else jnp.zeros((64, 128), F32)
        lu_ref[j] = jnp.where(low, left, up)

    def invert(lines, step):
        slots = (len(lines) + 1) // 2
        for s in range(slots):
            first = d_ref[lines[2 * s]]
            second = d_ref[lines[min(2 * s + 1, len(lines) - 1)]]
            m_ref[s] = jnp.where(low, first, pltpu.roll(second, 64, 1))
        (invert_chains if step == 1 and len(lines) > 1 else invert_pairs)(m_ref, slots)
        out = []
        for i in range(len(lines)):
            v = m_ref[i // 2]
            out.append(v[:, :64] if i % 2 == 0 else pltpu.roll(v, 64, 1)[:, :64])
        return out

    step = 1
    levels = []
    while step < nb:
        lines = list(range(step, nb, 2 * step))
        inverses = invert(lines, step)
        for j, inv in zip(lines, inverses):
            right = jnp.concatenate([lu_ref[j], y_ref[j]], axis=1)
            lut = jnp.transpose(lu_ref[j])
            w = mm(split3(inv), split3(right))
            w_ref[j] = w
            p = mm(split3(lut), split3(w))
            i, k = j - step, j + step
            d_ref[i] = d_ref[i] - p[:64, :128]
            y_ref[i] = y_ref[i] - p[:64, 128:]
            lu_ref[i] = jnp.where(low, lu_ref[i], -p[:64, :128])
            if k < nb:
                d_ref[k] = d_ref[k] - pltpu.roll(p[64:, :128], 64, 1)
                y_ref[k] = y_ref[k] - p[64:, 128:]
                lu_ref[k] = jnp.where(low, -p[64:, :128], lu_ref[k])
        levels.append((step, lines))
        step *= 2
    inv = invert([0], step)[0]
    x_ref[0:64] = mm(split3(inv), split3(y_ref[0]))
    for step, lines in reversed(levels):
        for j in lines:
            i, k = j - step, j + step
            below = x_ref[64 * i : 64 * i + 64]
            above = x_ref[64 * k : 64 * k + 64] if k < nb else jnp.zeros((64, 128), F32)
            both = jnp.concatenate([below, above], axis=0)
            w = w_ref[j]
            x_ref[64 * j : 64 * j + 64] = w[:, 128:] - mm(split3(w[:, :128]), split3(both))
    for k in range(8):
        xt_ref[k] = jnp.transpose(x_ref[pl.ds(k, na * nb, stride=8), :])[:40, :]


def total_rows(accs):
    sub = iota((8, 128), 0)
    out = jnp.zeros((8, 128), F32)
    for i, acc in enumerate(accs):
        out = jnp.where(sub == i, jnp.sum(acc, axis=0, keepdims=True), out)
    return jnp.broadcast_to(jnp.sum(out, axis=1, keepdims=True), (8, 128))


def fold(value):
    rows, cols = value.shape
    pieces = [value[8 * i : 8 * i + 8, 128 * j : 128 * j + 128] for i in range(rows // 8) for j in range(cols // 128)]
    while len(pieces) > 1:
        pieces = [pieces[i] + pieces[i + 1] if i + 1 < len(pieces) else pieces[i] for i in range(0, len(pieces), 2)]
    return pieces[0]


def face_of(lower, upper):
    summed = lower + upper
    return jnp.where((lower > 0.0) & (upper > 0.0), 2.0 * lower * upper / summed, summed)


def body(na, nb, rhs_hbm, x0_hbm, c_hbm, z_hbm, sol_hbm, res_hbm, dir_hbm, *scratch):
    (zf, az, cf, xf, rf, vf, wf, uf, tf, pf, qf, ph, qh, fx, fyl, fyh, fzl, fzh, dg, rd,
     wx, wy, hxz, hyz, hxc, hyc, hxx, hyx, hxv, hyv, pyz, pyc, pyx, pyv, nx, ny, fcx, fcy,
     cc, et, gb,
     d_ref, lu_ref, w_ref, y_ref, m_ref, x_ref, xt_ref,
     ld_sem, st_sem, hs_sem, hr_sem, es_sem, er_sem, gs_sem, gr_sem, all_sem) = scratch
    cx, cy, nz = cf.shape
    nk = zf.shape[0]
    a = lax.axis_index("gx")
    b = lax.axis_index("gy")
    mesh_id = pl.DeviceIdType.MESH
    loads = [
        pltpu.make_async_copy(c_hbm, cf, ld_sem.at[0]),
        pltpu.make_async_copy(x0_hbm, xf, ld_sem.at[1]),
        pltpu.make_async_copy(rhs_hbm, rf, ld_sem.at[2]),
        pltpu.make_async_copy(z_hbm, zf, ld_sem.at[3]),
    ]
    for i in (0, 3, 1, 2):
        loads[i].start()
    barrier = pltpu.get_barrier_semaphore()
    for o in range(1, na):
        pl.semaphore_signal(barrier, inc=1, device_id=(lax.rem(a + o, na), b), device_id_type=mesh_id)
    for o in range(1, nb):
        pl.semaphore_signal(barrier, inc=1, device_id=(a, lax.rem(b + o, nb)), device_id_type=mesh_id)

    has = [a > 0, a < na - 1, b > 0, b < nb - 1]
    peers = [(a - 1, b), (a + 1, b), (a, b - 1), (a, b + 1)]

    def halo(slot, sources, targets):
        def copy(s):
            return pltpu.make_async_remote_copy(
                src_ref=sources[s], dst_ref=targets[s ^ 1],
                send_sem=hs_sem.at[slot, s], recv_sem=hr_sem.at[slot, s ^ 1],
                device_id=peers[s], device_id_type=mesh_id)

        def start():
            for s in range(4):
                @pl.when(has[s])
                def _():
                    copy(s).start()

        def wait_recv():
            for s in range(4):
                @pl.when(has[s])
                def _():
                    pltpu.make_async_remote_copy(
                        src_ref=sources[s], dst_ref=targets[s],
                        send_sem=hs_sem.at[slot, s], recv_sem=hr_sem.at[slot, s],
                        device_id=peers[s], device_id_type=mesh_id).wait_recv()

        def wait_send():
            for s in range(4):
                @pl.when(has[s])
                def _():
                    copy(s).wait_send()

        return start, wait_recv, wait_send

    row0 = iota((cy, nz), 0) == 0
    rowl = iota((cy, nz), 0) == cy - 1
    lan0 = iota((cy, nz), 1) == 0
    lanl = iota((cy, nz), 1) == nz - 1

    for s in range(2):
        @pl.when(jnp.logical_not(has[s]))
        def _():
            hxz[s] = jnp.zeros(hxz.shape[1:], F32)
            hxc[s] = jnp.zeros(hxc.shape[1:], F32)
            hxx[s] = jnp.zeros(hxx.shape[1:], F32)
            for i in range(2):
                hxv[i, s] = jnp.zeros(hxv.shape[2:], F32)

        @pl.when(jnp.logical_not(has[2 + s]))
        def _():
            hyz[s] = jnp.zeros(hyz.shape[1:], F32)
            hyc[s] = jnp.zeros(hyc.shape[1:], F32)
            hyx[s] = jnp.zeros(hyx.shape[1:], F32)
            for i in range(2):
                hyv[i, s] = jnp.zeros(hyv.shape[2:], F32)

    loads[0].wait()

    def pack(x, carry):
        pyc[0, pl.ds(x, 1), :] = cf[x, 0:1, :]
        pyc[1, pl.ds(x, 1), :] = cf[x, cy - 1 : cy, :]
        return carry

    lax.fori_loop(0, cx, pack, 0)

    fx[0] = jnp.zeros((cy, nz), F32)
    fx[cx] = jnp.zeros((cy, nz), F32)

    def faces_x(x, carry):
        fx[x] = face_of(cf[x - 1], cf[x])
        return carry

    lax.fori_loop(1, cx, faces_x, 0)

    def faces(x, carry):
        c = cf[x]
        yl = jnp.where(row0, 0.0, face_of(pltpu.roll(c, 1, 0), c))
        yh = jnp.where(rowl, 0.0, face_of(c, pltpu.roll(c, cy - 1, 0)))
        zl = jnp.where(lan0, c, face_of(pltpu.roll(c, 1, 1), c))
        zh = jnp.where(lanl, c, face_of(c, pltpu.roll(c, nz - 1, 1)))
        dg[x] = fx[x] + fx[x + 1] + yl + yh + zl + zh
        fyl[x] = yl
        fyh[x] = yh
        fzl[x] = jnp.where(lan0, 0.0, zl)
        fzh[x] = jnp.where(lanl, 0.0, zh)
        return carry

    lax.fori_loop(0, cx, faces, 0)

    pl.semaphore_wait(barrier, na + nb - 2)
    for o in range(1, nb):
        pl.semaphore_signal(all_sem, inc=1, device_id=(a, lax.rem(b + o, nb)), device_id_type=mesh_id)
    coef_halo = halo(0, [cf.at[0], cf.at[cx - 1], pyc.at[0], pyc.at[1]], [hxc.at[0], hxc.at[1], hyc.at[0], hyc.at[1]])
    coef_halo[0]()
    loads[3].wait()

    def packz(x, carry):
        for k in range(nk):
            pyz[0, k, pl.ds(x, 1), :] = zf[k, x, 0:1, :]
            pyz[1, k, pl.ds(x, 1), :] = zf[k, x, cy - 1 : cy, :]
        return carry

    lax.fori_loop(0, cx, packz, 0)
    z_halos = [
        halo(5 + k, [zf.at[k, 0], zf.at[k, cx - 1], pyz.at[0, k], pyz.at[1, k]],
             [hxz.at[0, k], hxz.at[1, k], hyz.at[0, k], hyz.at[1, k]])
        for k in range(nk)
    ]
    for z_halo in z_halos:
        z_halo[0]()
    loads[1].wait()

    def packx(x, carry):
        pyx[0, pl.ds(x, 1), :] = xf[x, 0:1, :]
        pyx[1, pl.ds(x, 1), :] = xf[x, cy - 1 : cy, :]
        return carry

    lax.fori_loop(0, cx, packx, 0)
    x_halo = halo(1, [xf.at[0], xf.at[cx - 1], pyx.at[0], pyx.at[1]], [hxx.at[0], hxx.at[1], hyx.at[0], hyx.at[1]])
    x_halo[0]()

    def inner_apply(v, before, after, x):
        near = fx[x] * before + fx[x + 1] * after
        near = near + fyl[x] * pltpu.roll(v, 1, 0) + fyh[x] * pltpu.roll(v, cy - 1, 0)
        near = near + fzl[x] * pltpu.roll(v, 1, 1) + fzh[x] * pltpu.roll(v, nz - 1, 1)
        return dg[x] * v - near

    def below(x):
        return jnp.maximum(x - 1, 0)

    def above(x):
        return jnp.minimum(x + 1, cx - 1)

    def make_az(x, carry):
        for k in range(nk):
            az[k, x] = inner_apply(zf[k, x], zf[k, below(x)], zf[k, above(x)], x)
        return carry

    lax.fori_loop(0, cx, make_az, 0)

    coef_halo[1]()
    for s in range(2):
        wx[s] = face_of(cf[s * (cx - 1)], hxc[s])
        wy[s] = face_of(pyc[s], hyc[s])
        dg[s * (cx - 1)] = dg[s * (cx - 1)] + wx[s]
        for k in range(nk):
            az[k, s * (cx - 1)] = az[k, s * (cx - 1)] + wx[s] * zf[k, s * (cx - 1)]
    top8 = iota((8, nz), 0) == 0
    bot8 = iota((8, nz), 0) == 7

    def fix(x, carry):
        lo = jnp.where(top8, wy[0, pl.ds(x, 1), :], 0.0)
        hi = jnp.where(bot8, wy[1, pl.ds(x, 1), :], 0.0)
        dg[x, 0:8, :] = dg[x, 0:8, :] + lo
        dg[x, cy - 8 : cy, :] = dg[x, cy - 8 : cy, :] + hi
        for k in range(nk):
            az[k, x, 0:8, :] = az[k, x, 0:8, :] + lo * zf[k, x, 0:8, :]
            az[k, x, cy - 8 : cy, :] = az[k, x, cy - 8 : cy, :] + hi * zf[k, x, cy - 8 : cy, :]
        rd[x] = 1.0 / dg[x]
        return carry

    lax.fori_loop(0, cx, fix, 0)

    pairs = [(k, l) for k in range(nk) for l in range(k, nk)]

    def gram(x, accs):
        accs = list(accs)
        for i in range(cy // 8):
            for j in range(nz // 128):
                zs = [zf[k, x, 8 * i : 8 * i + 8, 128 * j : 128 * j + 128] for k in range(nk)]
                for l in range(nk):
                    w = az[l, x, 8 * i : 8 * i + 8, 128 * j : 128 * j + 128]
                    for k in range(l + 1):
                        n = pairs.index((k, l))
                        accs[n] = accs[n] + zs[k] * w
        return tuple(accs)

    diag = lax.fori_loop(0, cx, gram, tuple(jnp.zeros((8, 128), F32) for _ in pairs))

    lane = iota((8, 128), 1)
    sub = iota((8, 128), 0)
    tile = jnp.zeros((8, 128), F32)
    for l in range(nk):
        v = total_rows([diag[pairs.index((min(k, l), max(k, l)))] for k in range(nk)])
        tile = tile + jnp.where(lane == 8 + l, v, 0.0)
    for l in range(nk):
        z_halos[l][1]()
        for s in range(2):
            nx[s, l] = -(wx[s] * hxz[s, l])
            ny[s, l] = -(wy[s] * hyz[s, l])
        for s in range(2):
            v = total_rows([fold(zf[k, s * (cx - 1)] * nx[s, l]) for k in range(nk)])
            tile = tile + jnp.where(lane == 16 * s + l, v, 0.0)
        v = total_rows([fold(pyz[0, k] * ny[0, l]) for k in range(nk)])
        tile = tile + jnp.where(lane == 24 + l, v, 0.0)
    tile = jnp.take_along_axis(tile, lane % 32, axis=1)
    tile = jnp.where(lane // 32 == sub % 4, tile, 0.0)
    upper = jnp.sum(jnp.where(sub < 4, tile, 0.0), axis=0, keepdims=True)
    lower = jnp.sum(jnp.where(sub < 4, 0.0, tile), axis=0, keepdims=True)


    def wait_bytes(ref, sem):
        pltpu.make_async_copy(ref, ref, sem).wait()

    def message_rows(groups):
        out = jnp.zeros((1, 128), F32)
        for q, accs in groups:
            v = total_rows(accs)
            out = out + jnp.sum(jnp.where(lane == 8 * q + sub, v, 0.0), axis=0, keepdims=True)
        return out

    half_y, half_z = na // 2, 4 if nb % 4 == 0 else 1
    side_x = nb // half_z
    hops = lambda d, n: min(d, n - d)
    offsets = sorted(
        [(i, j, k, 1 - c) for i in range(half_y) for j in range(half_z) for k in range(side_x) for c in range(2)],
        key=lambda o: -(hops(o[0], half_y) + hops(o[1], half_z) + hops(o[2], side_x)))
    me = b * na + a

    def spread(own, ssem, rsem):
        for dy, dz, dx, dc in offsets:
            if (dy, dz, dx, dc) == (0, 0, 0, 0):
                continue
            to_a = 2 * lax.rem(a // 2 + dy, half_y) + (1 - lax.rem(a, 2) if dc else lax.rem(a, 2))
            to_b = side_x * lax.rem(b // side_x + dz, half_z) + lax.rem(lax.rem(b, side_x) + dx, side_x)
            pltpu.make_async_remote_copy(
                src_ref=own, dst_ref=own, send_sem=ssem, recv_sem=rsem,
                device_id=(to_a, to_b), device_id_type=mesh_id).start()

    def send(phase, groups):
        gb[phase, pl.ds(me, 1), :] = message_rows(groups)
        spread(gb.at[phase, pl.ds(me, 1)], gs_sem.at[phase], gr_sem.at[phase])

    def receive(phase):
        wait_bytes(gb.at[phase, pl.ds(0, na * nb - 1)], gr_sem.at[phase])
        return jnp.transpose(gb[phase])

    et[pl.ds(2 * me, 1), :] = upper
    et[pl.ds(2 * me + 1, 1), :] = lower
    pl.semaphore_wait(all_sem, nb - 1)
    spread(et.at[pl.ds(pl.multiple_of(2 * me, 2), 2)], es_sem.at[0], er_sem.at[0])
    x_halo[1]()
    loads[2].wait()

    def minus_faces(v, x, hx, hy):
        v = v + jnp.where(row0, wy[0, pl.ds(x, 1), :] * hy[0, pl.ds(x, 1), :], 0.0)
        return v + jnp.where(rowl, wy[1, pl.ds(x, 1), :] * hy[1, pl.ds(x, 1), :], 0.0)

    def first(x, accs):
        ax = inner_apply(xf[x], xf[below(x)], xf[above(x)], x)
        r = minus_faces(rf[x] - ax, x, hxx, hyx)
        r = r + jnp.where(x == 0, wx[0] * hxx[0], 0.0) + jnp.where(x == cx - 1, wx[1] * hxx[1], 0.0)
        rf[x] = r
        return tuple(accs[k] + fold(zf[k, x] * r) for k in range(nk))

    rest = lax.fori_loop(0, cx, first, tuple(jnp.zeros((8, 128), F32) for _ in range(nk)))

    send(0, [(0, list(rest))])
    unit_columns(y_ref, a, b, na, nb)
    wait_bytes(et.at[pl.ds(0, 2 * (na * nb - 1))], er_sem.at[0])

    def expand(j, carry):
        start = pl.multiple_of(2 * na * j, 2 * na)
        for i in range(na):
            packed = jnp.where(sub < 4, et[pl.ds(start + 2 * i, 1), :], et[pl.ds(start + 2 * i + 1, 1), :])
            side = lane >= 64
            at = jnp.where(side, lane - 64 - 8 * i, lane + 8 - 8 * i)
            good = (at >= 0) & (at < jnp.where(side, 8, 24))
            source = 32 * (sub % 4) + jnp.where(good, at, 0) + jnp.where(side, 24, 0)
            d_ref[j, 8 * i : 8 * i + 8, :] = jnp.where(good, jnp.take_along_axis(packed, source, axis=1), 0.0)
        return carry

    lax.fori_loop(0, nb, expand, 0)

    factor(d_ref, lu_ref, w_ref, y_ref, m_ref, x_ref, xt_ref, a, b, na, nb)

    def coarse_of(got):
        g = got[0:8]
        g = g + pltpu.roll(got[8:16], na * nb - 1, 1) + pltpu.roll(got[16:24], 1, 1)
        g = g + pltpu.roll(got[24:32], na * nb - na, 1) + pltpu.roll(got[32:40], na, 1)
        c = xt_ref[0] * g[0:1, :]
        for k in range(1, nk):
            c = c + xt_ref[k] * g[k : k + 1, :]
        return jnp.broadcast_to(jnp.sum(c, axis=1, keepdims=True), (40, nz))

    def keep(c):
        cc[...] = c
        for s in range(2):
            u = nx[s, 0] * cc[8 * s + 8 : 8 * s + 9, :]
            v = ny[s, 0] * cc[8 * s + 24 : 8 * s + 25, :]
            for k in range(1, nk):
                u = u + nx[s, k] * cc[8 * s + 8 + k : 8 * s + 9 + k, :]
                v = v + ny[s, k] * cc[8 * s + 24 + k : 8 * s + 25 + k, :]
            fcx[s] = u
            fcy[s] = v

    def span(vectors, x):
        out = vectors[0, x] * cc[0:1, :]
        for k in range(1, nk):
            out = out + vectors[k, x] * cc[k : k + 1, :]
        return out

    def image(x):
        out = span(az, x)
        out = out + jnp.where(row0, fcy[0, pl.ds(x, 1), :], 0.0) + jnp.where(rowl, fcy[1, pl.ds(x, 1), :], 0.0)
        return out + jnp.where(x == 0, fcx[0], 0.0) + jnp.where(x == cx - 1, fcx[1], 0.0)

    def scalar(got, row):
        return jnp.sum(got[row : row + 1, :], axis=1, keepdims=True)

    zero = jnp.zeros((8, 128), F32)

    def restrict_slab(x, v, field, slot, accs):
        field[x] = v
        pyv[slot, 0, pl.ds(x, 1), :] = v[0:1, :]
        pyv[slot, 1, pl.ds(x, 1), :] = v[cy - 1 : cy, :]
        return tuple(accs[k] + fold(az[k, x] * v) for k in range(nk))

    def finish_groups(field, slot, accs):
        groups = [(0, list(accs[:nk])), (5, list(accs[nk:]))]
        for s in range(2):
            groups.append((1 + s, [fold(nx[s, k] * field[s * (cx - 1)]) for k in range(nk)]))
            groups.append((3 + s, [fold(ny[s, k] * pyv[slot, s]) for k in range(nk)]))
        return groups

    fields = [vf, uf]
    v_halos = [
        halo(3 + i, [fields[i].at[0], fields[i].at[cx - 1], pyv.at[i, 0], pyv.at[i, 1]],
             [hxv.at[i, 0], hxv.at[i, 1], hyv.at[i, 0], hyv.at[i, 1]])
        for i in range(2)
    ]

    def apply_all(i, out):
        field, hx, hy = fields[i], hxv.at[i], hyv.at[i]

        def slab(x, carry):
            w = inner_apply(field[x], field[below(x)], field[above(x)], x)
            w = w - jnp.where(row0, wy[0, pl.ds(x, 1), :] * hy[0, pl.ds(x, 1), :], 0.0)
            w = w - jnp.where(rowl, wy[1, pl.ds(x, 1), :] * hy[1, pl.ds(x, 1), :], 0.0)
            out[x] = w - jnp.where(x == 0, wx[0] * hx[0], 0.0) - jnp.where(x == cx - 1, wx[1] * hx[1], 0.0)
            return carry

        lax.fori_loop(0, cx, slab, 0)

    keep(coarse_of(receive(0)))
    x_halo[2]()

    def deflate(x, accs):
        xf[x] = xf[x] + span(zf, x)
        r = rf[x] - image(x)
        rf[x] = r
        v = r * rd[x]
        return restrict_slab(x, v, vf, 0, accs) + (accs[nk] + fold(r * v),)

    accs = lax.fori_loop(0, cx, deflate, (zero,) * (nk + 1))
    v_halos[0][0]()
    send(1, finish_groups(vf, 0, accs))
    v_halos[0][1]()
    apply_all(0, wf)
    got = receive(1)
    keep(coarse_of(got))
    inner = scalar(got, 40)

    def sums(x, p, q, v, slot, accs):
        u = q * rd[x]
        more = (accs[nk] + fold(p * q), accs[nk + 1] + fold(q * v), accs[nk + 2] + fold(q * u))
        return restrict_slab(x, u, uf, slot, accs) + more

    def direction(x, accs):
        v = vf[x]
        p = v - span(zf, x)
        q = wf[x] - image(x)
        pf[x] = p
        qf[x] = q
        return sums(x, p, q, v, 1, accs)

    accs = lax.fori_loop(0, cx, direction, (zero,) * (nk + 3))
    v_halos[1][0]()
    send(2, finish_groups(uf, 1, accs))
    v_halos[0][2]()
    v_halos[1][1]()
    apply_all(1, tf)

    def advance(got, inner):
        step = inner / scalar(got, 40)
        new = inner - 2.0 * step * scalar(got, 41) + step * step * scalar(got, 42)
        keep(cc[...] - step * coarse_of(got))
        return step, new, new / inner

    got = receive(2)
    step, inner, beta = advance(got, inner)
    v_halos[1][2]()

    def next_direction(x, accs):
        v = vf[x] - step * uf[x]
        vf[x] = v
        p = v + beta * pf[x] - span(zf, x)
        q = wf[x] - step * tf[x] + beta * qf[x] - image(x)
        ph[x] = p
        qh[x] = q
        return sums(x, p, q, v, 2, accs)

    accs = lax.fori_loop(0, cx, next_direction, (zero,) * (nk + 3))
    send(3, finish_groups(uf, 2, accs))

    def move(x, carry):
        xf[x] = xf[x] + step * pf[x]
        rf[x] = rf[x] - step * qf[x]
        return carry

    lax.fori_loop(0, cx, move, 0)
    got = receive(3)
    last_step, inner, beta = advance(got, inner)

    def last_move(x, carry):
        xf[x] = xf[x] + last_step * ph[x]
        rf[x] = rf[x] - last_step * qh[x]
        return carry

    def last(x, carry):
        pf[x] = vf[x] - last_step * uf[x] + beta * ph[x] - span(zf, x)
        return carry

    lax.fori_loop(0, cx, last_move, 0)
    stores = [
        pltpu.make_async_copy(xf, sol_hbm, st_sem.at[0]),
        pltpu.make_async_copy(rf, res_hbm, st_sem.at[1]),
        pltpu.make_async_copy(pf, dir_hbm, st_sem.at[2]),
    ]
    stores[0].start()
    stores[1].start()
    lax.fori_loop(0, cx, last, 0)
    stores[2].start()
    for h in [coef_halo] + z_halos:
        h[2]()
    wait_bytes(et.at[pl.ds(0, 2 * (na * nb - 1))], es_sem.at[0])
    for phase in range(4):
        wait_bytes(gb.at[phase, pl.ds(0, na * nb - 1)], gs_sem.at[phase])
    for store in stores:
        store.wait()


def hand_over(count, *refs):
    ins, outs, held = refs[:3], refs[3:6], refs[6:9]
    load_sem, store_sem = refs[9:]
    piece = ins[0].shape[0] // count
    every = [(i, j) for j in range(count) for i in range(3)]

    def load(i, j):
        part = pl.ds(j * piece, piece)
        return pltpu.make_async_copy(ins[i].at[part], held[i].at[part], load_sem.at[i, j])

    def store(i, j):
        part = pl.ds(j * piece, piece)
        return pltpu.make_async_copy(held[i].at[part], outs[i].at[part], store_sem.at[i, j])

    for i, j in every:
        load(i, j).start()
    for i, j in every:
        load(i, j).wait()
        store(i, j).start()
    for i, j in every:
        store(i, j).wait()


def solution(mesh):
    na, nb = mesh.shape["gx"], mesh.shape["gy"]

    def per_device(right_side, start_field, coef, deflation):
        nk, cx, cy, nz = deflation.shape
        vm = lambda *shape: pltpu.VMEM(shape, F32)
        dma = lambda *shape: pltpu.SemaphoreType.DMA(shape)
        field = (cx, cy, nz)
        scratch = [
            vm(nk, *field), vm(nk, *field)] + [vm(*field) for _ in range(11)] + [
            vm(cx + 1, cy, nz), vm(*field), vm(*field), vm(*field), vm(*field), vm(*field), vm(*field),
            vm(2, cy, nz), vm(2, cx, nz),
            vm(2, nk, cy, nz), vm(2, nk, cx, nz), vm(2, cy, nz), vm(2, cx, nz), vm(2, cy, nz), vm(2, cx, nz),
            vm(2, 2, cy, nz), vm(2, 2, cx, nz),
            vm(2, nk, cx, nz), vm(2, cx, nz), vm(2, cx, nz), vm(3, 2, cx, nz),
            vm(2, nk, cy, nz), vm(2, nk, cx, nz), vm(2, cy, nz), vm(2, cx, nz),
            vm(40, nz), vm(2 * na * nb, 128), vm(4, na * nb, 128),
            vm(nb, 64, 128), vm(nb, 64, 128), vm(nb, 64, 256), vm(nb, 64, 128), vm((nb // 2 + 1) // 2, 64, 128),
            vm(nb * 64, 128), vm(8, 40, 128),
            dma(4), dma(3), dma(5 + nk, 4), dma(5 + nk, 4), dma(1), dma(1), dma(4), dma(4), pltpu.SemaphoreType.REGULAR,
        ]
        out = jax.ShapeDtypeStruct(field, F32)
        results = pl.pallas_call(
            functools.partial(body, na, nb),
            out_shape=(out, out, out),
            in_specs=[pl.BlockSpec(memory_space=pl.ANY)] * 4,
            out_specs=(pl.BlockSpec(memory_space=pl.ANY),) * 3,
            scratch_shapes=scratch,
            compiler_params=pltpu.CompilerParams(
                collective_id=0, has_side_effects=True, vmem_limit_bytes=60000 * 1024),
            name="deflated_cg",
        )(right_side, start_field, coef, deflation)
        return pl.pallas_call(
            functools.partial(hand_over, 2),
            out_shape=(out, out, out),
            in_specs=[pl.BlockSpec(memory_space=pl.ANY)] * 3,
            out_specs=(pl.BlockSpec(memory_space=pl.ANY),) * 3,
            scratch_shapes=[vm(*field), vm(*field), vm(*field), dma(3, 2), dma(3, 2)],
            name="hand_over",
        )(*results)

    spec = P("gx", "gy", None)
    return jax.shard_map(
        per_device, mesh=mesh, in_specs=(spec, spec, spec, P(None, "gx", "gy", None)),
        out_specs=(spec, spec, spec), check_vma=False)
```

```python
import functools
import jax, jax.numpy as jnp
from jax import lax
from jax.experimental import pallas as pl
from jax.experimental.pallas import tpu as pltpu
from jax.sharding import PartitionSpec as P

F32 = jnp.float32
BF = jnp.bfloat16


def iota(shape, dim):
    return lax.broadcasted_iota(jnp.int32, shape, dim)


def split3(v):
    high = v.astype(BF)
    rest = v - high.astype(F32)
    mid = rest.astype(BF)
    low = (rest - mid.astype(F32)).astype(BF)
    return high, mid, low


def mm(left, right):
    lh, lm, ll = left
    rh, rm, rl = right
    if lh.shape[1] < 128:
        d = lambda p, q: jnp.dot(p, q, preferred_element_type=F32)
        return d(lh, rh) + (d(lh, rm) + d(lm, rh)) + (d(lm, rm) + d(lh, rl) + d(ll, rh))
    return jnp.dot(
        jnp.concatenate([lh, lh, lm, lm, lh, ll], axis=1),
        jnp.concatenate([rh, rm, rh, rm, rl, rh], axis=0), preferred_element_type=F32)


def invert_pairs(m_ref, count):
    w = 16 if count == 1 else 8
    lane = iota((w, 128), 1)
    sub = iota((w, 128), 0)
    half = lane // 64 * 64
    left = lane < 64
    wide_panel = iota((64, 128), 1) % 64 // w
    ahead = [m_ref[s, 0:w, :] for s in range(count)]
    for p in range(64 // w):
        in_panel = (lane - half) // w == p
        done = (lane - half) // w < p
        ident = (lane - half - p * w) == sub
        index = [half + p * w + j for j in range(w)]
        rows, piv, cols, near = [], [], [], []
        for s in range(count):
            r = ahead[s]
            piv.append([jnp.take_along_axis(r, index[j], axis=1) for j in range(w)])
            rows.append(jnp.where(in_panel, jnp.where(ident, 1.0, 0.0), r))
            flip = jnp.where(done, -r, r)
            c = jnp.concatenate([flip[:, :64], pltpu.roll(flip, 64, 1)[:, :64]], axis=0)
            ch, cm, cl = split3(c)
            cols.append(jnp.transpose(jnp.concatenate([ch, ch, cm, cm, ch, cl], axis=0).astype(F32)).astype(BF))
            if p < 64 // w - 1:
                raw = m_ref[s, w * p + w : w * p + 2 * w, :]
                near.append([jnp.take_along_axis(raw, index[j], axis=1) for j in range(w)])
                ahead[s] = jnp.where(in_panel, 0.0, raw)
        for t in range(w):
            own = sub == t
            for s in range(count):
                mult = piv[s][t]
                scale = 1.0 / mult[t : t + 1, :]
                row = rows[s][t : t + 1, :]
                rows[s] = jnp.where(own, row * scale, rows[s] - (mult * row) * scale)
                for j in range(t + 1, w):
                    prow = piv[s][j][t : t + 1, :]
                    piv[s][j] = jnp.where(own, prow * scale, piv[s][j] - (mult * prow) * scale)
        for s in range(count):
            if p < 64 // w - 1:
                terms = [near[s][j] * rows[s][j : j + 1, :] for j in range(w)]
                while len(terms) > 1:
                    terms = [terms[i] + terms[i + 1] for i in range(0, len(terms), 2)]
                ahead[s] = ahead[s] - terms[0]
            r = jnp.concatenate([jnp.where(left, rows[s], 0.0), jnp.where(left, 0.0, rows[s])], axis=0)
            rh, rm, rl = split3(r)
            right = jnp.concatenate([rh, rm, rh, rm, rl, rh], axis=0)
            new = jnp.where(wide_panel == p, 0.0, m_ref[s]) - jnp.dot(cols[s], right, preferred_element_type=F32)
            for v in range(64 // w):
                m_ref[s, w * v : w * v + w, :] = rows[s] if v == p else new[w * v : w * v + w, :]


def invert_chains(m_ref, count):
    lane = iota((8, 128), 1)
    sub = iota((8, 128), 0)
    half = lane // 64 * 64
    block = lane % 64 // 8
    left = lane < 64
    wide_block = iota((64, 128), 1) % 64 // 8
    gone = []
    for together in ([1, 3, 5, 7], [2, 6], [4], [0]):
        done = functools.reduce(jnp.logical_or, [block == q for q in gone], lane < 0)
        keys = [(s, p) for s in range(count) for p in together]
        rows, piv, cols = {}, {}, []
        for s, p in keys:
            r = m_ref[s, 8 * p : 8 * p + 8, :]
            piv[s, p] = [jnp.take_along_axis(r, half + p * 8 + j, axis=1) for j in range(8)]
            rows[s, p] = jnp.where(block == p, jnp.where(lane - half - p * 8 == sub, 1.0, 0.0), r)
        for s in range(count):
            flips = [jnp.where(done, -m_ref[s, 8 * p : 8 * p + 8, :], m_ref[s, 8 * p : 8 * p + 8, :]) for p in together]
            c = jnp.concatenate([f[:, :64] for f in flips] + [pltpu.roll(f, 64, 1)[:, :64] for f in flips], axis=0)
            ch, cm, cl = split3(c)
            cols.append(jnp.transpose(jnp.concatenate([ch, ch, cm, cm, ch, cl], axis=0).astype(F32)).astype(BF))
        for t in range(8):
            own = sub == t
            for key in keys:
                mult = piv[key][t]
                scale = 1.0 / mult[t : t + 1, :]
                row = rows[key][t : t + 1, :]
                rows[key] = jnp.where(own, row * scale, rows[key] - (mult * row) * scale)
                for j in range(t + 1, 8):
                    prow = piv[key][j][t : t + 1, :]
                    piv[key][j] = jnp.where(own, prow * scale, piv[key][j] - (mult * prow) * scale)
        cleared = functools.reduce(jnp.logical_or, [wide_block == p for p in together])
        for s in range(count):
            r = jnp.concatenate(
                [jnp.where(left, rows[s, p], 0.0) for p in together]
                + [jnp.where(left, 0.0, rows[s, p]) for p in together], axis=0)
            rh, rm, rl = split3(r)
            right = jnp.concatenate([rh, rm, rh, rm, rl, rh], axis=0)
            new = jnp.where(cleared, 0.0, m_ref[s]) - jnp.dot(cols[s], right, preferred_element_type=F32)
            for v in range(8):
                m_ref[s, 8 * v : 8 * v + 8, :] = rows[s, v] if v in together else new[8 * v : 8 * v + 8, :]
        gone = gone + together


def unit_columns(y_ref, a, b, na, nb):
    lane = iota((64, 128), 1)
    rowi = iota((64, 128), 0)
    group = lane // 8
    own = (b * na + a) * 8
    target = jnp.where(group == 0, own, -4096)
    target = jnp.where((group == 1) & (a > 0), own - 8, target)
    target = jnp.where((group == 2) & (a < na - 1), own + 8, target)
    target = jnp.where((group == 3) & (b > 0), own - 64, target)
    target = jnp.where((group == 4) & (b < nb - 1), own + 64, target)
    target = target + lane % 8
    for j in range(nb):
        y_ref[j] = jnp.where(rowi + 64 * j == target, 1.0, 0.0)


def factor(d_ref, lu_ref, w_ref, y_ref, m_ref, x_ref, xt_ref, a, b, na, nb):
    lane = iota((64, 128), 1)
    low = lane < 64
    for j in range(nb):
        left = pltpu.roll(d_ref[j], 64, 1)
        if j < nb - 1:
            up = jnp.transpose(d_ref[j + 1])[64:128, :]
            up = jnp.concatenate([jnp.zeros((64, 64), F32), up], axis=1)
        else:
            up = jnp.zeros((64, 128), F32)
        left = jnp.where(low, left, 0.0) if j > 0 else jnp.zeros((64, 128), F32)
        lu_ref[j] = jnp.where(low, left, up)

    def invert(lines, step):
        slots = (len(lines) + 1) // 2
        for s in range(slots):
            first = d_ref[lines[2 * s]]
            second = d_ref[lines[min(2 * s + 1, len(lines) - 1)]]
            m_ref[s] = jnp.where(low, first, pltpu.roll(second, 64, 1))
        (invert_chains if step == 1 and len(lines) > 1 else invert_pairs)(m_ref, slots)
        out = []
        for i in range(len(lines)):
            v = m_ref[i // 2]
            out.append(v[:, :64] if i % 2 == 0 else pltpu.roll(v, 64, 1)[:, :64])
        return out

    step = 1
    levels = []
    while step < nb:
        lines = list(range(step, nb, 2 * step))
        inverses = invert(lines, step)
        for j, inv in zip(lines, inverses):
            right = jnp.concatenate([lu_ref[j], y_ref[j]], axis=1)
            lut = jnp.transpose(lu_ref[j])
            w = mm(split3(inv), split3(right))
            w_ref[j] = w
            p = mm(split3(lut), split3(w))
            i, k = j - step, j + step
            d_ref[i] = d_ref[i] - p[:64, :128]
            y_ref[i] = y_ref[i] - p[:64, 128:]
            lu_ref[i] = jnp.where(low, lu_ref[i], -p[:64, :128])
            if k < nb:
                d_ref[k] = d_ref[k] - pltpu.roll(p[64:, :128], 64, 1)
                y_ref[k] = y_ref[k] - p[64:, 128:]
                lu_ref[k] = jnp.where(low, -p[64:, :128], lu_ref[k])
        levels.append((step, lines))
        step *= 2
    inv = invert([0], step)[0]
    x_ref[0:64] = mm(split3(inv), split3(y_ref[0]))
    for step, lines in reversed(levels):
        for j in lines:
            i, k = j - step, j + step
            below = x_ref[64 * i : 64 * i + 64]
            above = x_ref[64 * k : 64 * k + 64] if k < nb else jnp.zeros((64, 128), F32)
            both = jnp.concatenate([below, above], axis=0)
            w = w_ref[j]
            x_ref[64 * j : 64 * j + 64] = w[:, 128:] - mm(split3(w[:, :128]), split3(both))
    for k in range(8):
        xt_ref[k] = jnp.transpose(x_ref[pl.ds(k, na * nb, stride=8), :])[:40, :]


def total_rows(accs):
    sub = iota((8, 128), 0)
    out = jnp.zeros((8, 128), F32)
    for i, acc in enumerate(accs):
        out = jnp.where(sub == i, jnp.sum(acc, axis=0, keepdims=True), out)
    return jnp.broadcast_to(jnp.sum(out, axis=1, keepdims=True), (8, 128))


def fold(value):
    rows, cols = value.shape
    pieces = [value[8 * i : 8 * i + 8, 128 * j : 128 * j + 128] for i in range(rows // 8) for j in range(cols // 128)]
    while len(pieces) > 1:
        pieces = [pieces[i] + pieces[i + 1] if i + 1 < len(pieces) else pieces[i] for i in range(0, len(pieces), 2)]
    return pieces[0]


def face_of(lower, upper):
    summed = lower + upper
    return jnp.where((lower > 0.0) & (upper > 0.0), 2.0 * lower * upper / summed, summed)


def body(na, nb, rhs_hbm, x0_hbm, c_hbm, z_hbm, sol_hbm, res_hbm, dir_hbm, *scratch):
    (zf, az, cf, xf, rf, vf, wf, uf, tf, pf, qf, ph, qh, fx, fyl, fyh, fzl, fzh, dg, rd,
     wx, wy, hxz, hyz, hxc, hyc, hxx, hyx, hxv, hyv, pyz, pyc, pyx, pyv, nx, ny, fcx, fcy,
     cc, et, gb,
     d_ref, lu_ref, w_ref, y_ref, m_ref, x_ref, xt_ref,
     ld_sem, st_sem, hs_sem, hr_sem, es_sem, er_sem, gs_sem, gr_sem, all_sem) = scratch
    cx, cy, nz = cf.shape
    nk = zf.shape[0]
    a = lax.axis_index("gx")
    b = lax.axis_index("gy")
    mesh_id = pl.DeviceIdType.MESH
    loads = [
        pltpu.make_async_copy(c_hbm, cf, ld_sem.at[0]),
        pltpu.make_async_copy(x0_hbm, xf, ld_sem.at[1]),
        pltpu.make_async_copy(rhs_hbm, rf, ld_sem.at[2]),
        pltpu.make_async_copy(z_hbm, zf, ld_sem.at[3]),
    ]
    for i in (0, 3, 1, 2):
        loads[i].start()
    barrier = pltpu.get_barrier_semaphore()
    for o in range(1, na):
        pl.semaphore_signal(barrier, inc=1, device_id=(lax.rem(a + o, na), b), device_id_type=mesh_id)
    for o in range(1, nb):
        pl.semaphore_signal(barrier, inc=1, device_id=(a, lax.rem(b + o, nb)), device_id_type=mesh_id)

    has = [a > 0, a < na - 1, b > 0, b < nb - 1]
    peers = [(a - 1, b), (a + 1, b), (a, b - 1), (a, b + 1)]

    def halo(slot, sources, targets):
        def copy(s):
            return pltpu.make_async_remote_copy(
                src_ref=sources[s], dst_ref=targets[s ^ 1],
                send_sem=hs_sem.at[slot, s], recv_sem=hr_sem.at[slot, s ^ 1],
                device_id=peers[s], device_id_type=mesh_id)

        def start():
            for s in range(4):
                @pl.when(has[s])
                def _():
                    copy(s).start()

        def wait_recv():
            for s in range(4):
                @pl.when(has[s])
                def _():
                    pltpu.make_async_remote_copy(
                        src_ref=sources[s], dst_ref=targets[s],
                        send_sem=hs_sem.at[slot, s], recv_sem=hr_sem.at[slot, s],
                        device_id=peers[s], device_id_type=mesh_id).wait_recv()

        def wait_send():
            for s in range(4):
                @pl.when(has[s])
                def _():
                    copy(s).wait_send()

        return start, wait_recv, wait_send

    row0 = iota((cy, nz), 0) == 0
    rowl = iota((cy, nz), 0) == cy - 1
    lan0 = iota((cy, nz), 1) == 0
    lanl = iota((cy, nz), 1) == nz - 1

    for s in range(2):
        @pl.when(jnp.logical_not(has[s]))
        def _():
            hxz[s] = jnp.zeros(hxz.shape[1:], F32)
            hxc[s] = jnp.zeros(hxc.shape[1:], F32)
            hxx[s] = jnp.zeros(hxx.shape[1:], F32)
            for i in range(2):
                hxv[i, s] = jnp.zeros(hxv.shape[2:], F32)

        @pl.when(jnp.logical_not(has[2 + s]))
        def _():
            hyz[s] = jnp.zeros(hyz.shape[1:], F32)
            hyc[s] = jnp.zeros(hyc.shape[1:], F32)
            hyx[s] = jnp.zeros(hyx.shape[1:], F32)
            for i in range(2):
                hyv[i, s] = jnp.zeros(hyv.shape[2:], F32)

    loads[0].wait()

    def pack(x, carry):
        pyc[0, pl.ds(x, 1), :] = cf[x, 0:1, :]
        pyc[1, pl.ds(x, 1), :] = cf[x, cy - 1 : cy, :]
        return carry

    lax.fori_loop(0, cx, pack, 0)

    fx[0] = jnp.zeros((cy, nz), F32)
    fx[cx] = jnp.zeros((cy, nz), F32)

    def faces_x(x, carry):
        fx[x] = face_of(cf[x - 1], cf[x])
        return carry

    lax.fori_loop(1, cx, faces_x, 0)

    def faces(x, carry):
        c = cf[x]
        yl = jnp.where(row0, 0.0, face_of(pltpu.roll(c, 1, 0), c))
        yh = jnp.where(rowl, 0.0, face_of(c, pltpu.roll(c, cy - 1, 0)))
        zl = jnp.where(lan0, c, face_of(pltpu.roll(c, 1, 1), c))
        zh = jnp.where(lanl, c, face_of(c, pltpu.roll(c, nz - 1, 1)))
        dg[x] = fx[x] + fx[x + 1] + yl + yh + zl + zh
        fyl[x] = yl
        fyh[x] = yh
        fzl[x] = jnp.where(lan0, 0.0, zl)
        fzh[x] = jnp.where(lanl, 0.0, zh)
        return carry

    lax.fori_loop(0, cx, faces, 0)

    pl.semaphore_wait(barrier, na + nb - 2)
    for o in range(1, nb):
        pl.semaphore_signal(all_sem, inc=1, device_id=(a, lax.rem(b + o, nb)), device_id_type=mesh_id)
    coef_halo = halo(0, [cf.at[0], cf.at[cx - 1], pyc.at[0], pyc.at[1]], [hxc.at[0], hxc.at[1], hyc.at[0], hyc.at[1]])
    coef_halo[0]()
    loads[3].wait()

    def packz(x, carry):
        for k in range(nk):
            pyz[0, k, pl.ds(x, 1), :] = zf[k, x, 0:1, :]
            pyz[1, k, pl.ds(x, 1), :] = zf[k, x, cy - 1 : cy, :]
        return carry

    lax.fori_loop(0, cx, packz, 0)
    z_halos = [
        halo(5 + k, [zf.at[k, 0], zf.at[k, cx - 1], pyz.at[0, k], pyz.at[1, k]],
             [hxz.at[0, k], hxz.at[1, k], hyz.at[0, k], hyz.at[1, k]])
        for k in range(nk)
    ]
    for z_halo in z_halos:
        z_halo[0]()
    loads[1].wait()

    def packx(x, carry):
        pyx[0, pl.ds(x, 1), :] = xf[x, 0:1, :]
        pyx[1, pl.ds(x, 1), :] = xf[x, cy - 1 : cy, :]
        return carry

    lax.fori_loop(0, cx, packx, 0)
    x_halo = halo(1, [xf.at[0], xf.at[cx - 1], pyx.at[0], pyx.at[1]], [hxx.at[0], hxx.at[1], hyx.at[0], hyx.at[1]])
    x_halo[0]()

    def inner_apply(v, before, after, x):
        near = fx[x] * before + fx[x + 1] * after
        near = near + fyl[x] * pltpu.roll(v, 1, 0) + fyh[x] * pltpu.roll(v, cy - 1, 0)
        near = near + fzl[x] * pltpu.roll(v, 1, 1) + fzh[x] * pltpu.roll(v, nz - 1, 1)
        return dg[x] * v - near

    def below(x):
        return jnp.maximum(x - 1, 0)

    def above(x):
        return jnp.minimum(x + 1, cx - 1)

    def make_az(x, carry):
        for k in range(nk):
            az[k, x] = inner_apply(zf[k, x], zf[k, below(x)], zf[k, above(x)], x)
        return carry

    lax.fori_loop(0, cx, make_az, 0)

    coef_halo[1]()
    for s in range(2):
        wx[s] = face_of(cf[s * (cx - 1)], hxc[s])
        wy[s] = face_of(pyc[s], hyc[s])
        dg[s * (cx - 1)] = dg[s * (cx - 1)] + wx[s]
        for k in range(nk):
            az[k, s * (cx - 1)] = az[k, s * (cx - 1)] + wx[s] * zf[k, s * (cx - 1)]
    top8 = iota((8, nz), 0) == 0
    bot8 = iota((8, nz), 0) == 7

    def fix(x, carry):
        lo = jnp.where(top8, wy[0, pl.ds(x, 1), :], 0.0)
        hi = jnp.where(bot8, wy[1, pl.ds(x, 1), :], 0.0)
        dg[x, 0:8, :] = dg[x, 0:8, :] + lo
        dg[x, cy - 8 : cy, :] = dg[x, cy - 8 : cy, :] + hi
        for k in range(nk):
            az[k, x, 0:8, :] = az[k, x, 0:8, :] + lo * zf[k, x, 0:8, :]
            az[k, x, cy - 8 : cy, :] = az[k, x, cy - 8 : cy, :] + hi * zf[k, x, cy - 8 : cy, :]
        rd[x] = 1.0 / dg[x]
        return carry

    lax.fori_loop(0, cx, fix, 0)

    pairs = [(k, l) for k in range(nk) for l in range(k, nk)]

    def gram(x, accs):
        accs = list(accs)
        for i in range(cy // 8):
            for j in range(nz // 128):
                zs = [zf[k, x, 8 * i : 8 * i + 8, 128 * j : 128 * j + 128] for k in range(nk)]
                for l in range(nk):
                    w = az[l, x, 8 * i : 8 * i + 8, 128 * j : 128 * j + 128]
                    for k in range(l + 1):
                        n = pairs.index((k, l))
                        accs[n] = accs[n] + zs[k] * w
        return tuple(accs)

    diag = lax.fori_loop(0, cx, gram, tuple(jnp.zeros((8, 128), F32) for _ in pairs))

    lane = iota((8, 128), 1)
    sub = iota((8, 128), 0)
    tile = jnp.zeros((8, 128), F32)
    for l in range(nk):
        v = total_rows([diag[pairs.index((min(k, l), max(k, l)))] for k in range(nk)])
        tile = tile + jnp.where(lane == 8 + l, v, 0.0)
    for l in range(nk):
        z_halos[l][1]()
        for s in range(2):
            nx[s, l] = -(wx[s] * hxz[s, l])
            ny[s, l] = -(wy[s] * hyz[s, l])
        for s in range(2):
            v = total_rows([fold(zf[k, s * (cx - 1)] * nx[s, l]) for k in range(nk)])
            tile = tile + jnp.where(lane == 16 * s + l, v, 0.0)
        v = total_rows([fold(pyz[0, k] * ny[0, l]) for k in range(nk)])
        tile = tile + jnp.where(lane == 24 + l, v, 0.0)
    tile = jnp.take_along_axis(tile, lane % 32, axis=1)
    tile = jnp.where(lane // 32 == sub % 4, tile, 0.0)
    upper = jnp.sum(jnp.where(sub < 4, tile, 0.0), axis=0, keepdims=True)
    lower = jnp.sum(jnp.where(sub < 4, 0.0, tile), axis=0, keepdims=True)


    def wait_bytes(ref, sem):
        pltpu.make_async_copy(ref, ref, sem).wait()

    def message_rows(groups):
        out = jnp.zeros((1, 128), F32)
        for q, accs in groups:
            v = total_rows(accs)
            out = out + jnp.sum(jnp.where(lane == 8 * q + sub, v, 0.0), axis=0, keepdims=True)
        return out

    half_y, half_z = na // 2, 4 if nb % 4 == 0 else 1
    side_x = nb // half_z
    hops = lambda d, n: min(d, n - d)
    offsets = sorted(
        [(i, j, k, 1 - c) for i in range(half_y) for j in range(half_z) for k in range(side_x) for c in range(2)],
        key=lambda o: -(hops(o[0], half_y) + hops(o[1], half_z) + hops(o[2], side_x)))
    me = b * na + a

    def spread(own, ssem, rsem, between=None):
        for n, (dy, dz, dx, dc) in enumerate(offsets):
            if n == 44 and between is not None:
                between()
            if (dy, dz, dx, dc) == (0, 0, 0, 0):
                continue
            to_a = 2 * lax.rem(a // 2 + dy, half_y) + (1 - lax.rem(a, 2) if dc else lax.rem(a, 2))
            to_b = side_x * lax.rem(b // side_x + dz, half_z) + lax.rem(lax.rem(b, side_x) + dx, side_x)
            pltpu.make_async_remote_copy(
                src_ref=own, dst_ref=own, send_sem=ssem, recv_sem=rsem,
                device_id=(to_a, to_b), device_id_type=mesh_id).start()

    def send(phase, groups, between=None):
        gb[phase, pl.ds(me, 1), :] = message_rows(groups)
        spread(gb.at[phase, pl.ds(me, 1)], gs_sem.at[phase], gr_sem.at[phase], between)

    def receive(phase):
        wait_bytes(gb.at[phase, pl.ds(0, na * nb - 1)], gr_sem.at[phase])
        return jnp.transpose(gb[phase])

    et[pl.ds(2 * me, 1), :] = upper
    et[pl.ds(2 * me + 1, 1), :] = lower
    pl.semaphore_wait(all_sem, nb - 1)
    spread(et.at[pl.ds(pl.multiple_of(2 * me, 2), 2)], es_sem.at[0], er_sem.at[0])
    x_halo[1]()
    loads[2].wait()

    def minus_faces(v, x, hx, hy):
        v = v + jnp.where(row0, wy[0, pl.ds(x, 1), :] * hy[0, pl.ds(x, 1), :], 0.0)
        return v + jnp.where(rowl, wy[1, pl.ds(x, 1), :] * hy[1, pl.ds(x, 1), :], 0.0)

    def first(x, accs):
        ax = inner_apply(xf[x], xf[below(x)], xf[above(x)], x)
        r = minus_faces(rf[x] - ax, x, hxx, hyx)
        r = r + jnp.where(x == 0, wx[0] * hxx[0], 0.0) + jnp.where(x == cx - 1, wx[1] * hxx[1], 0.0)
        rf[x] = r
        return tuple(accs[k] + fold(zf[k, x] * r) for k in range(nk))

    rest = lax.fori_loop(0, cx, first, tuple(jnp.zeros((8, 128), F32) for _ in range(nk)))

    send(0, [(0, list(rest))])
    unit_columns(y_ref, a, b, na, nb)
    wait_bytes(et.at[pl.ds(0, 2 * (na * nb - 1))], er_sem.at[0])

    def expand(j, carry):
        start = pl.multiple_of(2 * na * j, 2 * na)
        for i in range(na):
            packed = jnp.where(sub < 4, et[pl.ds(start + 2 * i, 1), :], et[pl.ds(start + 2 * i + 1, 1), :])
            side = lane >= 64
            at = jnp.where(side, lane - 64 - 8 * i, lane + 8 - 8 * i)
            good = (at >= 0) & (at < jnp.where(side, 8, 24))
            source = 32 * (sub % 4) + jnp.where(good, at, 0) + jnp.where(side, 24, 0)
            d_ref[j, 8 * i : 8 * i + 8, :] = jnp.where(good, jnp.take_along_axis(packed, source, axis=1), 0.0)
        return carry

    lax.fori_loop(0, nb, expand, 0, unroll=2)

    factor(d_ref, lu_ref, w_ref, y_ref, m_ref, x_ref, xt_ref, a, b, na, nb)

    def coarse_of(got):
        g = got[0:8]
        g = g + pltpu.roll(got[8:16], na * nb - 1, 1) + pltpu.roll(got[16:24], 1, 1)
        g = g + pltpu.roll(got[24:32], na * nb - na, 1) + pltpu.roll(got[32:40], na, 1)
        c = xt_ref[0] * g[0:1, :]
        for k in range(1, nk):
            c = c + xt_ref[k] * g[k : k + 1, :]
        return jnp.broadcast_to(jnp.sum(c, axis=1, keepdims=True), (40, nz))

    def keep(c):
        cc[...] = c
        for s in range(2):
            u = nx[s, 0] * cc[8 * s + 8 : 8 * s + 9, :]
            v = ny[s, 0] * cc[8 * s + 24 : 8 * s + 25, :]
            for k in range(1, nk):
                u = u + nx[s, k] * cc[8 * s + 8 + k : 8 * s + 9 + k, :]
                v = v + ny[s, k] * cc[8 * s + 24 + k : 8 * s + 25 + k, :]
            fcx[s] = u
            fcy[s] = v

    def span(vectors, x):
        out = vectors[0, x] * cc[0:1, :]
        for k in range(1, nk):
            out = out + vectors[k, x] * cc[k : k + 1, :]
        return out

    def image(x):
        out = span(az, x)
        out = out + jnp.where(row0, fcy[0, pl.ds(x, 1), :], 0.0) + jnp.where(rowl, fcy[1, pl.ds(x, 1), :], 0.0)
        return out + jnp.where(x == 0, fcx[0], 0.0) + jnp.where(x == cx - 1, fcx[1], 0.0)

    def scalar(got, row):
        return jnp.sum(got[row : row + 1, :], axis=1, keepdims=True)

    zero = jnp.zeros((8, 128), F32)

    def restrict_slab(x, v, field, slot, accs):
        field[x] = v
        pyv[slot, 0, pl.ds(x, 1), :] = v[0:1, :]
        pyv[slot, 1, pl.ds(x, 1), :] = v[cy - 1 : cy, :]
        return tuple(accs[k] + fold(az[k, x] * v) for k in range(nk))

    def finish_groups(field, slot, accs):
        groups = [(0, list(accs[:nk])), (5, list(accs[nk:]))]
        for s in range(2):
            groups.append((1 + s, [fold(nx[s, k] * field[s * (cx - 1)]) for k in range(nk)]))
            groups.append((3 + s, [fold(ny[s, k] * pyv[slot, s]) for k in range(nk)]))
        return groups

    fields = [vf, uf]
    v_halos = [
        halo(3 + i, [fields[i].at[0], fields[i].at[cx - 1], pyv.at[i, 0], pyv.at[i, 1]],
             [hxv.at[i, 0], hxv.at[i, 1], hyv.at[i, 0], hyv.at[i, 1]])
        for i in range(2)
    ]

    def apply_all(i, out):
        field, hx, hy = fields[i], hxv.at[i], hyv.at[i]

        def slab(x, carry):
            w = inner_apply(field[x], field[below(x)], field[above(x)], x)
            w = w - jnp.where(row0, wy[0, pl.ds(x, 1), :] * hy[0, pl.ds(x, 1), :], 0.0)
            w = w - jnp.where(rowl, wy[1, pl.ds(x, 1), :] * hy[1, pl.ds(x, 1), :], 0.0)
            out[x] = w - jnp.where(x == 0, wx[0] * hx[0], 0.0) - jnp.where(x == cx - 1, wx[1] * hx[1], 0.0)
            return carry

        lax.fori_loop(0, cx, slab, 0)

    keep(coarse_of(receive(0)))
    x_halo[2]()

    def deflate(x, accs):
        xf[x] = xf[x] + span(zf, x)
        r = rf[x] - image(x)
        rf[x] = r
        v = r * rd[x]
        return restrict_slab(x, v, vf, 0, accs) + (accs[nk] + fold(r * v),)

    accs = lax.fori_loop(0, cx, deflate, (zero,) * (nk + 1), unroll=2)
    send(1, finish_groups(vf, 0, accs), v_halos[0][0])
    v_halos[0][1]()
    apply_all(0, wf)
    got = receive(1)
    keep(coarse_of(got))
    inner = scalar(got, 40)

    def sums(x, p, q, v, slot, accs):
        u = q * rd[x]
        more = (accs[nk] + fold(p * q), accs[nk + 1] + fold(q * v), accs[nk + 2] + fold(q * u))
        return restrict_slab(x, u, uf, slot, accs) + more

    def direction(x, accs):
        v = vf[x]
        p = v - span(zf, x)
        q = wf[x] - image(x)
        pf[x] = p
        qf[x] = q
        return sums(x, p, q, v, 1, accs)

    accs = lax.fori_loop(0, cx, direction, (zero,) * (nk + 3), unroll=2)
    send(2, finish_groups(uf, 1, accs), v_halos[1][0])
    v_halos[0][2]()
    v_halos[1][1]()
    apply_all(1, tf)

    def advance(got, inner):
        step = inner / scalar(got, 40)
        new = inner - 2.0 * step * scalar(got, 41) + step * step * scalar(got, 42)
        keep(cc[...] - step * coarse_of(got))
        return step, new, new / inner

    got = receive(2)
    step, inner, beta = advance(got, inner)
    v_halos[1][2]()

    def next_direction(x, accs):
        v = vf[x] - step * uf[x]
        vf[x] = v
        p = v + beta * pf[x] - span(zf, x)
        q = wf[x] - step * tf[x] + beta * qf[x] - image(x)
        ph[x] = p
        qh[x] = q
        return sums(x, p, q, v, 2, accs)

    accs = lax.fori_loop(0, cx, next_direction, (zero,) * (nk + 3), unroll=2)
    send(3, finish_groups(uf, 2, accs))

    def move(x, carry):
        xf[x] = xf[x] + step * pf[x]
        rf[x] = rf[x] - step * qf[x]
        return carry

    lax.fori_loop(0, cx, move, 0)
    got = receive(3)
    last_step, inner, beta = advance(got, inner)

    def last_move(x, carry):
        xf[x] = xf[x] + last_step * ph[x]
        rf[x] = rf[x] - last_step * qh[x]
        return carry

    def last(x, carry):
        pf[x] = vf[x] - last_step * uf[x] + beta * ph[x] - span(zf, x)
        return carry

    lax.fori_loop(0, cx, last_move, 0, unroll=2)
    stores = [
        pltpu.make_async_copy(xf, sol_hbm, st_sem.at[0]),
        pltpu.make_async_copy(rf, res_hbm, st_sem.at[1]),
        pltpu.make_async_copy(pf, dir_hbm, st_sem.at[2]),
    ]
    stores[0].start()
    stores[1].start()
    lax.fori_loop(0, cx, last, 0, unroll=2)
    stores[2].start()
    for h in [coef_halo] + z_halos:
        h[2]()
    wait_bytes(et.at[pl.ds(0, 2 * (na * nb - 1))], es_sem.at[0])
    for phase in range(4):
        wait_bytes(gb.at[phase, pl.ds(0, na * nb - 1)], gs_sem.at[phase])
    for store in stores:
        store.wait()


def hand_over(count, *refs):
    ins, outs, held = refs[:3], refs[3:6], refs[6:9]
    load_sem, store_sem = refs[9:]
    piece = ins[0].shape[0] // count
    every = [(i, j) for j in range(count) for i in range(3)]

    def load(i, j):
        part = pl.ds(j * piece, piece)
        return pltpu.make_async_copy(ins[i].at[part], held[i].at[part], load_sem.at[i, j])

    def store(i, j):
        part = pl.ds(j * piece, piece)
        return pltpu.make_async_copy(held[i].at[part], outs[i].at[part], store_sem.at[i, j])

    for i, j in every:
        load(i, j).start()
    for i, j in every:
        load(i, j).wait()
        store(i, j).start()
    for i, j in every:
        store(i, j).wait()


def solution(mesh):
    na, nb = mesh.shape["gx"], mesh.shape["gy"]

    def per_device(right_side, start_field, coef, deflation):
        nk, cx, cy, nz = deflation.shape
        vm = lambda *shape: pltpu.VMEM(shape, F32)
        dma = lambda *shape: pltpu.SemaphoreType.DMA(shape)
        field = (cx, cy, nz)
        scratch = [
            vm(nk, *field), vm(nk, *field)] + [vm(*field) for _ in range(11)] + [
            vm(cx + 1, cy, nz), vm(*field), vm(*field), vm(*field), vm(*field), vm(*field), vm(*field),
            vm(2, cy, nz), vm(2, cx, nz),
            vm(2, nk, cy, nz), vm(2, nk, cx, nz), vm(2, cy, nz), vm(2, cx, nz), vm(2, cy, nz), vm(2, cx, nz),
            vm(2, 2, cy, nz), vm(2, 2, cx, nz),
            vm(2, nk, cx, nz), vm(2, cx, nz), vm(2, cx, nz), vm(3, 2, cx, nz),
            vm(2, nk, cy, nz), vm(2, nk, cx, nz), vm(2, cy, nz), vm(2, cx, nz),
            vm(40, nz), vm(2 * na * nb, 128), vm(4, na * nb, 128),
            vm(nb, 64, 128), vm(nb, 64, 128), vm(nb, 64, 256), vm(nb, 64, 128), vm((nb // 2 + 1) // 2, 64, 128),
            vm(nb * 64, 128), vm(8, 40, 128),
            dma(4), dma(3), dma(5 + nk, 4), dma(5 + nk, 4), dma(1), dma(1), dma(4), dma(4), pltpu.SemaphoreType.REGULAR,
        ]
        out = jax.ShapeDtypeStruct(field, F32)
        results = pl.pallas_call(
            functools.partial(body, na, nb),
            out_shape=(out, out, out),
            in_specs=[pl.BlockSpec(memory_space=pl.ANY)] * 4,
            out_specs=(pl.BlockSpec(memory_space=pl.ANY),) * 3,
            scratch_shapes=scratch,
            compiler_params=pltpu.CompilerParams(
                collective_id=0, has_side_effects=True, vmem_limit_bytes=60000 * 1024),
            name="deflated_cg",
        )(right_side, start_field, coef, deflation)
        return pl.pallas_call(
            functools.partial(hand_over, 2),
            out_shape=(out, out, out),
            in_specs=[pl.BlockSpec(memory_space=pl.ANY)] * 3,
            out_specs=(pl.BlockSpec(memory_space=pl.ANY),) * 3,
            scratch_shapes=[vm(*field), vm(*field), vm(*field), dma(3, 2), dma(3, 2)],
            name="hand_over",
        )(*results)

    spec = P("gx", "gy", None)
    return jax.shard_map(
        per_device, mesh=mesh, in_specs=(spec, spec, spec, P(None, "gx", "gy", None)),
        out_specs=(spec, spec, spec), check_vma=False)
```
